256 devices in a mesh: row: 32 (over z, y_lo, core), col: 8 (over x, y_hi).
Axes of the slice: x: 4, y: 4 (y_hi: 2, y_lo: 2; y = y_hi * 2 + y_lo), z: 8, core: 2. Of those that a mesh axis runs over, the one named last changes fastest.
Arguments:
- half_panel: bfloat16 [48, 2048, 2048], P(None, 'row', 'col'), may hold values from -6 to 6
- orbitals: bfloat16 [2048, 2048], replicated, may hold values from -0.125 to 0.125
Outputs:
- integrals: bfloat16 [48, 2048, 2048], P(None, 'row', 'col')
The draws below stay inside these ranges and needn't reach their ends.
All inputs are finite; a program needn't handle non-finite values.
Results may differ from the reference program's by a relative error of at most 0.0049.
Values may be sent and summed in bfloat16 or wider, within the bound.
No kernel may reach another device: no remote copies, remote signals or barrier semaphores. Data moves between devices by JAX's collectives and lax.ppermute only.
A program may use at most 64 MiB of HBM per device.

```python
import jax
import jax.numpy as jnp
from jax import lax

KL = 48
NORB = 2048


def level_of(own_key, dims, shards, least, top_value):
    factor_of, own = 1.0, jax.random.fold_in(own_key, 6)
    for dim, parts in shards:
        draws = jnp.exp(jax.random.uniform(jax.random.fold_in(own, dim), (parts,), jnp.float32, least / len(shards), top_value / len(shards)))
        factor_of = factor_of * jnp.repeat(draws, dims[dim] // parts).reshape([-1 if axis == dim else 1 for axis in range(len(dims))])
    return factor_of


def noise(rng, dims, deviation, limit, shards=(), kind=jnp.bfloat16):
    drawn = jax.random.normal(rng, dims, jnp.float32) * deviation
    if len(shards) > 0:
        drawn = level_of(rng, dims, shards, -0.22, 0.18) * drawn
    return jnp.clip(drawn, min=-limit, max=limit).astype(kind)


def setup_inputs(seed: int = 0) -> dict:
    keys = jax.random.split(jax.random.key(seed), 3)
    half_panel = noise(keys[0], (KL, NORB, NORB), 1.0, 6.0, ((1, 32), (2, 8)))
    orbitals = noise(keys[1], (NORB, NORB), NORB ** -0.5, 0.125)
    return {"half_panel": half_panel, "orbitals": orbitals}


def reference(half_panel, orbitals):
    index = jnp.arange(NORB, dtype=jnp.int32)
    keep_upper = index[:, None] <= index[None, :]

    def transform(panel):
        symmetric = jnp.where(keep_upper, panel, panel.T)
        partial_value = jnp.dot(symmetric, orbitals, preferred_element_type=jnp.float32).astype(jnp.bfloat16)
        return jnp.dot(orbitals.T, partial_value, preferred_element_type=jnp.float32).astype(jnp.bfloat16)

    return lax.map(transform, half_panel)
```

```python
import jax
import jax.numpy as jnp
from jax import lax
from jax.experimental import pallas as pl
from jax.experimental.pallas import tpu as pltpu
from jax.sharding import Mesh, PartitionSpec as P

Z, YLO, CORE, X, YHI = 8, 2, 2, 4, 2
COLS = X * YHI
PLANE = ("x", "yhi", "ylo")
F32 = jnp.float32
BF16 = jnp.bfloat16


def transposed(block):
    size = block.shape[1]
    row = lax.broadcasted_iota(jnp.int32, (size, size), 0)
    column = lax.broadcasted_iota(jnp.int32, (size, size), 1)
    eye = (row == column).astype(F32).astype(BF16)
    return lax.dot_general(
        eye, block, (((1,), (1,)), ((), ())), preferred_element_type=F32
    ).astype(BF16)


def pick_kernel(core_ref, c_ref, out_ref):
    half = c_ref.shape[1] // 4
    row = lax.broadcasted_iota(jnp.int32, (4 * half, 2 * half), 0)
    column = lax.broadcasted_iota(jnp.int32, (4 * half, 2 * half), 1)
    wanted = jnp.where(column < half, column, column + half) + core_ref[0] * half
    choose = (row == wanted).astype(F32).astype(BF16)
    out_ref[...] = jnp.dot(c_ref[...], choose, preferred_element_type=F32).astype(BF16)


def pick_columns(core, orbitals):
    size = orbitals.shape[0]
    block = size // Z
    return pl.pallas_call(
        pick_kernel,
        out_shape=jax.ShapeDtypeStruct((size, size // CORE), BF16),
        grid_spec=pltpu.PrefetchScalarGridSpec(
            num_scalar_prefetch=1,
            grid=(Z,),
            in_specs=[pl.BlockSpec((size, block), lambda g, s: (0, g))],
            out_specs=pl.BlockSpec((size, block // CORE), lambda g, s: (0, g)),
        ),
        name="pick_columns",
    )(core, orbitals)


def first_kernel(place, own, other, own_low, other_low, c_ref, t_ref, sym, turn):
    depth, rows = own.shape[2], own.shape[3]
    block = own.shape[4]
    z, core = place[0], place[1]

    @pl.when(pl.program_id(0) == 0)
    def _():
        def build(step, carry):
            k = step // Z
            b = step % Z
            base = pl.multiple_of(k * block, block)
            cols = pl.ds(pl.multiple_of(b * block, block), block)

            @pl.when(b >= z)
            def _():
                for y in range(YLO):
                    at = base + y * CORE * rows
                    sym[pl.ds(pl.multiple_of(at + core * rows, rows), rows), cols] = own[b, y, k]
                    sym[pl.ds(pl.multiple_of(at + (1 - core) * rows, rows), rows), cols] = other[b, y, k]

            @pl.when(b == z)
            def _():
                upper = sym[pl.ds(base, block), cols]
                lower = transposed(upper)
                row = lax.broadcasted_iota(jnp.int32, (block, block), 0)
                column = lax.broadcasted_iota(jnp.int32, (block, block), 1)
                sym[pl.ds(base, block), cols] = jnp.where(row <= column, upper, lower)

            @pl.when(b < z)
            def _():
                for y in range(YLO):
                    at = y * CORE * rows
                    turn[pl.ds(pl.multiple_of(at + core * rows, rows), rows), :] = own_low[b, y, k]
                    turn[pl.ds(pl.multiple_of(at + (1 - core) * rows, rows), rows), :] = other_low[b, y, k]
                sym[pl.ds(base, block), cols] = transposed(turn[...])

            return carry

        lax.fori_loop(0, depth * Z, build, 0)

    product = jnp.dot(sym[...], c_ref[...], preferred_element_type=F32).astype(BF16)
    lanes = t_ref.shape[3]
    for part in range(t_ref.shape[0]):
        for k in range(depth):
            t_ref[part, k] = product[k * block:(k + 1) * block, part * lanes:(part + 1) * lanes]


def first_half(place, own, other, own_low, other_low, picked):
    depth = own.shape[2]
    block = own.shape[4]
    size = picked.shape[0]
    lanes = picked.shape[1] // Z
    step = 2
    whole = pl.BlockSpec(own.shape, lambda g, s: (0, 0, 0, 0, 0))
    return pl.pallas_call(
        first_kernel,
        out_shape=jax.ShapeDtypeStruct((Z, depth, block, lanes), BF16),
        grid_spec=pltpu.PrefetchScalarGridSpec(
            num_scalar_prefetch=1,
            grid=(Z // step,),
            in_specs=[whole, whole, whole, whole,
                      pl.BlockSpec((size, step * lanes), lambda g, s: (0, g))],
            out_specs=pl.BlockSpec((step, depth, block, lanes), lambda g, s: (g, 0, 0, 0)),
            scratch_shapes=[pltpu.VMEM((depth * block, size), BF16),
                            pltpu.VMEM((block, block), BF16)],
        ),
        compiler_params=pltpu.CompilerParams(vmem_limit_bytes=48 * 2**20),
        name="first_half",
    )(place, own, other, own_low, other_low, picked)


def second_kernel(t_ref, c_ref, out_ref, left):
    count, depth, block, lanes = t_ref.shape
    rows = lanes // YLO

    @pl.when(pl.program_id(0) == 0)
    def _():
        for k in range(depth):
            for b in range(count):
                left[k * lanes:(k + 1) * lanes, b * block:(b + 1) * block] = transposed(t_ref[b, k])

    product = jnp.dot(left[...], c_ref[...], preferred_element_type=F32).astype(BF16)
    for k in range(depth):
        for y in range(YLO):
            at = k * lanes + y * rows
            out_ref[0, y, k] = product[at:at + rows]


def second_half(partial_value, orbitals):
    count, depth, block, lanes = partial_value.shape
    size = orbitals.shape[0]
    rows = lanes // YLO
    return pl.pallas_call(
        second_kernel,
        out_shape=jax.ShapeDtypeStruct((COLS, YLO, depth, rows, block), BF16),
        grid=(COLS,),
        in_specs=[pl.BlockSpec(partial_value.shape, lambda g: (0, 0, 0, 0)),
                  pl.BlockSpec((size, block), lambda g: (0, g))],
        out_specs=pl.BlockSpec((1, YLO, depth, rows, block), lambda g: (g, 0, 0, 0, 0)),
        scratch_shapes=[pltpu.VMEM((depth * lanes, size), BF16)],
        compiler_params=pltpu.CompilerParams(vmem_limit_bytes=48 * 2**20),
        name="second_half",
    )(partial_value, orbitals)


def swap_cores(value):
    return lax.ppermute(value, "core", [(0, 1), (1, 0)])


def per_device(half_panel, orbitals):
    pairs, rows, block = half_panel.shape
    depth = pairs // (COLS * YLO)
    place = jnp.stack([lax.axis_index("z"), lax.axis_index("core")]).astype(jnp.int32)
    picked = pick_columns(place[1:], orbitals)
    with jax.named_scope("panels_in"):
        own = half_panel.reshape(COLS * YLO, depth, rows, block)
        own = lax.all_to_all(own, PLANE, 0, 0, tiled=True)
        own = own.reshape(COLS, YLO, depth, rows, block)
    other = swap_cores(own)
    with jax.named_scope("mirror"):
        own_low = lax.all_to_all(own, "z", 0, 0, tiled=True)
    other_low = swap_cores(own_low)
    partial_value = first_half(place, own, other, own_low, other_low, picked)
    with jax.named_scope("partial"):
        partial_value = lax.all_to_all(partial_value, "z", 0, 0, tiled=True)
    result = second_half(partial_value, orbitals)
    with jax.named_scope("panels_out"):
        result = result.reshape(COLS * YLO, depth, rows, block)
        result = lax.all_to_all(result, PLANE, 0, 0, tiled=True)
    return result.reshape(pairs, rows, block)


def solution(mesh):
    fine = Mesh(mesh.devices.reshape(Z, YLO, CORE, X, YHI), ("z", "ylo", "core", "x", "yhi"))
    spec = P(None, ("z", "ylo", "core"), ("x", "yhi"))
    return jax.shard_map(
        per_device, mesh=fine, in_specs=(spec, P()), out_specs=spec, check_vma=False
    )
```

```python
import jax
import jax.numpy as jnp
from jax import lax
from jax.experimental import pallas as pl
from jax.experimental.pallas import tpu as pltpu
from jax.sharding import Mesh, PartitionSpec as P

Z, YLO, CORE, X, YHI = 8, 2, 2, 4, 2
COLS = X * YHI
BLOCKS = 8
PLANE = ("x", "yhi", "ylo")
SIDE = ("x", "yhi")
F32 = jnp.float32
BF16 = jnp.bfloat16
PARAMS = pltpu.CompilerParams(vmem_limit_bytes=16 * 2**20)
SMALL = pltpu.CompilerParams(vmem_limit_bytes=4 * 2**20)


def transposed(block):
    size = block.shape[1]
    row = lax.broadcasted_iota(jnp.int32, (size, size), 0)
    column = lax.broadcasted_iota(jnp.int32, (size, size), 1)
    eye = (row == column).astype(F32).astype(BF16)
    return lax.dot_general(
        eye, block, (((1,), (1,)), ((), ())), preferred_element_type=F32
    ).astype(BF16)


def pick_kernel(core_ref, c_ref, out_ref):
    block = c_ref.shape[1] // BLOCKS
    lanes = block // CORE
    half = lanes // 2
    row = lax.broadcasted_iota(jnp.int32, (block, lanes), 0)
    column = lax.broadcasted_iota(jnp.int32, (block, lanes), 1)
    wanted = jnp.where(column < half, column, column + half) + core_ref[0] * half
    choose = (row == wanted).astype(F32).astype(BF16)
    for b in range(BLOCKS):
        out_ref[:, b * lanes:(b + 1) * lanes] = jnp.dot(
            c_ref[:, b * block:(b + 1) * block], choose, preferred_element_type=F32
        ).astype(BF16)


def pick_columns(core, orbitals):
    size = orbitals.shape[0]
    block = size // BLOCKS
    return pl.pallas_call(
        pick_kernel,
        out_shape=jax.ShapeDtypeStruct((size, size // CORE), BF16),
        grid_spec=pltpu.PrefetchScalarGridSpec(
            num_scalar_prefetch=1,
            grid=(BLOCKS,),
            in_specs=[pl.BlockSpec((block, size), lambda g, s: (g, 0))],
            out_specs=pl.BlockSpec((block, size // CORE), lambda g, s: (g, 0)),
        ),
        name="pick_columns",
    )(core, orbitals)


def accumulate(total, product):
    step = pl.program_id(0)

    @pl.when(step == 0)
    def _():
        total[...] = product

    @pl.when(step > 0)
    def _():
        total[...] += product


def first_kernel(place, direct, direct_other, turned, turned_other, c_ref, t_ref, sym, turn, total):
    per_step, _, depth, rows, block = direct.shape
    mine, core = place[0], place[1]
    step = pl.program_id(0)

    for u in range(per_step):
        b = step * per_step + u
        cols = slice(u * block, (u + 1) * block)

        @pl.when(b >= mine)
        def _():
            for k in range(depth):
                for y in range(YLO):
                    at = k * block + y * CORE * rows
                    sym[pl.ds(pl.multiple_of(at + core * rows, rows), rows), cols] = direct[u, y, k]
                    sym[pl.ds(pl.multiple_of(at + (1 - core) * rows, rows), rows), cols] = direct_other[u, y, k]

        @pl.when(b == mine)
        def _():
            row = lax.broadcasted_iota(jnp.int32, (block, block), 0)
            column = lax.broadcasted_iota(jnp.int32, (block, block), 1)
            for k in range(depth):
                upper = sym[k * block:(k + 1) * block, cols]
                sym[k * block:(k + 1) * block, cols] = jnp.where(row <= column, upper, transposed(upper))

        @pl.when(b < mine)
        def _():
            for k in range(depth):
                for y in range(YLO):
                    at = k * block + y * CORE * rows
                    turn[pl.ds(pl.multiple_of(at + core * rows, rows), rows), :] = turned[u, y, k]
                    turn[pl.ds(pl.multiple_of(at + (1 - core) * rows, rows), rows), :] = turned_other[u, y, k]
            for k in range(depth):
                sym[k * block:(k + 1) * block, cols] = transposed(turn[k * block:(k + 1) * block])

    accumulate(total, jnp.dot(sym[...], c_ref[...], preferred_element_type=F32))

    @pl.when(step == pl.num_programs(0) - 1)
    def _():
        lanes = t_ref.shape[3]
        for part in range(t_ref.shape[0]):
            for k in range(depth):
                t_ref[part, k] = total[k * block:(k + 1) * block, part * lanes:(part + 1) * lanes].astype(BF16)


def first_half(place, direct, direct_other, turned, turned_other, picked, name):
    _, _, depth, rows, block = direct.shape
    size, width = picked.shape
    per_step = 2
    piece = pl.BlockSpec((per_step, YLO, depth, rows, block), lambda g, s: (g, 0, 0, 0, 0))
    out = (BLOCKS, depth, block, width // BLOCKS)
    return pl.pallas_call(
        first_kernel,
        out_shape=jax.ShapeDtypeStruct(out, BF16),
        grid_spec=pltpu.PrefetchScalarGridSpec(
            num_scalar_prefetch=1,
            grid=(BLOCKS // per_step,),
            in_specs=[piece, piece, piece, piece,
                      pl.BlockSpec((per_step * block, width), lambda g, s: (g, 0))],
            out_specs=pl.BlockSpec(out, lambda g, s: (0, 0, 0, 0)),
            scratch_shapes=[pltpu.VMEM((depth * block, per_step * block), BF16),
                            pltpu.VMEM((depth * block, block), BF16),
                            pltpu.VMEM((depth * block, width), F32)],
        ),
        compiler_params=PARAMS,
        name=name,
    )(place, direct, direct_other, turned, turned_other, picked)


def second_kernel(t_ref, c_ref, out_ref, left, total):
    per_step, depth, block, lanes = t_ref.shape
    rows = lanes // YLO
    for u in range(per_step):
        for k in range(depth):
            left[k * lanes:(k + 1) * lanes, u * block:(u + 1) * block] = transposed(t_ref[u, k])
    accumulate(total, jnp.dot(left[...], c_ref[...], preferred_element_type=F32))

    @pl.when(pl.program_id(0) == pl.num_programs(0) - 1)
    def _():
        for c in range(COLS):
            for y in range(YLO):
                for k in range(depth):
                    at = k * lanes + y * rows
                    out_ref[c, y, k] = total[at:at + rows, c * block:(c + 1) * block].astype(BF16)


def second_half(partial_value, orbitals):
    _, depth, block, lanes = partial_value.shape
    size = orbitals.shape[0]
    rows = lanes // YLO
    per_step = 2
    out = (COLS, YLO, depth, rows, block)
    return pl.pallas_call(
        second_kernel,
        out_shape=jax.ShapeDtypeStruct(out, BF16),
        grid=(BLOCKS // per_step,),
        in_specs=[pl.BlockSpec((per_step, depth, block, lanes), lambda g: (g, 0, 0, 0)),
                  pl.BlockSpec((per_step * block, size), lambda g: (g, 0))],
        out_specs=pl.BlockSpec(out, lambda g: (0, 0, 0, 0, 0)),
        scratch_shapes=[pltpu.VMEM((depth * lanes, per_step * block), BF16),
                        pltpu.VMEM((depth * lanes, size), F32)],
        compiler_params=PARAMS,
        name="second_half",
    )(partial_value, orbitals)


def second_side_kernel(place, t_ref, other_ref, c_ref, keep, send, left, total, final):
    per_step, _, block, lanes = t_ref.shape
    rows = lanes // YLO
    ylo, core = place[0], place[1]
    for u in range(per_step):
        cols = slice(u * block, (u + 1) * block)
        own = transposed(t_ref[u, 0])
        other = transposed(other_ref[u, 0])
        for y in range(YLO):
            at = y * CORE * rows
            left[pl.ds(pl.multiple_of(at + core * rows, rows), rows), cols] = own[y * rows:(y + 1) * rows]
            left[pl.ds(pl.multiple_of(at + (1 - core) * rows, rows), rows), cols] = other[y * rows:(y + 1) * rows]
    accumulate(total, jnp.dot(left[...], c_ref[...], preferred_element_type=F32))

    @pl.when(pl.program_id(0) == pl.num_programs(0) - 1)
    def _():
        for part in range(total.shape[1] // block):
            cols = slice(part * block, (part + 1) * block)
            final[cols] = transposed(total[:, cols].astype(BF16))
        for z in range(Z):
            at = z * YLO * rows
            keep[z] = final[pl.ds(pl.multiple_of(at + ylo * rows, rows), rows)]
            send[z] = final[pl.ds(pl.multiple_of(at + (1 - ylo) * rows, rows), rows)]


def second_half_side(place, own, other, picked):
    _, _, block, lanes = own.shape
    size, width = picked.shape
    per_step = 2
    piece = pl.BlockSpec((per_step, 1, block, lanes), lambda g, s: (g, 0, 0, 0))
    out = jax.ShapeDtypeStruct((Z, lanes // YLO, block), BF16)
    whole = pl.BlockSpec(out.shape, lambda g, s: (0, 0, 0))
    return pl.pallas_call(
        second_side_kernel,
        out_shape=[out, out],
        grid_spec=pltpu.PrefetchScalarGridSpec(
            num_scalar_prefetch=1,
            grid=(BLOCKS // per_step,),
            in_specs=[piece, piece, pl.BlockSpec((per_step * block, width), lambda g, s: (g, 0))],
            out_specs=[whole, whole],
            scratch_shapes=[pltpu.VMEM((block, per_step * block), BF16),
                            pltpu.VMEM((block, width), F32),
                            pltpu.VMEM((width, block), BF16)],
        ),
        compiler_params=PARAMS,
        name="second_half_side",
    )(place, own, other, picked)


def spread_kernel(place, x_ref, *out_refs):
    for d in range(BLOCKS):
        out_refs[d][...] = x_ref[(place[0] + d) % BLOCKS]


def spread(mine, value):
    vmem = pl.BlockSpec(memory_space=pltpu.VMEM)
    return pl.pallas_call(
        spread_kernel,
        out_shape=[jax.ShapeDtypeStruct(value.shape[1:], BF16)] * BLOCKS,
        in_specs=[pl.BlockSpec(memory_space=pltpu.SMEM), vmem],
        out_specs=[vmem] * BLOCKS,
        compiler_params=SMALL,
        name="spread",
    )(mine, value)


def join_kernel(place, keep, got, *out_refs):
    z, ylo = place[0], place[1]
    for d in range(BLOCKS):
        out_refs[d][ylo] = keep[(z + d) % BLOCKS]
        out_refs[d][1 - ylo] = got[(z + d) % BLOCKS]


def join_and_spread(place, keep, got):
    vmem = pl.BlockSpec(memory_space=pltpu.VMEM)
    return pl.pallas_call(
        join_kernel,
        out_shape=[jax.ShapeDtypeStruct((YLO,) + keep.shape[1:], BF16)] * BLOCKS,
        in_specs=[pl.BlockSpec(memory_space=pltpu.SMEM), vmem, vmem],
        out_specs=[vmem] * BLOCKS,
        compiler_params=SMALL,
        name="join_and_spread",
    )(place, keep, got)


def collect_kernel(place, *refs):
    out_ref = refs[BLOCKS]
    for d in range(BLOCKS):
        out_ref[(place[0] + BLOCKS - d) % BLOCKS] = refs[d][...]


def collect(mine, parts):
    vmem = pl.BlockSpec(memory_space=pltpu.VMEM)
    return pl.pallas_call(
        collect_kernel,
        out_shape=jax.ShapeDtypeStruct((BLOCKS,) + parts[0].shape, BF16),
        in_specs=[pl.BlockSpec(memory_space=pltpu.SMEM)] + [vmem] * BLOCKS,
        out_specs=vmem,
        compiler_params=SMALL,
        name="collect",
    )(mine, *parts)


def collect_last_kernel(place, *refs):
    out_ref = refs[BLOCKS]
    for d in range(BLOCKS):
        for y in range(YLO):
            out_ref[y, (place[0] + BLOCKS - d) % BLOCKS] = refs[d][y]


def collect_last(mine, parts):
    vmem = pl.BlockSpec(memory_space=pltpu.VMEM)
    return pl.pallas_call(
        collect_last_kernel,
        out_shape=jax.ShapeDtypeStruct((YLO, BLOCKS) + parts[0].shape[1:], BF16),
        in_specs=[pl.BlockSpec(memory_space=pltpu.SMEM)] + [vmem] * BLOCKS,
        out_specs=vmem,
        compiler_params=SMALL,
        name="collect_last",
    )(mine, *parts)


def rotate(parts, axes):
    out = [parts[0]]
    for d in range(1, BLOCKS):
        out.append(lax.ppermute(parts[d], axes, [(i, (i + d) % BLOCKS) for i in range(BLOCKS)]))
    return out


def swap(value, axis):
    return lax.ppermute(value, axis, [(0, 1), (1, 0)])


def per_device(half_panel, orbitals):
    pairs, rows, block = half_panel.shape
    side_pairs = Z * YLO
    main_pairs = pairs - side_pairs
    depth = main_pairs // (COLS * YLO)
    z, ylo, core = lax.axis_index("z"), lax.axis_index("ylo"), lax.axis_index("core")
    c = lax.axis_index("x") * YHI + lax.axis_index("yhi")

    def scalars(*values):
        return jnp.stack(values).astype(jnp.int32)

    def deep(value):
        return value.reshape(BLOCKS, YLO, 1, rows, block)

    together = lax.optimization_barrier

    side = half_panel[main_pairs:].reshape(YLO, Z, rows, block)
    with jax.named_scope("panels_in"):
        own = half_panel[:main_pairs].reshape(COLS * YLO, depth, rows, block)
        own = lax.all_to_all(own, PLANE, 0, 0, tiled=True)
        own = own.reshape(COLS, YLO, depth, rows, block)
    with jax.named_scope("side_in"):
        got = swap(lax.dynamic_index_in_dim(side, 1 - ylo, 0, keepdims=False), "ylo")
        keep = lax.dynamic_index_in_dim(side, ylo, 0, keepdims=False)
        parts = rotate(join_and_spread(scalars(z, ylo), keep, got), "z")
        side_own = collect(scalars(z), parts)
    picked = pick_columns(scalars(core), orbitals)
    own, side_own, picked = together((own, side_own, picked))

    with jax.named_scope("mirror"):
        own_low = lax.all_to_all(own, "z", 0, 0, tiled=True)
    other = swap(own, "core")
    with jax.named_scope("side_mirror"):
        side_other = swap(side_own, "core")
        parts = rotate(spread(scalars(c), side_own), SIDE)
        side_low = collect(scalars(c), parts)
        side_other_low = swap(side_low, "core")
        side_partial = first_half(
            scalars(c, core), deep(side_low), deep(side_other_low), deep(side_own), deep(side_other),
            picked, "first_half_side"
        )
    own_low, other, side_partial = together((own_low, other, side_partial))

    other_low = swap(own_low, "core")
    partial_value = first_half(scalars(z, core), own, other, own_low, other_low, picked, "first_half")
    with jax.named_scope("partial"):
        partial_value = lax.all_to_all(partial_value, "z", 0, 0, tiled=True)
    with jax.named_scope("side_partial"):
        parts = rotate(spread(scalars(c), side_partial), SIDE)
        side_partial = collect(scalars(c), parts)
        side_partial_other = swap(side_partial, "core")
        keep, send = second_half_side(scalars(ylo, core), side_partial, side_partial_other, picked)
    partial_value, keep, send = together((partial_value, keep, send))

    got = swap(send, "ylo")
    result = second_half(partial_value, orbitals)
    with jax.named_scope("panels_out"):
        result = result.reshape(COLS * YLO, depth, rows, block)
        result = lax.all_to_all(result, PLANE, 0, 0, tiled=True)
        result = result.reshape(main_pairs, rows, block)
    with jax.named_scope("side_out"):
        parts = rotate(join_and_spread(scalars(z, ylo), keep, got), "z")
        side_result = collect_last(scalars(z), parts).reshape(side_pairs, rows, block)
    return jnp.concatenate([result, side_result], axis=0)


def solution(mesh):
    fine = Mesh(mesh.devices.reshape(Z, YLO, CORE, X, YHI), ("z", "ylo", "core", "x", "yhi"))
    spec = P(None, ("z", "ylo", "core"), ("x", "yhi"))
    return jax.shard_map(
        per_device, mesh=fine, in_specs=(spec, P()), out_specs=spec, check_vma=False
    )
```

```python
import jax
import jax.numpy as jnp
from jax import lax
from jax.experimental import pallas as pl
from jax.experimental.pallas import tpu as pltpu
from jax.sharding import Mesh, PartitionSpec as P

Z, YLO, CORE, X, YHI = 8, 2, 2, 4, 2
BLOCKS = 8
CHUNKS = 4
SIDE = ("x", "yhi")
LINE = ("z", "ylo")
F32 = jnp.float32
BF16 = jnp.bfloat16
BIG = pltpu.CompilerParams(vmem_limit_bytes=26 * 2**20)
SMALL = pltpu.CompilerParams(vmem_limit_bytes=8 * 2**20)
SCALARS = pl.BlockSpec(memory_space=pltpu.SMEM)
VMEM = pl.BlockSpec(memory_space=pltpu.VMEM)
HBM = pl.BlockSpec(memory_space=pltpu.HBM)


def transposed(block):
    size = block.shape[1]
    row = lax.broadcasted_iota(jnp.int32, (size, size), 0)
    column = lax.broadcasted_iota(jnp.int32, (size, size), 1)
    eye = (row == column).astype(F32).astype(BF16)
    return lax.dot_general(
        eye, block, (((1,), (1,)), ((), ())), preferred_element_type=F32
    ).astype(BF16)


def aligned(start, size):
    return pl.ds(pl.multiple_of(start, size), size)


def fetches(c_hbm, c_ref, sems):
    count = c_ref.shape[0]
    rows = c_ref.shape[1]
    copies = [
        pltpu.make_async_copy(c_hbm.at[pl.ds(g * rows, rows)], c_ref.at[g], sems.at[g])
        for g in range(count)
    ]
    for copy in copies:
        copy.start()
    return copies


def orbital_scratch(size):
    return [pltpu.VMEM((CHUNKS, size // CHUNKS, size), BF16), pltpu.SemaphoreType.DMA((CHUNKS,))]


def add_to(total, product, step):
    if step == 0:
        total[...] = product
    else:
        total[...] += product


def first_main_kernel(place, own, other, low, other_low, c_hbm, t_ref, c_ref, sems, sym, turn, total):
    _, halves, _, rows, lanes = own.shape
    depth = t_ref.shape[1]
    height, block = CORE * rows, halves * lanes
    per_step = BLOCKS // CHUNKS
    z, ylo, core = place[0], place[1], place[2]
    copies = fetches(c_hbm, c_ref, sems)
    for step in range(CHUNKS):
        for u in range(per_step):
            b = step * per_step + u
            cols = slice(u * block, (u + 1) * block)

            @pl.when(b >= z)
            def _():
                for k in range(depth):
                    for h in range(halves):
                        part = slice(u * block + h * lanes, u * block + (h + 1) * lanes)
                        sym[aligned(k * height + core * rows, rows), part] = own[b, h, core * depth + k]
                        sym[aligned(k * height + (1 - core) * rows, rows), part] = other[b, h, core * depth + k]

            @pl.when(b <= z)
            def _():
                for k in range(depth):
                    for y in range(YLO):
                        at = k * block + y * height
                        turn[aligned(at + core * rows, rows), :] = low[b * YLO + y, core * depth + k]
                        turn[aligned(at + (1 - core) * rows, rows), :] = other_low[b * YLO + y, core * depth + k]

            @pl.when(b == z)
            def _():
                row = lax.broadcasted_iota(jnp.int32, (height, block), 0) + ylo * height
                column = lax.broadcasted_iota(jnp.int32, (height, block), 1)
                for k in range(depth):
                    at = slice(k * height, (k + 1) * height)
                    lower = transposed(turn[k * block:(k + 1) * block])
                    sym[at, cols] = jnp.where(row <= column, sym[at, cols], lower)

            @pl.when(b < z)
            def _():
                for k in range(depth):
                    sym[k * height:(k + 1) * height, cols] = transposed(turn[k * block:(k + 1) * block])

        copies[step].wait()
        add_to(total, jnp.dot(sym[...], c_ref[step], preferred_element_type=F32), step)
    for e in range(t_ref.shape[0]):
        for k in range(depth):
            t_ref[e, k] = total[k * height:(k + 1) * height, e * height:(e + 1) * height].astype(BF16)


def first_main(place, own, other, low, other_low, orbitals):
    size = orbitals.shape[0]
    _, halves, pairs, rows, lanes = own.shape
    depth = pairs // CORE
    height, block = CORE * rows, halves * lanes
    return pl.pallas_call(
        first_main_kernel,
        out_shape=jax.ShapeDtypeStruct((Z * YLO, depth, height, height), BF16),
        in_specs=[SCALARS, VMEM, VMEM, VMEM, VMEM, HBM],
        out_specs=VMEM,
        scratch_shapes=orbital_scratch(size) + [
            pltpu.VMEM((depth * height, size // CHUNKS), BF16),
            pltpu.VMEM((depth * block, height), BF16),
            pltpu.VMEM((depth * height, size), F32)],
        compiler_params=BIG,
        name="first_main",
    )(place, own, other, low, other_low, orbitals)


def second_main_kernel(place, t_ref, c_hbm, keep, send, c_ref, sems, left, total):
    count, depth, height, lanes = t_ref.shape
    _, _, rows, block = keep.shape
    per_step = count // CHUNKS
    core = place[0]
    copies = fetches(c_hbm, c_ref, sems)
    for step in range(CHUNKS):
        for u in range(per_step):
            for k in range(depth):
                left[k * lanes:(k + 1) * lanes, u * height:(u + 1) * height] = transposed(t_ref[step * per_step + u, k])
        copies[step].wait()
        add_to(total, jnp.dot(left[...], c_ref[step], preferred_element_type=F32), step)
    for c in range(BLOCKS):
        cols = slice(c * block, (c + 1) * block)
        for k in range(depth):
            keep[c, k] = total[aligned(k * lanes + core * rows, rows), cols].astype(BF16)
            send[c, k] = total[aligned(k * lanes + (1 - core) * rows, rows), cols].astype(BF16)


def second_main(place, partial_value, orbitals):
    _, depth, height, lanes = partial_value.shape
    size = orbitals.shape[0]
    out = jax.ShapeDtypeStruct((BLOCKS, depth, lanes // CORE, size // BLOCKS), BF16)
    return pl.pallas_call(
        second_main_kernel,
        out_shape=[out, out],
        in_specs=[SCALARS, VMEM, HBM],
        out_specs=[VMEM, VMEM],
        scratch_shapes=orbital_scratch(size) + [
            pltpu.VMEM((depth * lanes, size // CHUNKS), BF16),
            pltpu.VMEM((depth * lanes, size), F32)],
        compiler_params=BIG,
        name="second_main",
    )(place, partial_value, orbitals)


def first_side_kernel(place, direct, direct_other, turned, turned_other, c_hbm, *rest):
    t_refs = rest[:BLOCKS]
    c_ref, sems, chosen, sym, turn, total = rest[BLOCKS:]
    _, _, rows, block = direct.shape
    lanes = t_refs[0].shape[1]
    per_step = BLOCKS // CHUNKS
    mine, core = place[0], place[1]
    copies = fetches(c_hbm, c_ref, sems)
    for step in range(CHUNKS):
        for u in range(per_step):
            b = step * per_step + u
            cols = slice(u * block, (u + 1) * block)

            @pl.when(b >= mine)
            def _():
                for y in range(YLO):
                    at = y * CORE * rows
                    sym[aligned(at + core * rows, rows), cols] = direct[b, y]
                    sym[aligned(at + (1 - core) * rows, rows), cols] = direct_other[b, y]

            @pl.when(b == mine)
            def _():
                row = lax.broadcasted_iota(jnp.int32, (block, block), 0)
                column = lax.broadcasted_iota(jnp.int32, (block, block), 1)
                upper = sym[:, cols]
                sym[:, cols] = jnp.where(row <= column, upper, transposed(upper))

            @pl.when(b < mine)
            def _():
                for y in range(YLO):
                    at = y * CORE * rows
                    turn[aligned(at + core * rows, rows), :] = turned[b, y]
                    turn[aligned(at + (1 - core) * rows, rows), :] = turned_other[b, y]
                sym[:, cols] = transposed(turn[...])

        copies[step].wait()
        for e in range(BLOCKS):
            chosen[:, e * lanes:(e + 1) * lanes] = c_ref[step, :, aligned(e * block + core * lanes, lanes)]
        add_to(total, jnp.dot(sym[...], chosen[...], preferred_element_type=F32), step)
    for d in range(BLOCKS):
        t_refs[d][...] = total[:, aligned((mine + d) % BLOCKS * lanes, lanes)].astype(BF16)


def first_side(place, direct, direct_other, turned, turned_other, orbitals):
    size = orbitals.shape[0]
    block = direct.shape[3]
    lanes = block // CORE
    return pl.pallas_call(
        first_side_kernel,
        out_shape=[jax.ShapeDtypeStruct((block, lanes), BF16)] * BLOCKS,
        in_specs=[SCALARS, VMEM, VMEM, VMEM, VMEM, HBM],
        out_specs=[VMEM] * BLOCKS,
        scratch_shapes=orbital_scratch(size) + [
            pltpu.VMEM((size // CHUNKS, size // CORE), BF16),
            pltpu.VMEM((block, size // CHUNKS), BF16),
            pltpu.VMEM((block, block), BF16),
            pltpu.VMEM((block, size // CORE), F32)],
        compiler_params=BIG,
        name="first_side",
    )(place, direct, direct_other, turned, turned_other, orbitals)


def second_side_kernel(place, *refs):
    t_refs, c_hbm = refs[:BLOCKS], refs[BLOCKS]
    keep, send, c_ref, sems, left, total, final = refs[BLOCKS + 1:]
    block, lanes = t_refs[0].shape
    rows = keep.shape[1]
    mine, core = place[0], place[1]
    width = c_ref.shape[1]
    copies = fetches(c_hbm, c_ref, sems)
    for d in range(BLOCKS):
        left[:, aligned((mine + BLOCKS - d) % BLOCKS * block, block)] = transposed(t_refs[d][...])
    for step in range(CHUNKS):
        copies[step].wait()
        add_to(
            total,
            jnp.dot(left[:, step * width:(step + 1) * width], c_ref[step], preferred_element_type=F32),
            step,
        )
    for b in range(BLOCKS):
        cols = slice(b * block, (b + 1) * block)
        final[cols] = transposed(total[:, cols].astype(BF16))
    for e in range(keep.shape[0]):
        keep[e] = final[aligned(e * CORE * rows + core * rows, rows)]
        send[e] = final[aligned(e * CORE * rows + (1 - core) * rows, rows)]


def second_side(place, parts, orbitals):
    size = orbitals.shape[0]
    _, lanes = parts[0].shape
    rows = lanes // CORE
    out = jax.ShapeDtypeStruct((Z * YLO, rows, lanes), BF16)
    return pl.pallas_call(
        second_side_kernel,
        out_shape=[out, out],
        in_specs=[SCALARS] + [VMEM] * BLOCKS + [HBM],
        out_specs=[VMEM, VMEM],
        scratch_shapes=orbital_scratch(size) + [
            pltpu.VMEM((lanes, size), BF16),
            pltpu.VMEM((lanes, size), F32),
            pltpu.VMEM((size, lanes), BF16)],
        compiler_params=BIG,
        name="second_side",
    )(place, *parts, orbitals)


def beside_kernel(place, keep, got, out_ref):
    lanes = keep.shape[2]
    core = place[0]
    out_ref[:, :, aligned(core * lanes, lanes)] = keep[...]
    out_ref[:, :, aligned((1 - core) * lanes, lanes)] = got[...]


def beside(place, keep, got):
    count, rows, lanes = keep.shape
    return pl.pallas_call(
        beside_kernel,
        out_shape=jax.ShapeDtypeStruct((count, rows, CORE * lanes), BF16),
        in_specs=[SCALARS, VMEM, VMEM],
        out_specs=VMEM,
        compiler_params=SMALL,
        name="beside",
    )(place, keep, got)


def spread_kernel(place, x_ref, *out_refs):
    for d in range(BLOCKS):
        out_refs[d][...] = x_ref[(place[0] + d) % BLOCKS]


def spread(place, value):
    return pl.pallas_call(
        spread_kernel,
        out_shape=[jax.ShapeDtypeStruct(value.shape[1:], BF16)] * BLOCKS,
        in_specs=[SCALARS, VMEM],
        out_specs=[VMEM] * BLOCKS,
        compiler_params=SMALL,
        name="spread",
    )(place, value)


def collect_kernel(place, *refs):
    out_ref = refs[BLOCKS]
    for d in range(BLOCKS):
        out_ref[(place[0] + BLOCKS - d) % BLOCKS] = refs[d][...]


def collect(place, parts):
    return pl.pallas_call(
        collect_kernel,
        out_shape=jax.ShapeDtypeStruct((BLOCKS,) + parts[0].shape, BF16),
        in_specs=[SCALARS] + [VMEM] * BLOCKS,
        out_specs=VMEM,
        compiler_params=SMALL,
        name="collect",
    )(place, *parts)


def collect_main_kernel(place, *refs):
    out_ref = refs[BLOCKS]
    lanes = out_ref.shape[4]
    for d in range(BLOCKS):
        b = (place[0] + BLOCKS - d) % BLOCKS
        for h in range(out_ref.shape[1]):
            out_ref[b, h] = refs[d][:, :, h * lanes:(h + 1) * lanes]


def collect_main(place, parts):
    pairs, rows, block = parts[0].shape
    return pl.pallas_call(
        collect_main_kernel,
        out_shape=jax.ShapeDtypeStruct((BLOCKS, YLO, pairs, rows, block // YLO), BF16),
        in_specs=[SCALARS] + [VMEM] * BLOCKS,
        out_specs=VMEM,
        compiler_params=SMALL,
        name="collect_main",
    )(place, *parts)


def join_kernel(place, keep, got, *out_refs):
    depth = keep.shape[1]
    c, core = place[0], place[1]
    for d in range(BLOCKS):
        out_refs[d][pl.ds(core * depth, depth)] = keep[(c + d) % BLOCKS]
        out_refs[d][pl.ds((1 - core) * depth, depth)] = got[(c + d) % BLOCKS]


def join_and_spread(place, keep, got):
    _, depth, rows, block = keep.shape
    return pl.pallas_call(
        join_kernel,
        out_shape=[jax.ShapeDtypeStruct((CORE * depth, rows, block), BF16)] * BLOCKS,
        in_specs=[SCALARS, VMEM, VMEM],
        out_specs=[VMEM] * BLOCKS,
        compiler_params=SMALL,
        name="join_and_spread",
    )(place, keep, got)


def finish_kernel(place, *refs):
    side_ref, out_ref = refs[BLOCKS:]
    pairs = refs[0].shape[0]
    for d in range(BLOCKS):
        out_ref[pl.ds((place[0] + BLOCKS - d) % BLOCKS * pairs, pairs)] = refs[d][...]
    out_ref[BLOCKS * pairs:] = side_ref[...]


def finish(place, parts, side):
    pairs, rows, block = parts[0].shape
    return pl.pallas_call(
        finish_kernel,
        out_shape=jax.ShapeDtypeStruct((BLOCKS * pairs + side.shape[0], rows, block), BF16),
        in_specs=[SCALARS] + [VMEM] * (BLOCKS + 1),
        out_specs=VMEM,
        compiler_params=SMALL,
        name="finish",
    )(place, *parts, side)


def rotate(parts, axes):
    out = [parts[0]]
    for d in range(1, BLOCKS):
        out.append(lax.ppermute(parts[d], axes, [(i, (i + d) % BLOCKS) for i in range(BLOCKS)]))
    return out


def swap(value):
    return lax.ppermute(value, "core", [(0, 1), (1, 0)])


def per_device(half_panel, orbitals):
    pairs, rows, block = half_panel.shape
    side_pairs = Z * YLO
    main_pairs = pairs - side_pairs
    depth = main_pairs // BLOCKS
    z, ylo, core = lax.axis_index("z"), lax.axis_index("ylo"), lax.axis_index("core")
    c = lax.axis_index("x") * YHI + lax.axis_index("yhi")

    def scalars(*values):
        return jnp.stack(values).astype(jnp.int32)

    together = lax.optimization_barrier

    with jax.named_scope("side_in"):
        side = lax.all_to_all(half_panel[main_pairs:], LINE, 0, 0, tiled=True)
        side = side.reshape(Z, YLO, rows, block)
    with jax.named_scope("main_in"):
        own = half_panel[:main_pairs].reshape(BLOCKS, depth, rows, block)
        own = collect_main(scalars(c), rotate(spread(scalars(c), own), SIDE))
    own, side = together((own, side))

    with jax.named_scope("mirror"):
        low = own.reshape(Z * YLO, depth, rows, block // YLO)
        low = lax.all_to_all(low, LINE, 0, 0, tiled=True)
    other = swap(own)
    with jax.named_scope("side_mirror"):
        side_other = swap(side)
        side_low = collect(scalars(c), rotate(spread(scalars(c), side), SIDE))
        side_other_low = swap(side_low)
        side_parts = first_side(
            scalars(c, core), side_low, side_other_low, side, side_other, orbitals
        )
    low, other, side_parts = together((low, other, side_parts))

    other_low = swap(low)
    partial_value = first_main(scalars(z, ylo, core), own, other, low, other_low, orbitals)
    with jax.named_scope("partial"):
        partial_value = lax.all_to_all(partial_value, LINE, 0, 0, tiled=True)
    with jax.named_scope("side_partial"):
        keep, send = second_side(scalars(c, core), rotate(side_parts, SIDE), orbitals)
        side = beside(scalars(core), keep, swap(send))
    partial_value, side = together((partial_value, side))

    with jax.named_scope("side_out"):
        side = lax.all_to_all(side, LINE, 0, 0, tiled=True)
    keep, send = second_main(scalars(core), partial_value, orbitals)
    with jax.named_scope("main_out"):
        parts = rotate(join_and_spread(scalars(c, core), keep, swap(send)), SIDE)
    return finish(scalars(c), parts, side)


def solution(mesh):
    fine = Mesh(mesh.devices.reshape(Z, YLO, CORE, X, YHI), ("z", "ylo", "core", "x", "yhi"))
    spec = P(None, ("z", "ylo", "core"), ("x", "yhi"))
    return jax.shard_map(
        per_device, mesh=fine, in_specs=(spec, P()), out_specs=spec, check_vma=False
    )
```

```python
import jax
import jax.numpy as jnp
from jax import lax
from jax.experimental import pallas as pl
from jax.experimental.pallas import tpu as pltpu
from jax.sharding import Mesh, PartitionSpec as P

Z, YLO, CORE, X, YHI = 8, 2, 2, 4, 2
COLS = X * YHI
BLOCKS = 8
PLANE = ("x", "yhi", "ylo")
SIDE = ("x", "yhi")
F32 = jnp.float32
BF16 = jnp.bfloat16
WIDE = pltpu.CompilerParams(vmem_limit_bytes=56 * 2**20)
NARROW = pltpu.CompilerParams(vmem_limit_bytes=60 * 2**20)
SMALL = pltpu.CompilerParams(vmem_limit_bytes=8 * 2**20)


def transposed(block):
    size = block.shape[1]
    row = lax.broadcasted_iota(jnp.int32, (size, size), 0)
    column = lax.broadcasted_iota(jnp.int32, (size, size), 1)
    eye = (row == column).astype(F32).astype(BF16)
    return lax.dot_general(
        eye, block, (((1,), (1,)), ((), ())), preferred_element_type=F32
    ).astype(BF16)


def pick_kernel(core_ref, c_ref, out_ref):
    block = c_ref.shape[1] // BLOCKS
    lanes = block // CORE
    half = lanes // 2
    for core in range(CORE):
        @pl.when(core_ref[0] == core)
        def _():
            for b in range(BLOCKS):
                pieces = []
                for y in range(YLO):
                    tile = c_ref[:, b * block + y * lanes:b * block + (y + 1) * lanes]
                    pieces.append(tile[:, core * half:(core + 1) * half])
                out_ref[:, b * lanes:(b + 1) * lanes] = jnp.concatenate(pieces, axis=1)


def pick_columns(core, orbitals):
    size = orbitals.shape[0]
    block = size // BLOCKS
    return pl.pallas_call(
        pick_kernel,
        out_shape=jax.ShapeDtypeStruct((size, size // CORE), BF16),
        grid_spec=pltpu.PrefetchScalarGridSpec(
            num_scalar_prefetch=1,
            grid=(BLOCKS,),
            in_specs=[pl.BlockSpec((block, size), lambda g, s: (g, 0))],
            out_specs=pl.BlockSpec((block, size // CORE), lambda g, s: (g, 0)),
        ),
        name="pick_columns",
    )(core, orbitals)


def accumulate(total, product):
    step = pl.program_id(0)

    @pl.when(step == 0)
    def _():
        total[...] = product

    @pl.when(step > 0)
    def _():
        total[...] += product


def first_kernel(place, direct, direct_other, turned, turned_other, c_ref, t_ref, sym, turn, total):
    per_step, _, depth, rows, block = direct.shape
    mine, core = place[0], place[1]
    step = pl.program_id(0)

    for u in range(per_step):
        b = step * per_step + u
        cols = slice(u * block, (u + 1) * block)

        @pl.when(b >= mine)
        def _():
            for k in range(depth):
                for y in range(YLO):
                    at = k * block + y * CORE * rows
                    sym[pl.ds(pl.multiple_of(at + core * rows, rows), rows), cols] = direct[u, y, k]
                    sym[pl.ds(pl.multiple_of(at + (1 - core) * rows, rows), rows), cols] = direct_other[u, y, k]

        @pl.when(b == mine)
        def _():
            row = lax.broadcasted_iota(jnp.int32, (block, block), 0)
            column = lax.broadcasted_iota(jnp.int32, (block, block), 1)
            for k in range(depth):
                upper = sym[k * block:(k + 1) * block, cols]
                sym[k * block:(k + 1) * block, cols] = jnp.where(row <= column, upper, transposed(upper))

        @pl.when(b < mine)
        def _():
            for k in range(depth):
                for y in range(YLO):
                    at = k * block + y * CORE * rows
                    turn[pl.ds(pl.multiple_of(at + core * rows, rows), rows), :] = turned[u, y, k]
                    turn[pl.ds(pl.multiple_of(at + (1 - core) * rows, rows), rows), :] = turned_other[u, y, k]
            for k in range(depth):
                sym[k * block:(k + 1) * block, cols] = transposed(turn[k * block:(k + 1) * block])

    accumulate(total, jnp.dot(sym[...], c_ref[...], preferred_element_type=F32))

    @pl.when(step == pl.num_programs(0) - 1)
    def _():
        lanes = t_ref.shape[3]
        for part in range(t_ref.shape[0]):
            for k in range(depth):
                t_ref[part, k] = total[k * block:(k + 1) * block, part * lanes:(part + 1) * lanes].astype(BF16)


def first_half(place, direct, direct_other, turned, turned_other, picked, name):
    _, _, depth, rows, block = direct.shape
    size, width = picked.shape
    per_step = 2
    piece = pl.BlockSpec((per_step, YLO, depth, rows, block), lambda g, s: (g, 0, 0, 0, 0))
    out = (BLOCKS, depth, block, width // BLOCKS)
    return pl.pallas_call(
        first_kernel,
        out_shape=jax.ShapeDtypeStruct(out, BF16),
        grid_spec=pltpu.PrefetchScalarGridSpec(
            num_scalar_prefetch=1,
            grid=(BLOCKS // per_step,),
            in_specs=[piece, piece, piece, piece,
                      pl.BlockSpec((per_step * block, width), lambda g, s: (g, 0))],
            out_specs=pl.BlockSpec(out, lambda g, s: (0, 0, 0, 0)),
            scratch_shapes=[pltpu.VMEM((depth * block, per_step * block), BF16),
                            pltpu.VMEM((depth * block, block), BF16),
                            pltpu.VMEM((depth * block, width), F32)],
        ),
        compiler_params=NARROW,
        name=name,
    )(place, direct, direct_other, turned, turned_other, picked)


def second_kernel(t_ref, c_ref, out_ref, left, total):
    per_step, depth, block, lanes = t_ref.shape
    rows = lanes // YLO
    for u in range(per_step):
        for k in range(depth):
            left[k * lanes:(k + 1) * lanes, u * block:(u + 1) * block] = transposed(t_ref[u, k])
    accumulate(total, jnp.dot(left[...], c_ref[...], preferred_element_type=F32))

    @pl.when(pl.program_id(0) == pl.num_programs(0) - 1)
    def _():
        for c in range(COLS):
            for y in range(YLO):
                for k in range(depth):
                    at = k * lanes + y * rows
                    out_ref[c, y, k] = total[at:at + rows, c * block:(c + 1) * block].astype(BF16)


def second_half(partial_value, orbitals):
    _, depth, block, lanes = partial_value.shape
    size = orbitals.shape[0]
    rows = lanes // YLO
    per_step = 2
    out = (COLS, YLO, depth, rows, block)
    return pl.pallas_call(
        second_kernel,
        out_shape=jax.ShapeDtypeStruct(out, BF16),
        grid=(BLOCKS // per_step,),
        in_specs=[pl.BlockSpec((per_step, depth, block, lanes), lambda g: (g, 0, 0, 0)),
                  pl.BlockSpec((per_step * block, size), lambda g: (g, 0))],
        out_specs=pl.BlockSpec(out, lambda g: (0, 0, 0, 0, 0)),
        scratch_shapes=[pltpu.VMEM((depth * lanes, per_step * block), BF16),
                        pltpu.VMEM((depth * lanes, size), F32)],
        compiler_params=WIDE,
        name="second_half",
    )(partial_value, orbitals)


def second_side_kernel(place, t_ref, other_ref, c_ref, keep, send, left, total, final):
    per_step, _, block, lanes = t_ref.shape
    rows = lanes // YLO
    ylo, core = place[0], place[1]
    for u in range(per_step):
        cols = slice(u * block, (u + 1) * block)
        own = transposed(t_ref[u, 0])
        other = transposed(other_ref[u, 0])
        for y in range(YLO):
            at = y * CORE * rows
            left[pl.ds(pl.multiple_of(at + core * rows, rows), rows), cols] = own[y * rows:(y + 1) * rows]
            left[pl.ds(pl.multiple_of(at + (1 - core) * rows, rows), rows), cols] = other[y * rows:(y + 1) * rows]
    accumulate(total, jnp.dot(left[...], c_ref[...], preferred_element_type=F32))

    @pl.when(pl.program_id(0) == pl.num_programs(0) - 1)
    def _():
        for part in range(total.shape[1] // block):
            cols = slice(part * block, (part + 1) * block)
            final[cols] = transposed(total[:, cols].astype(BF16))
        for z in range(Z):
            at = z * YLO * rows
            keep[z] = final[pl.ds(pl.multiple_of(at + ylo * rows, rows), rows)]
            send[z] = final[pl.ds(pl.multiple_of(at + (1 - ylo) * rows, rows), rows)]


def second_half_side(place, own, other, picked):
    _, _, block, lanes = own.shape
    size, width = picked.shape
    per_step = 2
    piece = pl.BlockSpec((per_step, 1, block, lanes), lambda g, s: (g, 0, 0, 0))
    out = jax.ShapeDtypeStruct((Z, lanes // YLO, block), BF16)
    whole = pl.BlockSpec(out.shape, lambda g, s: (0, 0, 0))
    return pl.pallas_call(
        second_side_kernel,
        out_shape=[out, out],
        grid_spec=pltpu.PrefetchScalarGridSpec(
            num_scalar_prefetch=1,
            grid=(BLOCKS // per_step,),
            in_specs=[piece, piece, pl.BlockSpec((per_step * block, width), lambda g, s: (g, 0))],
            out_specs=[whole, whole],
            scratch_shapes=[pltpu.VMEM((block, per_step * block), BF16),
                            pltpu.VMEM((block, width), F32),
                            pltpu.VMEM((width, block), BF16)],
        ),
        compiler_params=NARROW,
        name="second_half_side",
    )(place, own, other, picked)


def spread_kernel(place, x_ref, *out_refs):
    for d in range(BLOCKS):
        out_refs[d][...] = x_ref[(place[0] + d) % BLOCKS]


def spread(mine, value):
    vmem = pl.BlockSpec(memory_space=pltpu.VMEM)
    return pl.pallas_call(
        spread_kernel,
        out_shape=[jax.ShapeDtypeStruct(value.shape[1:], BF16)] * BLOCKS,
        in_specs=[pl.BlockSpec(memory_space=pltpu.SMEM), vmem],
        out_specs=[vmem] * BLOCKS,
        compiler_params=SMALL,
        name="spread",
    )(mine, value)


def join_kernel(place, keep, got, *out_refs):
    z, ylo = place[0], place[1]
    for d in range(BLOCKS):
        out_refs[d][ylo] = keep[(z + d) % BLOCKS]
        out_refs[d][1 - ylo] = got[(z + d) % BLOCKS]


def join_and_spread(place, keep, got):
    vmem = pl.BlockSpec(memory_space=pltpu.VMEM)
    return pl.pallas_call(
        join_kernel,
        out_shape=[jax.ShapeDtypeStruct((YLO,) + keep.shape[1:], BF16)] * BLOCKS,
        in_specs=[pl.BlockSpec(memory_space=pltpu.SMEM), vmem, vmem],
        out_specs=[vmem] * BLOCKS,
        compiler_params=SMALL,
        name="join_and_spread",
    )(place, keep, got)


def collect_kernel(place, *refs):
    out_ref = refs[BLOCKS]
    for d in range(BLOCKS):
        out_ref[(place[0] + BLOCKS - d) % BLOCKS] = refs[d][...]


def collect(mine, parts):
    vmem = pl.BlockSpec(memory_space=pltpu.VMEM)
    return pl.pallas_call(
        collect_kernel,
        out_shape=jax.ShapeDtypeStruct((BLOCKS,) + parts[0].shape, BF16),
        in_specs=[pl.BlockSpec(memory_space=pltpu.SMEM)] + [vmem] * BLOCKS,
        out_specs=vmem,
        compiler_params=SMALL,
        name="collect",
    )(mine, *parts)


def finish_kernel(place, *refs):
    main_ref, out_ref = refs[BLOCKS:]
    main = main_ref.shape[0]
    out_ref[:main] = main_ref[...]
    for d in range(BLOCKS):
        for y in range(YLO):
            out_ref[main + y * BLOCKS + (place[0] + BLOCKS - d) % BLOCKS] = refs[d][y]


def finish(mine, parts, main):
    pairs, rows, block = main.shape
    vmem = pl.BlockSpec(memory_space=pltpu.VMEM)
    return pl.pallas_call(
        finish_kernel,
        out_shape=jax.ShapeDtypeStruct((pairs + YLO * BLOCKS, rows, block), BF16),
        in_specs=[pl.BlockSpec(memory_space=pltpu.SMEM)] + [vmem] * (BLOCKS + 1),
        out_specs=vmem,
        compiler_params=SMALL,
        name="finish",
    )(mine, *parts, main)


def rotate(parts, axes):
    out = [parts[0]]
    for d in range(1, BLOCKS):
        out.append(lax.ppermute(parts[d], axes, [(i, (i + d) % BLOCKS) for i in range(BLOCKS)]))
    return out


def swap(value, axis):
    return lax.ppermute(value, axis, [(0, 1), (1, 0)])


def per_device(half_panel, orbitals):
    pairs, rows, block = half_panel.shape
    side_pairs = Z * YLO
    main_pairs = pairs - side_pairs
    depth = main_pairs // (COLS * YLO)
    z, ylo, core = lax.axis_index("z"), lax.axis_index("ylo"), lax.axis_index("core")
    c = lax.axis_index("x") * YHI + lax.axis_index("yhi")

    def scalars(*values):
        return jnp.stack(values).astype(jnp.int32)

    def deep(value):
        return value.reshape(BLOCKS, YLO, 1, rows, block)

    together = lax.optimization_barrier

    with jax.named_scope("side_in"):
        side = half_panel[main_pairs:].reshape(YLO, Z, rows, block)
        got = swap(lax.dynamic_index_in_dim(side, 1 - ylo, 0, keepdims=False), "ylo")
        keep = lax.dynamic_index_in_dim(side, ylo, 0, keepdims=False)
    picked = pick_columns(scalars(core), orbitals)
    own = half_panel[:main_pairs].reshape(COLS * YLO, depth, rows, block)
    own, got, keep, picked = together((own, got, keep, picked))

    with jax.named_scope("panels_in"):
        own = lax.all_to_all(own, PLANE, 0, 0, tiled=True)
        own = own.reshape(COLS, YLO, depth, rows, block)
    with jax.named_scope("side_in"):
        parts = rotate(join_and_spread(scalars(z, ylo), keep, got), "z")
        side_own = collect(scalars(z), parts)
    own, side_own, picked = together((own, side_own, picked))

    with jax.named_scope("mirror"):
        own_low = lax.all_to_all(own, "z", 0, 0, tiled=True)
    other = swap(own, "core")
    with jax.named_scope("side_mirror"):
        side_other = swap(side_own, "core")
        parts = rotate(spread(scalars(c), side_own), SIDE)
        side_low = collect(scalars(c), parts)
        side_other_low = swap(side_low, "core")
        side_partial = first_half(
            scalars(c, core), deep(side_low), deep(side_other_low), deep(side_own), deep(side_other),
            picked, "first_half_side"
        )
    own_low, other, side_partial = together((own_low, other, side_partial))

    other_low = swap(own_low, "core")
    partial_value = first_half(scalars(z, core), own, other, own_low, other_low, picked, "first_half")
    with jax.named_scope("partial"):
        partial_value = lax.all_to_all(partial_value, "z", 0, 0, tiled=True)
    with jax.named_scope("side_partial"):
        parts = rotate(spread(scalars(c), side_partial), SIDE)
        side_partial = collect(scalars(c), parts)
        side_partial_other = swap(side_partial, "core")
        keep, send = second_half_side(scalars(ylo, core), side_partial, side_partial_other, picked)
    partial_value, keep, send = together((partial_value, keep, send))

    got = swap(send, "ylo")
    result = second_half(partial_value, orbitals)
    result, got, keep = together((result, got, keep))

    with jax.named_scope("panels_out"):
        result = result.reshape(COLS * YLO, depth, rows, block)
        result = lax.all_to_all(result, PLANE, 0, 0, tiled=True)
        result = result.reshape(main_pairs, rows, block)
    with jax.named_scope("side_out"):
        parts = rotate(join_and_spread(scalars(z, ylo), keep, got), "z")
    return finish(scalars(z), parts, result)


def solution(mesh):
    fine = Mesh(mesh.devices.reshape(Z, YLO, CORE, X, YHI), ("z", "ylo", "core", "x", "yhi"))
    spec = P(None, ("z", "ylo", "core"), ("x", "yhi"))
    return jax.shard_map(
        per_device, mesh=fine, in_specs=(spec, P()), out_specs=spec, check_vma=False
    )
```

```python
import jax
import jax.numpy as jnp
from jax import lax
from jax.experimental import pallas as pl
from jax.experimental.pallas import tpu as pltpu
from jax.sharding import Mesh, PartitionSpec as P

Z, YLO, CORE, X, YHI = 8, 2, 2, 4, 2
COLS = X * YHI
BLOCKS = 8
RING = 4
PLANE = ("x", "yhi", "ylo")
F32 = jnp.float32
BF16 = jnp.bfloat16
AT_Z, AT_YLO, AT_CORE, AT_X, AT_YHI = range(5)
WIDE = pltpu.CompilerParams(vmem_limit_bytes=56 * 2**20)
NARROW = pltpu.CompilerParams(vmem_limit_bytes=60 * 2**20)
SMALL = pltpu.CompilerParams(vmem_limit_bytes=8 * 2**20)
SCALARS = pl.BlockSpec(memory_space=pltpu.SMEM)
VMEM = pl.BlockSpec(memory_space=pltpu.VMEM)


def array(*shape):
    return jax.ShapeDtypeStruct(shape, BF16)


def aligned(start, size):
    return pl.ds(pl.multiple_of(start, size), size)


def transposed(block):
    size = block.shape[1]
    row = lax.broadcasted_iota(jnp.int32, (size, size), 0)
    column = lax.broadcasted_iota(jnp.int32, (size, size), 1)
    eye = (row == column).astype(F32).astype(BF16)
    return lax.dot_general(
        eye, block, (((1,), (1,)), ((), ())), preferred_element_type=F32
    ).astype(BF16)


def pick_kernel(place, c_ref, out_ref):
    block = c_ref.shape[1] // BLOCKS
    lanes = block // CORE
    half = lanes // 2
    for core in range(CORE):
        @pl.when(place[AT_CORE] == core)
        def _():
            for b in range(BLOCKS):
                pieces = []
                for y in range(YLO):
                    tile = c_ref[:, b * block + y * lanes:b * block + (y + 1) * lanes]
                    pieces.append(tile[:, core * half:(core + 1) * half])
                out_ref[:, b * lanes:(b + 1) * lanes] = jnp.concatenate(pieces, axis=1)


def pick_columns(place, orbitals):
    size = orbitals.shape[0]
    block = size // BLOCKS
    return pl.pallas_call(
        pick_kernel,
        out_shape=array(size, size // CORE),
        grid_spec=pltpu.PrefetchScalarGridSpec(
            num_scalar_prefetch=1,
            grid=(BLOCKS,),
            in_specs=[pl.BlockSpec((block, size), lambda g, s: (g, 0))],
            out_specs=pl.BlockSpec((block, size // CORE), lambda g, s: (g, 0)),
        ),
        name="pick_columns",
    )(place, orbitals)


def accumulate(total, product):
    step = pl.program_id(0)

    @pl.when(step == 0)
    def _():
        total[...] = product

    @pl.when(step > 0)
    def _():
        total[...] += product


def build_symmetric(mine, core, direct, direct_other, turned, turned_other, sym, turn):
    per_step, _, depth, rows, block = direct.shape
    step = pl.program_id(0)
    for u in range(per_step):
        b = step * per_step + u
        cols = slice(u * block, (u + 1) * block)

        @pl.when(b >= mine)
        def _():
            for k in range(depth):
                for y in range(YLO):
                    at = k * block + y * CORE * rows
                    sym[aligned(at + core * rows, rows), cols] = direct[u, y, k]
                    sym[aligned(at + (1 - core) * rows, rows), cols] = direct_other[u, y, k]

        @pl.when(b == mine)
        def _():
            row = lax.broadcasted_iota(jnp.int32, (block, block), 0)
            column = lax.broadcasted_iota(jnp.int32, (block, block), 1)
            for k in range(depth):
                upper = sym[k * block:(k + 1) * block, cols]
                sym[k * block:(k + 1) * block, cols] = jnp.where(row <= column, upper, transposed(upper))

        @pl.when(b < mine)
        def _():
            for k in range(depth):
                for y in range(YLO):
                    at = k * block + y * CORE * rows
                    turn[aligned(at + core * rows, rows), :] = turned[u, y, k]
                    turn[aligned(at + (1 - core) * rows, rows), :] = turned_other[u, y, k]
            for k in range(depth):
                sym[k * block:(k + 1) * block, cols] = transposed(turn[k * block:(k + 1) * block])


def last_step():
    return pl.program_id(0) == pl.num_programs(0) - 1


def first_main_kernel(place, direct, direct_other, turned, turned_other, c_ref, t_ref, sym, turn, total):
    build_symmetric(place[AT_Z], place[AT_CORE], direct, direct_other, turned, turned_other, sym, turn)
    accumulate(total, jnp.dot(sym[...], c_ref[...], preferred_element_type=F32))

    @pl.when(last_step())
    def _():
        count, depth, block, lanes = t_ref.shape
        for part in range(count):
            for k in range(depth):
                t_ref[part, k] = total[k * block:(k + 1) * block, part * lanes:(part + 1) * lanes].astype(BF16)


def first_side_kernel(place, direct, direct_other, turned, turned_other, c_ref, keep, send, sym, turn, total):
    mine, yhi = place[AT_X] * YHI + place[AT_YHI], place[AT_YHI]
    build_symmetric(mine, place[AT_CORE], direct, direct_other, turned, turned_other, sym, turn)
    accumulate(total, jnp.dot(sym[...], c_ref[...], preferred_element_type=F32))

    @pl.when(last_step())
    def _():
        lanes = keep.shape[2]
        for x in range(X):
            keep[x] = total[:, aligned((x * YHI + yhi) * lanes, lanes)].astype(BF16)
            send[x] = total[:, aligned((x * YHI + 1 - yhi) * lanes, lanes)].astype(BF16)


def first_half(kernel, outs, place, direct, direct_other, turned, turned_other, picked, name):
    _, _, depth, rows, block = direct.shape
    size, width = picked.shape
    per_step = 2
    piece = pl.BlockSpec((per_step, YLO, depth, rows, block), lambda g, s: (g, 0, 0, 0, 0))
    return pl.pallas_call(
        kernel,
        out_shape=outs,
        grid_spec=pltpu.PrefetchScalarGridSpec(
            num_scalar_prefetch=1,
            grid=(BLOCKS // per_step,),
            in_specs=[piece, piece, piece, piece,
                      pl.BlockSpec((per_step * block, width), lambda g, s: (g, 0))],
            out_specs=[pl.BlockSpec(out.shape, lambda g, s, n=len(out.shape): (0,) * n) for out in outs],
            scratch_shapes=[pltpu.VMEM((depth * block, per_step * block), BF16),
                            pltpu.VMEM((depth * block, block), BF16),
                            pltpu.VMEM((depth * block, width), F32)],
        ),
        compiler_params=NARROW,
        name=name,
    )(place, direct, direct_other, turned, turned_other, picked)


def second_main_kernel(t_ref, c_ref, out_ref, left, total):
    per_step, depth, block, lanes = t_ref.shape
    rows = lanes // YLO
    for u in range(per_step):
        for k in range(depth):
            left[k * lanes:(k + 1) * lanes, u * block:(u + 1) * block] = transposed(t_ref[u, k])
    accumulate(total, jnp.dot(left[...], c_ref[...], preferred_element_type=F32))

    @pl.when(last_step())
    def _():
        for c in range(COLS):
            for y in range(YLO):
                for k in range(depth):
                    at = k * lanes + y * rows
                    out_ref[c, y, k] = total[at:at + rows, c * block:(c + 1) * block].astype(BF16)


def second_main(partial_value, orbitals):
    _, depth, block, lanes = partial_value.shape
    size = orbitals.shape[0]
    per_step = 2
    out = (COLS, YLO, depth, lanes // YLO, block)
    return pl.pallas_call(
        second_main_kernel,
        out_shape=array(*out),
        grid=(BLOCKS // per_step,),
        in_specs=[pl.BlockSpec((per_step, depth, block, lanes), lambda g: (g, 0, 0, 0)),
                  pl.BlockSpec((per_step * block, size), lambda g: (g, 0))],
        out_specs=pl.BlockSpec(out, lambda g: (0, 0, 0, 0, 0)),
        scratch_shapes=[pltpu.VMEM((depth * lanes, per_step * block), BF16),
                        pltpu.VMEM((depth * lanes, size), F32)],
        compiler_params=WIDE,
        name="second_main",
    )(partial_value, orbitals)


def second_side_kernel(place, t_ref, other_ref, c_ref, *rest):
    out_refs = rest[:RING]
    left, total, final = rest[RING:]
    per_step, block, lanes = t_ref.shape
    rows = lanes // YLO
    core = place[AT_CORE]
    for u in range(per_step):
        cols = slice(u * block, (u + 1) * block)
        own = transposed(t_ref[u])
        other = transposed(other_ref[u])
        for y in range(YLO):
            at = y * CORE * rows
            left[aligned(at + core * rows, rows), cols] = own[y * rows:(y + 1) * rows]
            left[aligned(at + (1 - core) * rows, rows), cols] = other[y * rows:(y + 1) * rows]
    accumulate(total, jnp.dot(left[...], c_ref[...], preferred_element_type=F32))

    @pl.when(last_step())
    def _():
        for part in range(total.shape[1] // block):
            cols = slice(part * block, (part + 1) * block)
            final[cols] = transposed(total[:, cols].astype(BF16))
        for a, b, out_ref in steps(out_refs):
            z_low, ylo = near(place, a, b)
            for z_high in range(RING):
                out_ref[z_high] = final[aligned(((z_high * 2 + z_low) * YLO + ylo) * rows, rows)]


def second_side(place, own, other, picked):
    _, block, lanes = own.shape
    size, width = picked.shape
    per_step = 2
    piece = pl.BlockSpec((per_step, block, lanes), lambda g, s: (g, 0, 0))
    out = array(RING, lanes // YLO, block)
    return pl.pallas_call(
        second_side_kernel,
        out_shape=[out] * RING,
        grid_spec=pltpu.PrefetchScalarGridSpec(
            num_scalar_prefetch=1,
            grid=(BLOCKS // per_step,),
            in_specs=[piece, piece, pl.BlockSpec((per_step * block, width), lambda g, s: (g, 0))],
            out_specs=[pl.BlockSpec(out.shape, lambda g, s: (0, 0, 0))] * RING,
            scratch_shapes=[pltpu.VMEM((block, per_step * block), BF16),
                            pltpu.VMEM((block, width), F32),
                            pltpu.VMEM((width, block), BF16)],
        ),
        compiler_params=NARROW,
        name="second_side",
    )(place, own, other, picked)


def steps(refs):
    return [(a, b, refs[2 * a + b]) for a in range(2) for b in range(2)]


def near(place, a, b):
    z_low, ylo = place[AT_Z] % 2, place[AT_YLO]
    return (1 - z_low if a else z_low), (1 - ylo if b else ylo)


def small_call(kernel, outs, name, place, *values):
    return pl.pallas_call(
        kernel,
        out_shape=outs,
        in_specs=[SCALARS] + [VMEM] * len(values),
        out_specs=jax.tree.map(lambda _: VMEM, outs),
        compiler_params=SMALL,
        name=name,
    )(place, *values)


def split_near_kernel(place, x_ref, *out_refs):
    for a, b, out_ref in steps(out_refs):
        z_low, ylo = near(place, a, b)
        for z_high in range(RING):
            out_ref[z_high] = x_ref[ylo * Z + z_high * 2 + z_low]


def split_near(place, half_panel, count):
    pairs, rows, block = half_panel.shape
    out = array(RING, rows, block)
    return pl.pallas_call(
        split_near_kernel,
        out_shape=[out] * RING,
        grid_spec=pltpu.PrefetchScalarGridSpec(
            num_scalar_prefetch=1,
            grid=(1,),
            in_specs=[pl.BlockSpec((count, rows, block), lambda g, s: (pairs // count - 1, 0, 0))],
            out_specs=[pl.BlockSpec(out.shape, lambda g, s: (0, 0, 0))] * RING,
        ),
        compiler_params=SMALL,
        name="split_near",
    )(place, half_panel)


def split_far_kernel(place, *refs):
    in_refs, out_refs = refs[:RING], refs[RING:]
    z_high = place[AT_Z] // 2
    for d in range(RING):
        for s in range(RING):
            out_refs[d][s] = in_refs[s][(z_high + d) % RING]


def collect_z_kernel(place, *refs):
    out_ref = refs[RING]
    z_high = place[AT_Z] // 2
    for d in range(RING):
        for a, b, s in steps(range(RING)):
            z_low, ylo = near(place, a, b)
            out_ref[(z_high + RING - d) % RING * 2 + z_low, ylo] = refs[d][s]


def finish_kernel(place, *refs):
    main_ref, out_ref = refs[RING:]
    main = main_ref.shape[0]
    z_high = place[AT_Z] // 2
    out_ref[:main] = main_ref[...]
    for d in range(RING):
        for a, b, s in steps(range(RING)):
            z_low, ylo = near(place, a, b)
            out_ref[main + ylo * Z + (z_high + RING - d) % RING * 2 + z_low] = refs[d][s]


def split_yhi_kernel(place, x_ref, keep, send):
    yhi = place[AT_YHI]
    for x in range(X):
        keep[x] = x_ref[x * YHI + yhi]
        send[x] = x_ref[x * YHI + 1 - yhi]


def split_x_kernel(place, keep, got, *out_refs):
    x, yhi = place[AT_X], place[AT_YHI]
    for d in range(RING):
        out_refs[d][yhi] = keep[(x + d) % X]
        out_refs[d][1 - yhi] = got[(x + d) % X]


def collect_x_kernel(place, *refs):
    out_ref = refs[RING]
    for d in range(RING):
        for y in range(YHI):
            out_ref[(place[AT_X] + RING - d) % X * YHI + y] = refs[d][y]


def swap(value, axis):
    return lax.ppermute(value, axis, [(0, 1), (1, 0)])


def near_exchange(parts):
    out = []
    for a, b, part in steps(parts):
        if a or b:
            pairs = [(z * YLO + y, (z ^ a) * YLO + (y ^ b)) for z in range(Z) for y in range(YLO)]
            part = lax.ppermute(part, ("z", "ylo"), pairs)
        out.append(part)
    return out


def far_exchange(place, parts):
    rows, block = parts[0].shape[1:]
    parts = small_call(split_far_kernel, [array(RING, rows, block)] * RING, "split_far", place, *parts)
    return [parts[0]] + [
        lax.ppermute(parts[d], "z", [(z, (z + 2 * d) % Z) for z in range(Z)]) for d in range(1, RING)
    ]


def x_exchange(place, keep, send):
    got = swap(send, "yhi")
    shape = keep.shape[1:]
    parts = small_call(split_x_kernel, [array(YHI, *shape)] * RING, "split_x", place, keep, got)
    parts = [parts[0]] + [
        lax.ppermute(parts[d], "x", [(x, (x + d) % X) for x in range(X)]) for d in range(1, RING)
    ]
    return small_call(collect_x_kernel, array(BLOCKS, *shape), "collect_x", place, *parts)


def per_device(half_panel, orbitals):
    pairs, rows, block = half_panel.shape
    side_pairs = Z * YLO
    main_pairs = pairs - side_pairs
    depth = main_pairs // (COLS * YLO)
    lanes = block // CORE
    place = jnp.stack([lax.axis_index(name) for name in ("z", "ylo", "core", "x", "yhi")]).astype(jnp.int32)

    def deep(value):
        return value.reshape(BLOCKS, YLO, 1, rows, block)

    together = lax.optimization_barrier

    with jax.named_scope("side_in"):
        near_parts = near_exchange(split_near(place, half_panel, side_pairs))
    picked = pick_columns(place, orbitals)
    own = half_panel[:main_pairs].reshape(COLS * YLO, depth, rows, block)
    own, near_parts, picked = together((own, near_parts, picked))

    with jax.named_scope("panels_in"):
        own = lax.all_to_all(own, PLANE, 0, 0, tiled=True)
        own = own.reshape(COLS, YLO, depth, rows, block)
    with jax.named_scope("side_in"):
        side_own = small_call(
            collect_z_kernel, array(Z, YLO, rows, block), "collect_z", place, *far_exchange(place, near_parts)
        )
    own, side_own, picked = together((own, side_own, picked))

    with jax.named_scope("mirror"):
        own_low = lax.all_to_all(own, "z", 0, 0, tiled=True)
    other = swap(own, "core")
    with jax.named_scope("side_mirror"):
        side_other = swap(side_own, "core")
        half = array(X, YLO, rows, block)
        keep, send = small_call(split_yhi_kernel, [half, half], "split_yhi", place, side_own)
        side_low = x_exchange(place, keep, send)
        side_other_low = swap(side_low, "core")
        half = array(X, block, lanes)
        keep, send = first_half(
            first_side_kernel, [half, half], place, deep(side_low), deep(side_other_low),
            deep(side_own), deep(side_other), picked, "first_side"
        )
    own_low, other, keep, send = together((own_low, other, keep, send))

    other_low = swap(own_low, "core")
    partial_value, = first_half(
        first_main_kernel, [array(Z, depth, block, lanes)], place, own, other, own_low, other_low,
        picked, "first_main"
    )
    with jax.named_scope("partial"):
        partial_value = lax.all_to_all(partial_value, "z", 0, 0, tiled=True)
    with jax.named_scope("side_partial"):
        side_partial = x_exchange(place, keep, send)
        near_parts = second_side(place, side_partial, swap(side_partial, "core"), picked)
    partial_value, near_parts = together((partial_value, near_parts))

    near_parts = near_exchange(near_parts)
    result = second_main(partial_value, orbitals)
    result, near_parts = together((result, near_parts))

    with jax.named_scope("panels_out"):
        result = result.reshape(COLS * YLO, depth, rows, block)
        result = lax.all_to_all(result, PLANE, 0, 0, tiled=True)
        result = result.reshape(main_pairs, rows, block)
    with jax.named_scope("side_out"):
        parts = far_exchange(place, near_parts)
    return small_call(finish_kernel, array(pairs, rows, block), "finish", place, *parts, result)


def solution(mesh):
    fine = Mesh(mesh.devices.reshape(Z, YLO, CORE, X, YHI), ("z", "ylo", "core", "x", "yhi"))
    spec = P(None, ("z", "ylo", "core"), ("x", "yhi"))
    return jax.shard_map(
        per_device, mesh=fine, in_specs=(spec, P()), out_specs=spec, check_vma=False
    )
```

```python
import functools

import jax
import jax.numpy as jnp
from jax import lax
from jax.experimental import pallas as pl
from jax.experimental.pallas import tpu as pltpu
from jax.sharding import Mesh, PartitionSpec as P

Z, YLO, CORE, X, YHI = 8, 2, 2, 4, 2
COLS = X * YHI
BLOCKS = 8
PLANE = ("x", "yhi", "ylo")
SIDE = ("x", "yhi")
AT_Z, AT_YLO, AT_CORE, AT_C = range(4)
F32 = jnp.float32
BF16 = jnp.bfloat16
PARAMS = pltpu.CompilerParams(vmem_limit_bytes=24 * 2**20)
SMALL = pltpu.CompilerParams(vmem_limit_bytes=8 * 2**20)


STEPS = 4
HBM = pl.BlockSpec(memory_space=pltpu.HBM)


def in_hbm(value):
    return pltpu.with_memory_space_constraint(value, pltpu.HBM)


def fetches(c_hbm, c_ref, sems):
    rows = c_ref.shape[1]
    copies = [
        pltpu.make_async_copy(c_hbm.at[pl.ds(g * rows, rows)], c_ref.at[g], sems.at[g])
        for g in range(STEPS)
    ]
    for copy in copies:
        copy.start()
    return copies


def fetch_scratch(value):
    size, width = value.shape
    return [pltpu.VMEM((STEPS, size // STEPS, width), BF16), pltpu.SemaphoreType.DMA((STEPS,))]


def transposed(block):
    size = block.shape[1]
    row = lax.broadcasted_iota(jnp.int32, (size, size), 0)
    column = lax.broadcasted_iota(jnp.int32, (size, size), 1)
    eye = (row == column).astype(F32).astype(BF16)
    return lax.dot_general(
        eye, block, (((1,), (1,)), ((), ())), preferred_element_type=F32
    ).astype(BF16)


def pick_kernel(place, c_hbm, out_hbm, c_ref, sems, chosen, out_sems):
    size = c_hbm.shape[0]
    block = size // BLOCKS
    lanes = block // CORE
    half = lanes // 2
    rows = size // STEPS
    copies = fetches(c_hbm, c_ref, sems)
    stores = []
    for g in range(STEPS):
        copies[g].wait()
        for core in range(CORE):
            @pl.when(place[AT_CORE] == core)
            def _():
                for b in range(BLOCKS):
                    pieces = []
                    for y in range(YLO):
                        tile = c_ref[g, :, b * block + y * lanes:b * block + (y + 1) * lanes]
                        pieces.append(tile[:, core * half:(core + 1) * half])
                    chosen[g, :, b * lanes:(b + 1) * lanes] = jnp.concatenate(pieces, axis=1)
        stores.append(pltpu.make_async_copy(chosen.at[g], out_hbm.at[pl.ds(g * rows, rows)], out_sems.at[g]))
        stores[g].start()
    for store in stores:
        store.wait()


def pick_columns(place, orbitals):
    size = orbitals.shape[0]
    width = size // CORE
    return pl.pallas_call(
        pick_kernel,
        out_shape=jax.ShapeDtypeStruct((size, width), BF16),
        in_specs=[pl.BlockSpec(memory_space=pltpu.SMEM), HBM],
        out_specs=HBM,
        scratch_shapes=fetch_scratch(orbitals) + [
            pltpu.VMEM((STEPS, size // STEPS, width), BF16), pltpu.SemaphoreType.DMA((STEPS,))],
        compiler_params=PARAMS,
        name="pick_columns",
    )(place, in_hbm(orbitals))


def accumulate(total, product, step):
    if step == 0:
        total[...] = product
    else:
        total[...] += product


def first_kernel(index, place, direct, direct_other, turned, turned_other, c_hbm, t_ref,
                 c_ref, sems, sym, turn, total):
    _, _, depth, rows, block = direct.shape
    mine, core = place[index], place[AT_CORE]
    per_step = BLOCKS // STEPS
    copies = fetches(c_hbm, c_ref, sems)
    for step in range(STEPS):
        for u in range(per_step):
            b = step * per_step + u
            cols = slice(u * block, (u + 1) * block)

            @pl.when(b >= mine)
            def _():
                for k in range(depth):
                    for y in range(YLO):
                        at = k * block + y * CORE * rows
                        sym[pl.ds(pl.multiple_of(at + core * rows, rows), rows), cols] = direct[b, y, k]
                        sym[pl.ds(pl.multiple_of(at + (1 - core) * rows, rows), rows), cols] = direct_other[b, y, k]

            @pl.when(b == mine)
            def _():
                row = lax.broadcasted_iota(jnp.int32, (block, block), 0)
                column = lax.broadcasted_iota(jnp.int32, (block, block), 1)
                for k in range(depth):
                    upper = sym[k * block:(k + 1) * block, cols]
                    sym[k * block:(k + 1) * block, cols] = jnp.where(row <= column, upper, transposed(upper))

            @pl.when(b < mine)
            def _():
                for k in range(depth):
                    for y in range(YLO):
                        at = k * block + y * CORE * rows
                        turn[pl.ds(pl.multiple_of(at + core * rows, rows), rows), :] = turned[b, y, k]
                        turn[pl.ds(pl.multiple_of(at + (1 - core) * rows, rows), rows), :] = turned_other[b, y, k]
                for k in range(depth):
                    sym[k * block:(k + 1) * block, cols] = transposed(turn[k * block:(k + 1) * block])

        copies[step].wait()
        accumulate(total, jnp.dot(sym[...], c_ref[step], preferred_element_type=F32), step)
    lanes = t_ref.shape[3]
    for part in range(t_ref.shape[0]):
        for k in range(depth):
            t_ref[part, k] = total[k * block:(k + 1) * block, part * lanes:(part + 1) * lanes].astype(BF16)


def first_half(index, place, direct, direct_other, turned, turned_other, picked, name):
    _, _, depth, rows, block = direct.shape
    size, width = picked.shape
    vmem = pl.BlockSpec(memory_space=pltpu.VMEM)
    return pl.pallas_call(
        functools.partial(first_kernel, index),
        out_shape=jax.ShapeDtypeStruct((BLOCKS, depth, block, width // BLOCKS), BF16),
        in_specs=[pl.BlockSpec(memory_space=pltpu.SMEM), vmem, vmem, vmem, vmem, HBM],
        out_specs=vmem,
        scratch_shapes=fetch_scratch(picked) + [
            pltpu.VMEM((depth * block, size // STEPS), BF16),
            pltpu.VMEM((depth * block, block), BF16),
            pltpu.VMEM((depth * block, width), F32)],
        compiler_params=PARAMS,
        name=name,
    )(place, direct, direct_other, turned, turned_other, in_hbm(picked))


def second_kernel(t_ref, c_hbm, out_ref, c_ref, sems, left, total):
    count, depth, block, lanes = t_ref.shape
    rows = lanes // YLO
    per_step = count // STEPS
    copies = fetches(c_hbm, c_ref, sems)
    for step in range(STEPS):
        for u in range(per_step):
            for k in range(depth):
                left[k * lanes:(k + 1) * lanes, u * block:(u + 1) * block] = transposed(t_ref[step * per_step + u, k])
        copies[step].wait()
        accumulate(total, jnp.dot(left[...], c_ref[step], preferred_element_type=F32), step)
    for c in range(COLS):
        for y in range(YLO):
            for k in range(depth):
                at = k * lanes + y * rows
                out_ref[c, y, k] = total[at:at + rows, c * block:(c + 1) * block].astype(BF16)


def second_half(partial_value, orbitals):
    _, depth, block, lanes = partial_value.shape
    size = orbitals.shape[0]
    vmem = pl.BlockSpec(memory_space=pltpu.VMEM)
    return pl.pallas_call(
        second_kernel,
        out_shape=jax.ShapeDtypeStruct((COLS, YLO, depth, lanes // YLO, block), BF16),
        in_specs=[vmem, HBM],
        out_specs=vmem,
        scratch_shapes=fetch_scratch(orbitals) + [
            pltpu.VMEM((depth * lanes, size // STEPS), BF16),
            pltpu.VMEM((depth * lanes, size), F32)],
        compiler_params=PARAMS,
        name="second_half",
    )(partial_value, in_hbm(orbitals))


def second_side_kernel(place, t_ref, other_ref, c_hbm, keep, send, c_ref, sems, left, total, final):
    count, _, block, lanes = t_ref.shape
    rows = lanes // YLO
    per_step = count // STEPS
    ylo, core = place[AT_YLO], place[AT_CORE]
    copies = fetches(c_hbm, c_ref, sems)
    for step in range(STEPS):
        for u in range(per_step):
            cols = slice(u * block, (u + 1) * block)
            own = transposed(t_ref[step * per_step + u, 0])
            other = transposed(other_ref[step * per_step + u, 0])
            for y in range(YLO):
                at = y * CORE * rows
                left[pl.ds(pl.multiple_of(at + core * rows, rows), rows), cols] = own[y * rows:(y + 1) * rows]
                left[pl.ds(pl.multiple_of(at + (1 - core) * rows, rows), rows), cols] = other[y * rows:(y + 1) * rows]
        copies[step].wait()
        accumulate(total, jnp.dot(left[...], c_ref[step], preferred_element_type=F32), step)
    for part in range(total.shape[1] // block):
        cols = slice(part * block, (part + 1) * block)
        final[cols] = transposed(total[:, cols].astype(BF16))
    for z in range(Z):
        at = z * YLO * rows
        keep[z] = final[pl.ds(pl.multiple_of(at + ylo * rows, rows), rows)]
        send[z] = final[pl.ds(pl.multiple_of(at + (1 - ylo) * rows, rows), rows)]


def second_half_side(place, own, other, picked):
    _, _, block, lanes = own.shape
    size, width = picked.shape
    vmem = pl.BlockSpec(memory_space=pltpu.VMEM)
    out = jax.ShapeDtypeStruct((Z, lanes // YLO, block), BF16)
    return pl.pallas_call(
        second_side_kernel,
        out_shape=[out, out],
        in_specs=[pl.BlockSpec(memory_space=pltpu.SMEM), vmem, vmem, HBM],
        out_specs=[vmem, vmem],
        scratch_shapes=fetch_scratch(picked) + [
            pltpu.VMEM((block, size // STEPS), BF16),
            pltpu.VMEM((block, width), F32),
            pltpu.VMEM((width, block), BF16)],
        compiler_params=PARAMS,
        name="second_half_side",
    )(place, own, other, in_hbm(picked))


def spread_kernel(index, place, x_ref, *out_refs):
    for d in range(BLOCKS):
        out_refs[d][...] = x_ref[(place[index] + d) % BLOCKS]


def spread(index, place, value):
    vmem = pl.BlockSpec(memory_space=pltpu.VMEM)
    return pl.pallas_call(
        functools.partial(spread_kernel, index),
        out_shape=[jax.ShapeDtypeStruct(value.shape[1:], BF16)] * BLOCKS,
        in_specs=[pl.BlockSpec(memory_space=pltpu.SMEM), vmem],
        out_specs=[vmem] * BLOCKS,
        compiler_params=SMALL,
        name="spread",
    )(place, value)


def join_kernel(place, keep, got, *out_refs):
    z, ylo = place[AT_Z], place[AT_YLO]
    for d in range(BLOCKS):
        out_refs[d][ylo] = keep[(z + d) % BLOCKS]
        out_refs[d][1 - ylo] = got[(z + d) % BLOCKS]


def join_and_spread(place, keep, got):
    vmem = pl.BlockSpec(memory_space=pltpu.VMEM)
    return pl.pallas_call(
        join_kernel,
        out_shape=[jax.ShapeDtypeStruct((YLO,) + keep.shape[1:], BF16)] * BLOCKS,
        in_specs=[pl.BlockSpec(memory_space=pltpu.SMEM), vmem, vmem],
        out_specs=[vmem] * BLOCKS,
        compiler_params=SMALL,
        name="join_and_spread",
    )(place, keep, got)


def collect_kernel(index, place, *refs):
    out_ref = refs[BLOCKS]
    for d in range(BLOCKS):
        out_ref[(place[index] + BLOCKS - d) % BLOCKS] = refs[d][...]


def collect(index, place, parts):
    vmem = pl.BlockSpec(memory_space=pltpu.VMEM)
    return pl.pallas_call(
        functools.partial(collect_kernel, index),
        out_shape=jax.ShapeDtypeStruct((BLOCKS,) + parts[0].shape, BF16),
        in_specs=[pl.BlockSpec(memory_space=pltpu.SMEM)] + [vmem] * BLOCKS,
        out_specs=vmem,
        compiler_params=SMALL,
        name="collect",
    )(place, *parts)


def finish_kernel(place, *refs):
    main_ref, out_ref = refs[BLOCKS:]
    main = main_ref.shape[0]
    out_ref[:main] = main_ref[...]
    for d in range(BLOCKS):
        for y in range(YLO):
            out_ref[main + y * BLOCKS + (place[AT_Z] + BLOCKS - d) % BLOCKS] = refs[d][y]


def finish(place, parts, main):
    pairs, rows, block = main.shape
    vmem = pl.BlockSpec(memory_space=pltpu.VMEM)
    return pl.pallas_call(
        finish_kernel,
        out_shape=jax.ShapeDtypeStruct((pairs + YLO * BLOCKS, rows, block), BF16),
        in_specs=[pl.BlockSpec(memory_space=pltpu.SMEM)] + [vmem] * (BLOCKS + 1),
        out_specs=vmem,
        compiler_params=SMALL,
        name="finish",
    )(place, *parts, main)


def rotate(parts, axes):
    out = [parts[0]]
    for d in range(1, BLOCKS):
        out.append(lax.ppermute(parts[d], axes, [(i, (i + d) % BLOCKS) for i in range(BLOCKS)]))
    return out


def swap(value, axis):
    return lax.ppermute(value, axis, [(0, 1), (1, 0)])


def per_device(half_panel, orbitals):
    pairs, rows, block = half_panel.shape
    side_pairs = Z * YLO
    main_pairs = pairs - side_pairs
    depth = main_pairs // (COLS * YLO)
    z, ylo, core = lax.axis_index("z"), lax.axis_index("ylo"), lax.axis_index("core")
    c = lax.axis_index("x") * YHI + lax.axis_index("yhi")

    place = jnp.stack([z, ylo, core, c]).astype(jnp.int32)

    def deep(value):
        return value.reshape(BLOCKS, YLO, 1, rows, block)

    together = lax.optimization_barrier

    with jax.named_scope("side_in"):
        side = half_panel[main_pairs:].reshape(YLO, Z, rows, block)
        got = swap(lax.dynamic_index_in_dim(side, 1 - ylo, 0, keepdims=False), "ylo")
        keep = lax.dynamic_index_in_dim(side, ylo, 0, keepdims=False)
    picked = pick_columns(place, orbitals)
    own = half_panel[:main_pairs].reshape(COLS * YLO, depth, rows, block)
    own, got, keep, picked = together((own, got, keep, picked))

    with jax.named_scope("panels_in"):
        own = lax.all_to_all(own, PLANE, 0, 0, tiled=True)
        own = own.reshape(COLS, YLO, depth, rows, block)
    with jax.named_scope("side_in"):
        parts = rotate(join_and_spread(place, keep, got), "z")
        side_own = collect(AT_Z, place, parts)
    own, side_own, picked = together((own, side_own, picked))

    with jax.named_scope("mirror"):
        own_low = lax.all_to_all(own, "z", 0, 0, tiled=True)
    other = swap(own, "core")
    with jax.named_scope("side_mirror"):
        side_other = swap(side_own, "core")
        parts = rotate(spread(AT_C, place, side_own), SIDE)
        side_low = collect(AT_C, place, parts)
        side_other_low = swap(side_low, "core")
        side_partial = first_half(
            AT_C, place, deep(side_low), deep(side_other_low), deep(side_own), deep(side_other),
            picked, "first_half_side"
        )
    own_low, other, side_partial = together((own_low, other, side_partial))

    other_low = swap(own_low, "core")
    partial_value = first_half(AT_Z, place, own, other, own_low, other_low, picked, "first_half")
    with jax.named_scope("partial"):
        partial_value = lax.all_to_all(partial_value, "z", 0, 0, tiled=True)
    with jax.named_scope("side_partial"):
        parts = rotate(spread(AT_C, place, side_partial), SIDE)
        side_partial = collect(AT_C, place, parts)
        side_partial_other = swap(side_partial, "core")
        keep, send = second_half_side(place, side_partial, side_partial_other, picked)
    partial_value, keep, send = together((partial_value, keep, send))

    got = swap(send, "ylo")
    result = second_half(partial_value, orbitals)
    result, got, keep = together((result, got, keep))

    with jax.named_scope("panels_out"):
        result = result.reshape(COLS * YLO, depth, rows, block)
        result = lax.all_to_all(result, PLANE, 0, 0, tiled=True)
        result = result.reshape(main_pairs, rows, block)
    with jax.named_scope("side_out"):
        parts = rotate(join_and_spread(place, keep, got), "z")
    return finish(place, parts, result)


def solution(mesh):
    fine = Mesh(mesh.devices.reshape(Z, YLO, CORE, X, YHI), ("z", "ylo", "core", "x", "yhi"))
    spec = P(None, ("z", "ylo", "core"), ("x", "yhi"))
    return jax.shard_map(
        per_device, mesh=fine, in_specs=(spec, P()), out_specs=spec, check_vma=False
    )
```

```python
import functools

import jax
import jax.numpy as jnp
from jax import lax
from jax.experimental import pallas as pl
from jax.experimental.pallas import tpu as pltpu
from jax.sharding import Mesh, PartitionSpec as P

Z, YLO, CORE, X, YHI = 8, 2, 2, 4, 2
COLS = X * YHI
BLOCKS = 8
PLANE = ("x", "yhi", "ylo")
SIDE = ("x", "yhi")
AT_Z, AT_YLO, AT_CORE, AT_C = range(4)
F32 = jnp.float32
BF16 = jnp.bfloat16
PARAMS = pltpu.CompilerParams(vmem_limit_bytes=24 * 2**20)
SMALL = pltpu.CompilerParams(vmem_limit_bytes=8 * 2**20)


STEPS = 4
HBM = pl.BlockSpec(memory_space=pltpu.HBM)


def in_hbm(value):
    return pltpu.with_memory_space_constraint(value, pltpu.HBM)


def fetch_of(c_hbm, c_ref, sems, step):
    rows = c_ref.shape[1]
    return pltpu.make_async_copy(
        c_hbm.at[pl.ds(pl.multiple_of(step * rows, rows), rows)], c_ref.at[step], sems.at[step]
    )


def steps(c_hbm, c_ref, sems, body):
    def start(step, carry):
        fetch_of(c_hbm, c_ref, sems, step).start()
        return carry

    def run(step, carry):
        body(step)
        return carry

    lax.fori_loop(0, STEPS, start, 0)
    lax.fori_loop(0, STEPS, run, 0)


def fetch_scratch(value):
    size, width = value.shape
    return [pltpu.VMEM((STEPS, size // STEPS, width), BF16), pltpu.SemaphoreType.DMA((STEPS,))]


def transposed(block):
    size = block.shape[1]
    row = lax.broadcasted_iota(jnp.int32, (size, size), 0)
    column = lax.broadcasted_iota(jnp.int32, (size, size), 1)
    eye = (row == column).astype(F32).astype(BF16)
    return lax.dot_general(
        eye, block, (((1,), (1,)), ((), ())), preferred_element_type=F32
    ).astype(BF16)


def pick_kernel(place, c_hbm, out_hbm, c_ref, sems, chosen, out_sems):
    block = c_hbm.shape[1] // BLOCKS
    lanes = block // CORE
    half = lanes // 2
    rows = c_hbm.shape[0] // STEPS

    def store_of(step):
        return pltpu.make_async_copy(
            chosen.at[step], out_hbm.at[pl.ds(pl.multiple_of(step * rows, rows), rows)], out_sems.at[step]
        )

    def choose(step):
        fetch_of(c_hbm, c_ref, sems, step).wait()
        for core in range(CORE):
            @pl.when(place[AT_CORE] == core)
            def _():
                for b in range(BLOCKS):
                    pieces = []
                    for y in range(YLO):
                        tile = c_ref[step, :, b * block + y * lanes:b * block + (y + 1) * lanes]
                        pieces.append(tile[:, core * half:(core + 1) * half])
                    chosen[step, :, b * lanes:(b + 1) * lanes] = jnp.concatenate(pieces, axis=1)
        store_of(step).start()

    def finish_store(step, carry):
        store_of(step).wait()
        return carry

    steps(c_hbm, c_ref, sems, choose)
    lax.fori_loop(0, STEPS, finish_store, 0)


def pick_columns(place, orbitals):
    size = orbitals.shape[0]
    width = size // CORE
    return pl.pallas_call(
        pick_kernel,
        out_shape=pltpu.HBM((size, width), BF16),
        in_specs=[pl.BlockSpec(memory_space=pltpu.SMEM), HBM],
        out_specs=HBM,
        scratch_shapes=fetch_scratch(orbitals) + [
            pltpu.VMEM((STEPS, size // STEPS, width), BF16), pltpu.SemaphoreType.DMA((STEPS,))],
        compiler_params=PARAMS,
        name="pick_columns",
    )(place, in_hbm(orbitals))


def first_kernel(index, place, direct, direct_other, turned, turned_other, c_hbm, t_ref,
                 c_ref, sems, sym, turn, total):
    _, _, depth, rows, block = direct.shape
    mine, core = place[index], place[AT_CORE]
    per_step = BLOCKS // STEPS
    total[...] = jnp.zeros(total.shape, F32)

    def work(step):
        for u in range(per_step):
            b = step * per_step + u
            cols = slice(u * block, (u + 1) * block)

            @pl.when(b >= mine)
            def _():
                for k in range(depth):
                    for y in range(YLO):
                        at = k * block + y * CORE * rows
                        sym[pl.ds(pl.multiple_of(at + core * rows, rows), rows), cols] = direct[b, y, k]
                        sym[pl.ds(pl.multiple_of(at + (1 - core) * rows, rows), rows), cols] = direct_other[b, y, k]

            @pl.when(b == mine)
            def _():
                row = lax.broadcasted_iota(jnp.int32, (block, block), 0)
                column = lax.broadcasted_iota(jnp.int32, (block, block), 1)
                for k in range(depth):
                    upper = sym[k * block:(k + 1) * block, cols]
                    sym[k * block:(k + 1) * block, cols] = jnp.where(row <= column, upper, transposed(upper))

            @pl.when(b < mine)
            def _():
                for k in range(depth):
                    for y in range(YLO):
                        at = k * block + y * CORE * rows
                        turn[pl.ds(pl.multiple_of(at + core * rows, rows), rows), :] = turned[b, y, k]
                        turn[pl.ds(pl.multiple_of(at + (1 - core) * rows, rows), rows), :] = turned_other[b, y, k]
                for k in range(depth):
                    sym[k * block:(k + 1) * block, cols] = transposed(turn[k * block:(k + 1) * block])

        fetch_of(c_hbm, c_ref, sems, step).wait()
        total[...] += jnp.dot(sym[...], c_ref[step], preferred_element_type=F32)

    steps(c_hbm, c_ref, sems, work)
    lanes = t_ref.shape[3]
    for part in range(t_ref.shape[0]):
        for k in range(depth):
            t_ref[part, k] = total[k * block:(k + 1) * block, part * lanes:(part + 1) * lanes].astype(BF16)


def first_half(index, place, direct, direct_other, turned, turned_other, picked, name):
    _, _, depth, rows, block = direct.shape
    size, width = picked.shape
    vmem = pl.BlockSpec(memory_space=pltpu.VMEM)
    return pl.pallas_call(
        functools.partial(first_kernel, index),
        out_shape=jax.ShapeDtypeStruct((BLOCKS, depth, block, width // BLOCKS), BF16),
        in_specs=[pl.BlockSpec(memory_space=pltpu.SMEM), vmem, vmem, vmem, vmem, HBM],
        out_specs=vmem,
        scratch_shapes=fetch_scratch(picked) + [
            pltpu.VMEM((depth * block, size // STEPS), BF16),
            pltpu.VMEM((depth * block, block), BF16),
            pltpu.VMEM((depth * block, width), F32)],
        compiler_params=PARAMS,
        name=name,
    )(place, direct, direct_other, turned, turned_other, in_hbm(picked))


def second_kernel(t_ref, c_hbm, out_ref, c_ref, sems, left, total):
    count, depth, block, lanes = t_ref.shape
    rows = lanes // YLO
    per_step = count // STEPS
    total[...] = jnp.zeros(total.shape, F32)

    def work(step):
        for u in range(per_step):
            for k in range(depth):
                left[k * lanes:(k + 1) * lanes, u * block:(u + 1) * block] = transposed(t_ref[step * per_step + u, k])
        fetch_of(c_hbm, c_ref, sems, step).wait()
        total[...] += jnp.dot(left[...], c_ref[step], preferred_element_type=F32)

    steps(c_hbm, c_ref, sems, work)
    for c in range(COLS):
        for y in range(YLO):
            for k in range(depth):
                at = k * lanes + y * rows
                out_ref[c, y, k] = total[at:at + rows, c * block:(c + 1) * block].astype(BF16)


def second_half(partial_value, orbitals):
    _, depth, block, lanes = partial_value.shape
    size = orbitals.shape[0]
    vmem = pl.BlockSpec(memory_space=pltpu.VMEM)
    return pl.pallas_call(
        second_kernel,
        out_shape=jax.ShapeDtypeStruct((COLS, YLO, depth, lanes // YLO, block), BF16),
        in_specs=[vmem, HBM],
        out_specs=vmem,
        scratch_shapes=fetch_scratch(orbitals) + [
            pltpu.VMEM((depth * lanes, size // STEPS), BF16),
            pltpu.VMEM((depth * lanes, size), F32)],
        compiler_params=PARAMS,
        name="second_half",
    )(partial_value, in_hbm(orbitals))


def second_side_kernel(place, t_ref, other_ref, c_hbm, keep, send, c_ref, sems, left, total, final):
    count, _, block, lanes = t_ref.shape
    rows = lanes // YLO
    per_step = count // STEPS
    ylo, core = place[AT_YLO], place[AT_CORE]
    total[...] = jnp.zeros(total.shape, F32)

    def work(step):
        for u in range(per_step):
            cols = slice(u * block, (u + 1) * block)
            own = transposed(t_ref[step * per_step + u, 0])
            other = transposed(other_ref[step * per_step + u, 0])
            for y in range(YLO):
                at = y * CORE * rows
                left[pl.ds(pl.multiple_of(at + core * rows, rows), rows), cols] = own[y * rows:(y + 1) * rows]
                left[pl.ds(pl.multiple_of(at + (1 - core) * rows, rows), rows), cols] = other[y * rows:(y + 1) * rows]
        fetch_of(c_hbm, c_ref, sems, step).wait()
        total[...] += jnp.dot(left[...], c_ref[step], preferred_element_type=F32)

    steps(c_hbm, c_ref, sems, work)
    for part in range(total.shape[1] // block):
        cols = slice(part * block, (part + 1) * block)
        final[cols] = transposed(total[:, cols].astype(BF16))
    for z in range(Z):
        at = z * YLO * rows
        keep[z] = final[pl.ds(pl.multiple_of(at + ylo * rows, rows), rows)]
        send[z] = final[pl.ds(pl.multiple_of(at + (1 - ylo) * rows, rows), rows)]


def second_half_side(place, own, other, picked):
    _, _, block, lanes = own.shape
    size, width = picked.shape
    vmem = pl.BlockSpec(memory_space=pltpu.VMEM)
    out = jax.ShapeDtypeStruct((Z, lanes // YLO, block), BF16)
    return pl.pallas_call(
        second_side_kernel,
        out_shape=[out, out],
        in_specs=[pl.BlockSpec(memory_space=pltpu.SMEM), vmem, vmem, HBM],
        out_specs=[vmem, vmem],
        scratch_shapes=fetch_scratch(picked) + [
            pltpu.VMEM((block, size // STEPS), BF16),
            pltpu.VMEM((block, width), F32),
            pltpu.VMEM((width, block), BF16)],
        compiler_params=PARAMS,
        name="second_half_side",
    )(place, own, other, in_hbm(picked))


def spread_kernel(index, place, x_ref, *out_refs):
    for d in range(BLOCKS):
        out_refs[d][...] = x_ref[(place[index] + d) % BLOCKS]


def spread(index, place, value):
    vmem = pl.BlockSpec(memory_space=pltpu.VMEM)
    return pl.pallas_call(
        functools.partial(spread_kernel, index),
        out_shape=[jax.ShapeDtypeStruct(value.shape[1:], BF16)] * BLOCKS,
        in_specs=[pl.BlockSpec(memory_space=pltpu.SMEM), vmem],
        out_specs=[vmem] * BLOCKS,
        compiler_params=SMALL,
        name="spread",
    )(place, value)


def join_kernel(place, keep, got, *out_refs):
    z, ylo = place[AT_Z], place[AT_YLO]
    for d in range(BLOCKS):
        out_refs[d][ylo] = keep[(z + d) % BLOCKS]
        out_refs[d][1 - ylo] = got[(z + d) % BLOCKS]


def join_and_spread(place, keep, got):
    vmem = pl.BlockSpec(memory_space=pltpu.VMEM)
    return pl.pallas_call(
        join_kernel,
        out_shape=[jax.ShapeDtypeStruct((YLO,) + keep.shape[1:], BF16)] * BLOCKS,
        in_specs=[pl.BlockSpec(memory_space=pltpu.SMEM), vmem, vmem],
        out_specs=[vmem] * BLOCKS,
        compiler_params=SMALL,
        name="join_and_spread",
    )(place, keep, got)


def collect_kernel(index, place, *refs):
    out_ref = refs[BLOCKS]
    for d in range(BLOCKS):
        out_ref[(place[index] + BLOCKS - d) % BLOCKS] = refs[d][...]


def collect(index, place, parts):
    vmem = pl.BlockSpec(memory_space=pltpu.VMEM)
    return pl.pallas_call(
        functools.partial(collect_kernel, index),
        out_shape=jax.ShapeDtypeStruct((BLOCKS,) + parts[0].shape, BF16),
        in_specs=[pl.BlockSpec(memory_space=pltpu.SMEM)] + [vmem] * BLOCKS,
        out_specs=vmem,
        compiler_params=SMALL,
        name="collect",
    )(place, *parts)


def finish_kernel(place, *refs):
    main_ref, out_ref = refs[BLOCKS:]
    main = main_ref.shape[0]
    out_ref[:main] = main_ref[...]
    for d in range(BLOCKS):
        for y in range(YLO):
            out_ref[main + y * BLOCKS + (place[AT_Z] + BLOCKS - d) % BLOCKS] = refs[d][y]


def finish(place, parts, main):
    pairs, rows, block = main.shape
    vmem = pl.BlockSpec(memory_space=pltpu.VMEM)
    return pl.pallas_call(
        finish_kernel,
        out_shape=jax.ShapeDtypeStruct((pairs + YLO * BLOCKS, rows, block), BF16),
        in_specs=[pl.BlockSpec(memory_space=pltpu.SMEM)] + [vmem] * (BLOCKS + 1),
        out_specs=vmem,
        compiler_params=SMALL,
        name="finish",
    )(place, *parts, main)


def rotate(parts, axes):
    out = [parts[0]]
    for d in range(1, BLOCKS):
        out.append(lax.ppermute(parts[d], axes, [(i, (i + d) % BLOCKS) for i in range(BLOCKS)]))
    return out


def swap(value, axis):
    return lax.ppermute(value, axis, [(0, 1), (1, 0)])


def per_device(half_panel, orbitals):
    pairs, rows, block = half_panel.shape
    side_pairs = Z * YLO
    main_pairs = pairs - side_pairs
    depth = main_pairs // (COLS * YLO)
    z, ylo, core = lax.axis_index("z"), lax.axis_index("ylo"), lax.axis_index("core")
    c = lax.axis_index("x") * YHI + lax.axis_index("yhi")

    place = jnp.stack([z, ylo, core, c]).astype(jnp.int32)

    def deep(value):
        return value.reshape(BLOCKS, YLO, 1, rows, block)

    together = lax.optimization_barrier

    with jax.named_scope("side_in"):
        side = half_panel[main_pairs:].reshape(YLO, Z, rows, block)
        got = swap(lax.dynamic_index_in_dim(side, 1 - ylo, 0, keepdims=False), "ylo")
        keep = lax.dynamic_index_in_dim(side, ylo, 0, keepdims=False)
    picked = pick_columns(place, orbitals)
    own = half_panel[:main_pairs].reshape(COLS * YLO, depth, rows, block)
    own, got, keep, picked = together((own, got, keep, picked))

    with jax.named_scope("panels_in"):
        own = lax.all_to_all(own, PLANE, 0, 0, tiled=True)
        own = own.reshape(COLS, YLO, depth, rows, block)
    with jax.named_scope("side_in"):
        parts = rotate(join_and_spread(place, keep, got), "z")
        side_own = collect(AT_Z, place, parts)
    own, side_own, picked = together((own, side_own, picked))

    with jax.named_scope("mirror"):
        own_low = lax.all_to_all(own, "z", 0, 0, tiled=True)
    other = swap(own, "core")
    with jax.named_scope("side_mirror"):
        side_other = swap(side_own, "core")
        parts = rotate(spread(AT_C, place, side_own), SIDE)
        side_low = collect(AT_C, place, parts)
        side_other_low = swap(side_low, "core")
        side_partial = first_half(
            AT_C, place, deep(side_low), deep(side_other_low), deep(side_own), deep(side_other),
            picked, "first_half_side"
        )
    own_low, other, side_partial = together((own_low, other, side_partial))

    other_low = swap(own_low, "core")
    partial_value = first_half(AT_Z, place, own, other, own_low, other_low, picked, "first_half")
    with jax.named_scope("partial"):
        partial_value = lax.all_to_all(partial_value, "z", 0, 0, tiled=True)
    with jax.named_scope("side_partial"):
        parts = rotate(spread(AT_C, place, side_partial), SIDE)
        side_partial = collect(AT_C, place, parts)
        side_partial_other = swap(side_partial, "core")
        keep, send = second_half_side(place, side_partial, side_partial_other, picked)
    partial_value, keep, send = together((partial_value, keep, send))

    got = swap(send, "ylo")
    result = second_half(partial_value, orbitals)
    result, got, keep = together((result, got, keep))

    with jax.named_scope("panels_out"):
        result = result.reshape(COLS * YLO, depth, rows, block)
        result = lax.all_to_all(result, PLANE, 0, 0, tiled=True)
        result = result.reshape(main_pairs, rows, block)
    with jax.named_scope("side_out"):
        parts = rotate(join_and_spread(place, keep, got), "z")
    return finish(place, parts, result)


def solution(mesh):
    fine = Mesh(mesh.devices.reshape(Z, YLO, CORE, X, YHI), ("z", "ylo", "core", "x", "yhi"))
    spec = P(None, ("z", "ylo", "core"), ("x", "yhi"))
    return jax.shard_map(
        per_device, mesh=fine, in_specs=(spec, P()), out_specs=spec, check_vma=False
    )
```

```python
import functools

import jax
import jax.numpy as jnp
from jax import lax
from jax.experimental import pallas as pl
from jax.experimental.pallas import tpu as pltpu
from jax.sharding import Mesh, PartitionSpec as P

Z, YLO, CORE, X, YHI = 8, 2, 2, 4, 2
COLS = X * YHI
BLOCKS = 8
PLANE = ("x", "yhi", "ylo")
SIDE = ("x", "yhi")
AT_Z, AT_YLO, AT_CORE, AT_C = range(4)
F32 = jnp.float32
BF16 = jnp.bfloat16
PARAMS = pltpu.CompilerParams(vmem_limit_bytes=24 * 2**20)
SMALL = pltpu.CompilerParams(vmem_limit_bytes=8 * 2**20)


ORDER = {AT_Z: (0, 4, 3, 5, 2, 6, 1, 7), AT_C: (0, 3, 5, 1, 7, 4, 2, 6)}
STEPS = 4
HBM = pl.BlockSpec(memory_space=pltpu.HBM)


def in_hbm(value):
    return pltpu.with_memory_space_constraint(value, pltpu.HBM)


def fetch_of(c_hbm, c_ref, sems, step):
    rows = c_ref.shape[1]
    return pltpu.make_async_copy(
        c_hbm.at[pl.ds(pl.multiple_of(step * rows, rows), rows)], c_ref.at[step], sems.at[step]
    )


def steps(c_hbm, c_ref, sems, body):
    def start(step, carry):
        fetch_of(c_hbm, c_ref, sems, step).start()
        return carry

    def run(step, carry):
        body(step)
        return carry

    lax.fori_loop(0, STEPS, start, 0)
    lax.fori_loop(0, STEPS, run, 0)


def fetch_scratch(value):
    size, width = value.shape
    return [pltpu.VMEM((STEPS, size // STEPS, width), BF16), pltpu.SemaphoreType.DMA((STEPS,))]


def transposed(block):
    size = block.shape[1]
    row = lax.broadcasted_iota(jnp.int32, (size, size), 0)
    column = lax.broadcasted_iota(jnp.int32, (size, size), 1)
    eye = (row == column).astype(F32).astype(BF16)
    return lax.dot_general(
        eye, block, (((1,), (1,)), ((), ())), preferred_element_type=F32
    ).astype(BF16)


def pick_kernel(place, c_hbm, out_hbm, c_ref, sems, chosen, out_sems):
    block = c_hbm.shape[1] // BLOCKS
    lanes = block // CORE
    half = lanes // 2
    rows = c_hbm.shape[0] // STEPS

    def store_of(step):
        return pltpu.make_async_copy(
            chosen.at[step], out_hbm.at[pl.ds(pl.multiple_of(step * rows, rows), rows)], out_sems.at[step]
        )

    def choose(step):
        fetch_of(c_hbm, c_ref, sems, step).wait()
        for core in range(CORE):
            @pl.when(place[AT_CORE] == core)
            def _():
                for b in range(BLOCKS):
                    pieces = []
                    for y in range(YLO):
                        tile = c_ref[step, :, b * block + y * lanes:b * block + (y + 1) * lanes]
                        pieces.append(tile[:, core * half:(core + 1) * half])
                    chosen[step, :, b * lanes:(b + 1) * lanes] = jnp.concatenate(pieces, axis=1)
        store_of(step).start()

    def finish_store(step, carry):
        store_of(step).wait()
        return carry

    steps(c_hbm, c_ref, sems, choose)
    lax.fori_loop(0, STEPS, finish_store, 0)


def pick_columns(place, orbitals):
    size = orbitals.shape[0]
    width = size // CORE
    return pl.pallas_call(
        pick_kernel,
        out_shape=pltpu.HBM((size, width), BF16),
        in_specs=[pl.BlockSpec(memory_space=pltpu.SMEM), HBM],
        out_specs=HBM,
        scratch_shapes=fetch_scratch(orbitals) + [
            pltpu.VMEM((STEPS, size // STEPS, width), BF16), pltpu.SemaphoreType.DMA((STEPS,))],
        compiler_params=PARAMS,
        name="pick_columns",
    )(place, in_hbm(orbitals))


def first_kernel(index, place, direct, direct_other, turned, turned_other, c_hbm, *rest):
    t_refs = rest[:-5]
    c_ref, sems, sym, turn, total = rest[-5:]
    _, _, depth, rows, block = direct.shape
    mine, core = place[index], place[AT_CORE]
    per_step = BLOCKS // STEPS
    total[...] = jnp.zeros(total.shape, F32)

    def work(step):
        for u in range(per_step):
            b = step * per_step + u
            cols = slice(u * block, (u + 1) * block)

            @pl.when(b >= mine)
            def _():
                for k in range(depth):
                    for y in range(YLO):
                        at = k * block + y * CORE * rows
                        sym[pl.ds(pl.multiple_of(at + core * rows, rows), rows), cols] = direct[b, y, k]
                        sym[pl.ds(pl.multiple_of(at + (1 - core) * rows, rows), rows), cols] = direct_other[b, y, k]

            @pl.when(b == mine)
            def _():
                row = lax.broadcasted_iota(jnp.int32, (block, block), 0)
                column = lax.broadcasted_iota(jnp.int32, (block, block), 1)
                for k in range(depth):
                    upper = sym[k * block:(k + 1) * block, cols]
                    sym[k * block:(k + 1) * block, cols] = jnp.where(row <= column, upper, transposed(upper))

            @pl.when(b < mine)
            def _():
                for k in range(depth):
                    for y in range(YLO):
                        at = k * block + y * CORE * rows
                        turn[pl.ds(pl.multiple_of(at + core * rows, rows), rows), :] = turned[b, y, k]
                        turn[pl.ds(pl.multiple_of(at + (1 - core) * rows, rows), rows), :] = turned_other[b, y, k]
                for k in range(depth):
                    sym[k * block:(k + 1) * block, cols] = transposed(turn[k * block:(k + 1) * block])

        fetch_of(c_hbm, c_ref, sems, step).wait()
        total[...] += jnp.dot(sym[...], c_ref[step], preferred_element_type=F32)

    steps(c_hbm, c_ref, sems, work)
    if len(t_refs) == 1:
        lanes = t_refs[0].shape[3]
        for part in range(BLOCKS):
            for k in range(depth):
                t_refs[0][part, k] = total[k * block:(k + 1) * block, part * lanes:(part + 1) * lanes].astype(BF16)
    else:
        lanes = t_refs[0].shape[2]
        for d in range(BLOCKS):
            part = (mine + ORDER[index][d]) % BLOCKS
            t_refs[d][0] = total[:, pl.ds(pl.multiple_of(part * lanes, lanes), lanes)].astype(BF16)


def first_half(index, place, direct, direct_other, turned, turned_other, picked, outs, name):
    _, _, depth, rows, block = direct.shape
    size, width = picked.shape
    vmem = pl.BlockSpec(memory_space=pltpu.VMEM)
    return pl.pallas_call(
        functools.partial(first_kernel, index),
        out_shape=[jax.ShapeDtypeStruct(out, BF16) for out in outs],
        in_specs=[pl.BlockSpec(memory_space=pltpu.SMEM), vmem, vmem, vmem, vmem, HBM],
        out_specs=[vmem] * len(outs),
        scratch_shapes=fetch_scratch(picked) + [
            pltpu.VMEM((depth * block, size // STEPS), BF16),
            pltpu.VMEM((depth * block, block), BF16),
            pltpu.VMEM((depth * block, width), F32)],
        compiler_params=PARAMS,
        name=name,
    )(place, direct, direct_other, turned, turned_other, in_hbm(picked))


def second_kernel(t_ref, c_hbm, out_ref, c_ref, sems, left, total):
    count, depth, block, lanes = t_ref.shape
    rows = lanes // YLO
    per_step = count // STEPS
    total[...] = jnp.zeros(total.shape, F32)

    def work(step):
        for u in range(per_step):
            for k in range(depth):
                left[k * lanes:(k + 1) * lanes, u * block:(u + 1) * block] = transposed(t_ref[step * per_step + u, k])
        fetch_of(c_hbm, c_ref, sems, step).wait()
        total[...] += jnp.dot(left[...], c_ref[step], preferred_element_type=F32)

    steps(c_hbm, c_ref, sems, work)
    for c in range(COLS):
        for y in range(YLO):
            for k in range(depth):
                at = k * lanes + y * rows
                out_ref[c, y, k] = total[at:at + rows, c * block:(c + 1) * block].astype(BF16)


def second_half(partial_value, orbitals):
    _, depth, block, lanes = partial_value.shape
    size = orbitals.shape[0]
    vmem = pl.BlockSpec(memory_space=pltpu.VMEM)
    return pl.pallas_call(
        second_kernel,
        out_shape=jax.ShapeDtypeStruct((COLS, YLO, depth, lanes // YLO, block), BF16),
        in_specs=[vmem, HBM],
        out_specs=vmem,
        scratch_shapes=fetch_scratch(orbitals) + [
            pltpu.VMEM((depth * lanes, size // STEPS), BF16),
            pltpu.VMEM((depth * lanes, size), F32)],
        compiler_params=PARAMS,
        name="second_half",
    )(partial_value, in_hbm(orbitals))


def second_side_kernel(place, t_ref, other_ref, c_hbm, keep, send, c_ref, sems, left, total, final):
    count, _, block, lanes = t_ref.shape
    rows = lanes // YLO
    per_step = count // STEPS
    ylo, core = place[AT_YLO], place[AT_CORE]
    total[...] = jnp.zeros(total.shape, F32)

    def work(step):
        for u in range(per_step):
            cols = slice(u * block, (u + 1) * block)
            own = transposed(t_ref[step * per_step + u, 0])
            other = transposed(other_ref[step * per_step + u, 0])
            for y in range(YLO):
                at = y * CORE * rows
                left[pl.ds(pl.multiple_of(at + core * rows, rows), rows), cols] = own[y * rows:(y + 1) * rows]
                left[pl.ds(pl.multiple_of(at + (1 - core) * rows, rows), rows), cols] = other[y * rows:(y + 1) * rows]
        fetch_of(c_hbm, c_ref, sems, step).wait()
        total[...] += jnp.dot(left[...], c_ref[step], preferred_element_type=F32)

    steps(c_hbm, c_ref, sems, work)
    for part in range(total.shape[1] // block):
        cols = slice(part * block, (part + 1) * block)
        final[cols] = transposed(total[:, cols].astype(BF16))
    for z in range(Z):
        at = z * YLO * rows
        keep[z] = final[pl.ds(pl.multiple_of(at + ylo * rows, rows), rows)]
        send[z] = final[pl.ds(pl.multiple_of(at + (1 - ylo) * rows, rows), rows)]


def second_half_side(place, own, other, picked):
    _, _, block, lanes = own.shape
    size, width = picked.shape
    vmem = pl.BlockSpec(memory_space=pltpu.VMEM)
    out = jax.ShapeDtypeStruct((Z, lanes // YLO, block), BF16)
    return pl.pallas_call(
        second_side_kernel,
        out_shape=[out, out],
        in_specs=[pl.BlockSpec(memory_space=pltpu.SMEM), vmem, vmem, HBM],
        out_specs=[vmem, vmem],
        scratch_shapes=fetch_scratch(picked) + [
            pltpu.VMEM((block, size // STEPS), BF16),
            pltpu.VMEM((block, width), F32),
            pltpu.VMEM((width, block), BF16)],
        compiler_params=PARAMS,
        name="second_half_side",
    )(place, own, other, in_hbm(picked))


def spread_kernel(index, place, x_ref, *out_refs):
    for d in range(BLOCKS):
        out_refs[d][...] = x_ref[(place[index] + ORDER[index][d]) % BLOCKS]


def spread(index, place, value):
    vmem = pl.BlockSpec(memory_space=pltpu.VMEM)
    return pl.pallas_call(
        functools.partial(spread_kernel, index),
        out_shape=[jax.ShapeDtypeStruct(value.shape[1:], BF16)] * BLOCKS,
        in_specs=[pl.BlockSpec(memory_space=pltpu.SMEM), vmem],
        out_specs=[vmem] * BLOCKS,
        compiler_params=SMALL,
        name="spread",
    )(place, value)


def join_kernel(place, keep, got, *out_refs):
    z, ylo = place[AT_Z], place[AT_YLO]
    for d in range(BLOCKS):
        out_refs[d][ylo] = keep[(z + ORDER[AT_Z][d]) % BLOCKS]
        out_refs[d][1 - ylo] = got[(z + ORDER[AT_Z][d]) % BLOCKS]


def join_and_spread(place, keep, got):
    vmem = pl.BlockSpec(memory_space=pltpu.VMEM)
    return pl.pallas_call(
        join_kernel,
        out_shape=[jax.ShapeDtypeStruct((YLO,) + keep.shape[1:], BF16)] * BLOCKS,
        in_specs=[pl.BlockSpec(memory_space=pltpu.SMEM), vmem, vmem],
        out_specs=[vmem] * BLOCKS,
        compiler_params=SMALL,
        name="join_and_spread",
    )(place, keep, got)


def collect_kernel(index, place, *refs):
    out_ref = refs[BLOCKS]
    for d in range(BLOCKS):
        out_ref[(place[index] + BLOCKS - ORDER[index][d]) % BLOCKS] = refs[d][...]


def collect(index, place, parts):
    vmem = pl.BlockSpec(memory_space=pltpu.VMEM)
    return pl.pallas_call(
        functools.partial(collect_kernel, index),
        out_shape=jax.ShapeDtypeStruct((BLOCKS,) + parts[0].shape, BF16),
        in_specs=[pl.BlockSpec(memory_space=pltpu.SMEM)] + [vmem] * BLOCKS,
        out_specs=vmem,
        compiler_params=SMALL,
        name="collect",
    )(place, *parts)


def finish_kernel(place, *refs):
    main_ref, out_hbm, sems = refs[BLOCKS:]
    main = main_ref.shape[0]
    copies = [pltpu.make_async_copy(main_ref, out_hbm.at[pl.ds(0, main)], sems.at[BLOCKS * YLO])]
    for d in range(BLOCKS):
        for y in range(YLO):
            to = main + y * BLOCKS + (place[AT_Z] + BLOCKS - ORDER[AT_Z][d]) % BLOCKS
            copies.append(pltpu.make_async_copy(refs[d].at[y], out_hbm.at[to], sems.at[d * YLO + y]))
    for copy in copies:
        copy.start()
    for copy in copies:
        copy.wait()


def finish(place, parts, main):
    pairs, rows, block = main.shape
    vmem = pl.BlockSpec(memory_space=pltpu.VMEM)
    return pl.pallas_call(
        finish_kernel,
        out_shape=jax.ShapeDtypeStruct((pairs + YLO * BLOCKS, rows, block), BF16),
        in_specs=[pl.BlockSpec(memory_space=pltpu.SMEM)] + [vmem] * (BLOCKS + 1),
        out_specs=HBM,
        scratch_shapes=[pltpu.SemaphoreType.DMA((BLOCKS * YLO + 1,))],
        compiler_params=SMALL,
        name="finish",
    )(place, *parts, main)


def rotate(index, parts, axes):
    out = [parts[0]]
    for part, d in zip(parts[1:], ORDER[index][1:]):
        out.append(lax.ppermute(part, axes, [(i, (i + d) % BLOCKS) for i in range(BLOCKS)]))
    return out


def swap(value, axis):
    return lax.ppermute(value, axis, [(0, 1), (1, 0)])


def per_device(half_panel, orbitals):
    pairs, rows, block = half_panel.shape
    side_pairs = Z * YLO
    main_pairs = pairs - side_pairs
    depth = main_pairs // (COLS * YLO)
    z, ylo, core = lax.axis_index("z"), lax.axis_index("ylo"), lax.axis_index("core")
    c = lax.axis_index("x") * YHI + lax.axis_index("yhi")

    place = jnp.stack([z, ylo, core, c]).astype(jnp.int32)

    def deep(value):
        return value.reshape(BLOCKS, YLO, 1, rows, block)

    together = lax.optimization_barrier

    with jax.named_scope("side_in"):
        side = half_panel[main_pairs:].reshape(YLO, Z, rows, block)
        got = swap(lax.dynamic_index_in_dim(side, 1 - ylo, 0, keepdims=False), "ylo")
        keep = lax.dynamic_index_in_dim(side, ylo, 0, keepdims=False)
    picked = pick_columns(place, orbitals)
    own = half_panel[:main_pairs].reshape(COLS * YLO, depth, rows, block)
    own, got, keep, picked = together((own, got, keep, picked))

    with jax.named_scope("panels_in"):
        own = lax.all_to_all(own, PLANE, 0, 0, tiled=True)
        own = own.reshape(COLS, YLO, depth, rows, block)
    with jax.named_scope("side_in"):
        parts = rotate(AT_Z, join_and_spread(place, keep, got), "z")
        side_own = collect(AT_Z, place, parts)
    own, side_own, picked = together((own, side_own, picked))

    with jax.named_scope("mirror"):
        own_low = lax.all_to_all(own, "z", 0, 0, tiled=True)
    other = swap(own, "core")
    with jax.named_scope("side_mirror"):
        side_other = swap(side_own, "core")
        parts = rotate(AT_C, spread(AT_C, place, side_own), SIDE)
        side_low = collect(AT_C, place, parts)
        side_other_low = swap(side_low, "core")
        side_partial = first_half(
            AT_C, place, deep(side_low), deep(side_other_low), deep(side_own), deep(side_other),
            picked, [(1, block, block // CORE)] * BLOCKS, "first_half_side"
        )
    own_low, other, side_partial = together((own_low, other, side_partial))

    other_low = swap(own_low, "core")
    partial_value, = first_half(
        AT_Z, place, own, other, own_low, other_low, picked,
        [(BLOCKS, depth, block, block // CORE)], "first_half"
    )
    with jax.named_scope("partial"):
        partial_value = lax.all_to_all(partial_value, "z", 0, 0, tiled=True)
    with jax.named_scope("side_partial"):
        parts = rotate(AT_C, side_partial, SIDE)
        side_partial = collect(AT_C, place, parts)
        side_partial_other = swap(side_partial, "core")
        keep, send = second_half_side(place, side_partial, side_partial_other, picked)
    got = swap(send, "ylo")
    partial_value, keep = together((partial_value, keep))

    result = second_half(partial_value, orbitals)
    result, got, keep = together((result, got, keep))

    with jax.named_scope("panels_out"):
        result = result.reshape(COLS * YLO, depth, rows, block)
        result = lax.all_to_all(result, PLANE, 0, 0, tiled=True)
        result = result.reshape(main_pairs, rows, block)
    with jax.named_scope("side_out"):
        parts = rotate(AT_Z, join_and_spread(place, keep, got), "z")
    return finish(place, parts, result)


def solution(mesh):
    fine = Mesh(mesh.devices.reshape(Z, YLO, CORE, X, YHI), ("z", "ylo", "core", "x", "yhi"))
    spec = P(None, ("z", "ylo", "core"), ("x", "yhi"))
    return jax.shard_map(
        per_device, mesh=fine, in_specs=(spec, P()), out_specs=spec, check_vma=False
    )
```

```python
import functools

import jax
import jax.numpy as jnp
from jax import lax
from jax.experimental import pallas as pl
from jax.experimental.pallas import tpu as pltpu
from jax.sharding import Mesh, PartitionSpec as P

Z, YLO, CORE, X, YHI = 8, 2, 2, 4, 2
COLS = X * YHI
BLOCKS = 8
PLANE = ("x", "yhi", "ylo")
SIDE = ("x", "yhi")
AT_Z, AT_YLO, AT_CORE, AT_C = range(4)
F32 = jnp.float32
BF16 = jnp.bfloat16
PARAMS = pltpu.CompilerParams(vmem_limit_bytes=24 * 2**20)
SMALL = pltpu.CompilerParams(vmem_limit_bytes=8 * 2**20)


ORDER = {AT_Z: (0, 4, 3, 5, 2, 6, 1, 7), AT_C: (0, 3, 5, 1, 7, 4, 2, 6)}
STEPS = 4
HBM = pl.BlockSpec(memory_space=pltpu.HBM)


def in_hbm(value):
    return pltpu.with_memory_space_constraint(value, pltpu.HBM)


def fetch_of(c_hbm, c_ref, sems, step):
    rows = c_ref.shape[1]
    return pltpu.make_async_copy(
        c_hbm.at[pl.ds(pl.multiple_of(step * rows, rows), rows)], c_ref.at[step], sems.at[step]
    )


def steps(c_hbm, c_ref, sems, body):
    def start(step, carry):
        fetch_of(c_hbm, c_ref, sems, step).start()
        return carry

    def run(step, carry):
        body(step)
        return carry

    lax.fori_loop(0, STEPS, start, 0)
    lax.fori_loop(0, STEPS, run, 0)


def fetch_scratch(value):
    size, width = value.shape
    return [pltpu.VMEM((STEPS, size // STEPS, width), BF16), pltpu.SemaphoreType.DMA((STEPS,))]


def set_identity(eye):
    row = lax.broadcasted_iota(jnp.int32, eye.shape, 0)
    column = lax.broadcasted_iota(jnp.int32, eye.shape, 1)
    eye[...] = (row == column).astype(F32).astype(BF16)


def transposed(block, eye):
    size = block.shape[1]
    return lax.dot_general(
        eye[:size, :size], block, (((1,), (1,)), ((), ())), preferred_element_type=F32
    ).astype(BF16)


def pick_kernel(place, c_hbm, panel_hbm, out_hbm, main_hbm, c_ref, sems, chosen, out_sems, main_sem):
    main = pltpu.make_async_copy(panel_hbm.at[pl.ds(0, main_hbm.shape[0])], main_hbm, main_sem)
    main.start()
    block = c_hbm.shape[1] // BLOCKS
    lanes = block // CORE
    half = lanes // 2
    rows = c_hbm.shape[0] // STEPS

    def store_of(step):
        return pltpu.make_async_copy(
            chosen.at[step], out_hbm.at[pl.ds(pl.multiple_of(step * rows, rows), rows)], out_sems.at[step]
        )

    def choose(step):
        fetch_of(c_hbm, c_ref, sems, step).wait()
        for core in range(CORE):
            @pl.when(place[AT_CORE] == core)
            def _():
                for b in range(BLOCKS):
                    pieces = []
                    for y in range(YLO):
                        tile = c_ref[step, :, b * block + y * lanes:b * block + (y + 1) * lanes]
                        pieces.append(tile[:, core * half:(core + 1) * half])
                    chosen[step, :, b * lanes:(b + 1) * lanes] = jnp.concatenate(pieces, axis=1)
        store_of(step).start()

    def finish_store(step, carry):
        store_of(step).wait()
        return carry

    steps(c_hbm, c_ref, sems, choose)
    lax.fori_loop(0, STEPS, finish_store, 0)
    main.wait()


def pick_columns(place, orbitals, half_panel, main_pairs):
    size = orbitals.shape[0]
    width = size // CORE
    return pl.pallas_call(
        pick_kernel,
        out_shape=[pltpu.HBM((size, width), BF16), pltpu.HBM((main_pairs,) + half_panel.shape[1:], BF16)],
        in_specs=[pl.BlockSpec(memory_space=pltpu.SMEM), HBM, HBM],
        out_specs=[HBM, HBM],
        scratch_shapes=fetch_scratch(orbitals) + [
            pltpu.VMEM((STEPS, size // STEPS, width), BF16), pltpu.SemaphoreType.DMA((STEPS,)),
            pltpu.SemaphoreType.DMA(())],
        compiler_params=PARAMS,
        name="pick_columns",
    )(place, in_hbm(orbitals), in_hbm(half_panel))


def first_kernel(index, place, direct, direct_other, turned, turned_other, c_hbm, *rest):
    t_refs = rest[:-6]
    c_ref, sems, sym, turn, total, eye = rest[-6:]
    set_identity(eye)
    _, _, depth, rows, block = direct.shape
    mine, core = place[index], place[AT_CORE]
    per_step = BLOCKS // STEPS
    total[...] = jnp.zeros(total.shape, F32)

    def work(step):
        for u in range(per_step):
            b = step * per_step + u
            cols = slice(u * block, (u + 1) * block)

            @pl.when(b >= mine)
            def _():
                for k in range(depth):
                    for y in range(YLO):
                        at = k * block + y * CORE * rows
                        sym[pl.ds(pl.multiple_of(at + core * rows, rows), rows), cols] = direct[b, y, k]
                        sym[pl.ds(pl.multiple_of(at + (1 - core) * rows, rows), rows), cols] = direct_other[b, y, k]

            @pl.when(b == mine)
            def _():
                row = lax.broadcasted_iota(jnp.int32, (block, block), 0)
                column = lax.broadcasted_iota(jnp.int32, (block, block), 1)
                for k in range(depth):
                    upper = sym[k * block:(k + 1) * block, cols]
                    sym[k * block:(k + 1) * block, cols] = jnp.where(row <= column, upper, transposed(upper, eye))

            @pl.when(b < mine)
            def _():
                for k in range(depth):
                    for y in range(YLO):
                        at = k * block + y * CORE * rows
                        turn[pl.ds(pl.multiple_of(at + core * rows, rows), rows), :] = turned[b, y, k]
                        turn[pl.ds(pl.multiple_of(at + (1 - core) * rows, rows), rows), :] = turned_other[b, y, k]
                for k in range(depth):
                    sym[k * block:(k + 1) * block, cols] = transposed(turn[k * block:(k + 1) * block], eye)

        fetch_of(c_hbm, c_ref, sems, step).wait()
        total[...] += jnp.dot(sym[...], c_ref[step], preferred_element_type=F32)

    steps(c_hbm, c_ref, sems, work)
    if len(t_refs) == 1:
        lanes = t_refs[0].shape[3]
        for part in range(BLOCKS):
            for k in range(depth):
                t_refs[0][part, k] = total[k * block:(k + 1) * block, part * lanes:(part + 1) * lanes].astype(BF16)
    else:
        lanes = t_refs[0].shape[2]
        for d in range(BLOCKS):
            part = (mine + ORDER[index][d]) % BLOCKS
            t_refs[d][0] = total[:, pl.ds(pl.multiple_of(part * lanes, lanes), lanes)].astype(BF16)


def first_half(index, place, direct, direct_other, turned, turned_other, picked, outs, name):
    _, _, depth, rows, block = direct.shape
    size, width = picked.shape
    vmem = pl.BlockSpec(memory_space=pltpu.VMEM)
    return pl.pallas_call(
        functools.partial(first_kernel, index),
        out_shape=[jax.ShapeDtypeStruct(out, BF16) for out in outs],
        in_specs=[pl.BlockSpec(memory_space=pltpu.SMEM), vmem, vmem, vmem, vmem, HBM],
        out_specs=[vmem] * len(outs),
        scratch_shapes=fetch_scratch(picked) + [
            pltpu.VMEM((depth * block, size // STEPS), BF16),
            pltpu.VMEM((depth * block, block), BF16),
            pltpu.VMEM((depth * block, width), F32),
            pltpu.VMEM((block, block), BF16)],
        compiler_params=PARAMS,
        name=name,
    )(place, direct, direct_other, turned, turned_other, in_hbm(picked))


def second_kernel(t_ref, c_hbm, out_ref, c_ref, sems, left, total, eye):
    set_identity(eye)
    count, depth, block, lanes = t_ref.shape
    rows = lanes // YLO
    per_step = count // STEPS
    total[...] = jnp.zeros(total.shape, F32)

    def work(step):
        for u in range(per_step):
            for k in range(depth):
                left[k * lanes:(k + 1) * lanes, u * block:(u + 1) * block] = transposed(t_ref[step * per_step + u, k], eye)
        fetch_of(c_hbm, c_ref, sems, step).wait()
        total[...] += jnp.dot(left[...], c_ref[step], preferred_element_type=F32)

    steps(c_hbm, c_ref, sems, work)
    for c in range(COLS):
        for y in range(YLO):
            for k in range(depth):
                at = k * lanes + y * rows
                out_ref[c, y, k] = total[at:at + rows, c * block:(c + 1) * block].astype(BF16)


def second_half(partial_value, orbitals):
    _, depth, block, lanes = partial_value.shape
    size = orbitals.shape[0]
    vmem = pl.BlockSpec(memory_space=pltpu.VMEM)
    return pl.pallas_call(
        second_kernel,
        out_shape=jax.ShapeDtypeStruct((COLS, YLO, depth, lanes // YLO, block), BF16),
        in_specs=[vmem, HBM],
        out_specs=vmem,
        scratch_shapes=fetch_scratch(orbitals) + [
            pltpu.VMEM((depth * lanes, size // STEPS), BF16),
            pltpu.VMEM((depth * lanes, size), F32),
            pltpu.VMEM((lanes, lanes), BF16)],
        compiler_params=PARAMS,
        name="second_half",
    )(partial_value, in_hbm(orbitals))


def second_side_kernel(place, t_ref, other_ref, c_hbm, keep, send, c_ref, sems, left, total, final, eye):
    set_identity(eye)
    count, _, block, lanes = t_ref.shape
    rows = lanes // YLO
    per_step = count // STEPS
    ylo, core = place[AT_YLO], place[AT_CORE]
    total[...] = jnp.zeros(total.shape, F32)

    def work(step):
        for u in range(per_step):
            cols = slice(u * block, (u + 1) * block)
            own = transposed(t_ref[step * per_step + u, 0], eye)
            other = transposed(other_ref[step * per_step + u, 0], eye)
            for y in range(YLO):
                at = y * CORE * rows
                left[pl.ds(pl.multiple_of(at + core * rows, rows), rows), cols] = own[y * rows:(y + 1) * rows]
                left[pl.ds(pl.multiple_of(at + (1 - core) * rows, rows), rows), cols] = other[y * rows:(y + 1) * rows]
        fetch_of(c_hbm, c_ref, sems, step).wait()
        total[...] += jnp.dot(left[...], c_ref[step], preferred_element_type=F32)

    steps(c_hbm, c_ref, sems, work)
    for part in range(total.shape[1] // block):
        cols = slice(part * block, (part + 1) * block)
        final[cols] = transposed(total[:, cols].astype(BF16), eye)
    for z in range(Z):
        at = z * YLO * rows
        keep[z] = final[pl.ds(pl.multiple_of(at + ylo * rows, rows), rows)]
        send[z] = final[pl.ds(pl.multiple_of(at + (1 - ylo) * rows, rows), rows)]


def second_half_side(place, own, other, picked):
    _, _, block, lanes = own.shape
    size, width = picked.shape
    vmem = pl.BlockSpec(memory_space=pltpu.VMEM)
    out = jax.ShapeDtypeStruct((Z, lanes // YLO, block), BF16)
    return pl.pallas_call(
        second_side_kernel,
        out_shape=[out, out],
        in_specs=[pl.BlockSpec(memory_space=pltpu.SMEM), vmem, vmem, HBM],
        out_specs=[vmem, vmem],
        scratch_shapes=fetch_scratch(picked) + [
            pltpu.VMEM((block, size // STEPS), BF16),
            pltpu.VMEM((block, width), F32),
            pltpu.VMEM((width, block), BF16),
            pltpu.VMEM((block, block), BF16)],
        compiler_params=PARAMS,
        name="second_half_side",
    )(place, own, other, in_hbm(picked))


def spread_kernel(index, place, x_ref, *out_refs):
    for d in range(BLOCKS):
        out_refs[d][...] = x_ref[(place[index] + ORDER[index][d]) % BLOCKS]


def spread(index, place, value):
    vmem = pl.BlockSpec(memory_space=pltpu.VMEM)
    return pl.pallas_call(
        functools.partial(spread_kernel, index),
        out_shape=[jax.ShapeDtypeStruct(value.shape[1:], BF16)] * BLOCKS,
        in_specs=[pl.BlockSpec(memory_space=pltpu.SMEM), vmem],
        out_specs=[vmem] * BLOCKS,
        compiler_params=SMALL,
        name="spread",
    )(place, value)


def join_kernel(place, keep, got, *out_refs):
    z, ylo = place[AT_Z], place[AT_YLO]
    for d in range(BLOCKS):
        out_refs[d][ylo] = keep[(z + ORDER[AT_Z][d]) % BLOCKS]
        out_refs[d][1 - ylo] = got[(z + ORDER[AT_Z][d]) % BLOCKS]


def join_and_spread(place, keep, got):
    vmem = pl.BlockSpec(memory_space=pltpu.VMEM)
    return pl.pallas_call(
        join_kernel,
        out_shape=[jax.ShapeDtypeStruct((YLO,) + keep.shape[1:], BF16)] * BLOCKS,
        in_specs=[pl.BlockSpec(memory_space=pltpu.SMEM), vmem, vmem],
        out_specs=[vmem] * BLOCKS,
        compiler_params=SMALL,
        name="join_and_spread",
    )(place, keep, got)


def collect_kernel(index, place, *refs):
    out_ref = refs[BLOCKS]
    for d in range(BLOCKS):
        out_ref[(place[index] + BLOCKS - ORDER[index][d]) % BLOCKS] = refs[d][...]


def collect(index, place, parts):
    vmem = pl.BlockSpec(memory_space=pltpu.VMEM)
    return pl.pallas_call(
        functools.partial(collect_kernel, index),
        out_shape=jax.ShapeDtypeStruct((BLOCKS,) + parts[0].shape, BF16),
        in_specs=[pl.BlockSpec(memory_space=pltpu.SMEM)] + [vmem] * BLOCKS,
        out_specs=vmem,
        compiler_params=SMALL,
        name="collect",
    )(place, *parts)


def finish_kernel(place, *refs):
    main_ref, out_hbm, sems = refs[BLOCKS:]
    main = main_ref.shape[0]
    copies = [pltpu.make_async_copy(main_ref, out_hbm.at[pl.ds(0, main)], sems.at[BLOCKS * YLO])]
    for d in range(BLOCKS):
        for y in range(YLO):
            to = main + y * BLOCKS + (place[AT_Z] + BLOCKS - ORDER[AT_Z][d]) % BLOCKS
            copies.append(pltpu.make_async_copy(refs[d].at[y], out_hbm.at[to], sems.at[d * YLO + y]))
    for copy in copies:
        copy.start()
    for copy in copies:
        copy.wait()


def finish(place, parts, main):
    pairs, rows, block = main.shape
    vmem = pl.BlockSpec(memory_space=pltpu.VMEM)
    return pl.pallas_call(
        finish_kernel,
        out_shape=jax.ShapeDtypeStruct((pairs + YLO * BLOCKS, rows, block), BF16),
        in_specs=[pl.BlockSpec(memory_space=pltpu.SMEM)] + [vmem] * (BLOCKS + 1),
        out_specs=HBM,
        scratch_shapes=[pltpu.SemaphoreType.DMA((BLOCKS * YLO + 1,))],
        compiler_params=SMALL,
        name="finish",
    )(place, *parts, main)


def rotate(index, parts, axes):
    out = [parts[0]]
    for part, d in zip(parts[1:], ORDER[index][1:]):
        out.append(lax.ppermute(part, axes, [(i, (i + d) % BLOCKS) for i in range(BLOCKS)]))
    return out


def swap(value, axis):
    return lax.ppermute(value, axis, [(0, 1), (1, 0)])


def per_device(half_panel, orbitals):
    pairs, rows, block = half_panel.shape
    side_pairs = Z * YLO
    main_pairs = pairs - side_pairs
    depth = main_pairs // (COLS * YLO)
    z, ylo, core = lax.axis_index("z"), lax.axis_index("ylo"), lax.axis_index("core")
    c = lax.axis_index("x") * YHI + lax.axis_index("yhi")

    place = jnp.stack([z, ylo, core, c]).astype(jnp.int32)

    def deep(value):
        return value.reshape(BLOCKS, YLO, 1, rows, block)

    together = lax.optimization_barrier

    with jax.named_scope("side_in"):
        side = half_panel[main_pairs:].reshape(YLO, Z, rows, block)
        got = swap(lax.dynamic_index_in_dim(side, 1 - ylo, 0, keepdims=False), "ylo")
        keep = lax.dynamic_index_in_dim(side, ylo, 0, keepdims=False)
    picked, own = pick_columns(place, orbitals, half_panel, main_pairs)
    own = own.reshape(COLS * YLO, depth, rows, block)
    own, got, keep, picked = together((own, got, keep, picked))

    with jax.named_scope("panels_in"):
        own = lax.all_to_all(own, PLANE, 0, 0, tiled=True)
        own = own.reshape(COLS, YLO, depth, rows, block)
    with jax.named_scope("side_in"):
        parts = rotate(AT_Z, join_and_spread(place, keep, got), "z")
        side_own = collect(AT_Z, place, parts)
    own, side_own, picked = together((own, side_own, picked))

    with jax.named_scope("mirror"):
        own_low = lax.all_to_all(own, "z", 0, 0, tiled=True)
    other = swap(own, "core")
    with jax.named_scope("side_mirror"):
        side_other = swap(side_own, "core")
        parts = rotate(AT_C, spread(AT_C, place, side_own), SIDE)
        side_low = collect(AT_C, place, parts)
        side_other_low = swap(side_low, "core")
        side_partial = first_half(
            AT_C, place, deep(side_low), deep(side_other_low), deep(side_own), deep(side_other),
            picked, [(1, block, block // CORE)] * BLOCKS, "first_half_side"
        )
    own_low, other, side_partial = together((own_low, other, side_partial))

    other_low = swap(own_low, "core")
    partial_value, = first_half(
        AT_Z, place, own, other, own_low, other_low, picked,
        [(BLOCKS, depth, block, block // CORE)], "first_half"
    )
    with jax.named_scope("partial"):
        partial_value = lax.all_to_all(partial_value, "z", 0, 0, tiled=True)
    with jax.named_scope("side_partial"):
        parts = rotate(AT_C, side_partial, SIDE)
        side_partial = collect(AT_C, place, parts)
        side_partial_other = swap(side_partial, "core")
        keep, send = second_half_side(place, side_partial, side_partial_other, picked)
    got = swap(send, "ylo")
    partial_value, keep = together((partial_value, keep))

    result = second_half(partial_value, orbitals)
    result, got, keep = together((result, got, keep))

    with jax.named_scope("panels_out"):
        result = result.reshape(COLS * YLO, depth, rows, block)
        result = lax.all_to_all(result, PLANE, 0, 0, tiled=True)
        result = result.reshape(main_pairs, rows, block)
    with jax.named_scope("side_out"):
        parts = rotate(AT_Z, join_and_spread(place, keep, got), "z")
    return finish(place, parts, result)


def solution(mesh):
    fine = Mesh(mesh.devices.reshape(Z, YLO, CORE, X, YHI), ("z", "ylo", "core", "x", "yhi"))
    spec = P(None, ("z", "ylo", "core"), ("x", "yhi"))
    return jax.shard_map(
        per_device, mesh=fine, in_specs=(spec, P()), out_specs=spec, check_vma=False
    )
```

```python
import functools

import jax
import jax.numpy as jnp
from jax import lax
from jax.experimental import pallas as pl
from jax.experimental.pallas import tpu as pltpu
from jax.sharding import Mesh, PartitionSpec as P

Z, YLO, CORE, X, YHI = 8, 2, 2, 4, 2
COLS = X * YHI
BLOCKS = 8
PLANE = ("x", "yhi", "ylo")
SIDE = ("x", "yhi")
AT_Z, AT_YLO, AT_CORE, AT_C = range(4)
F32 = jnp.float32
BF16 = jnp.bfloat16
PARAMS = pltpu.CompilerParams(vmem_limit_bytes=24 * 2**20)
SMALL = pltpu.CompilerParams(vmem_limit_bytes=8 * 2**20)


ORDER = {AT_Z: (0, 4, 3, 5, 2, 6, 1, 7), AT_C: (0, 3, 5, 1, 7, 4, 2, 6)}
STEPS = 4
HBM = pl.BlockSpec(memory_space=pltpu.HBM)


def in_hbm(value):
    return pltpu.with_memory_space_constraint(value, pltpu.HBM)


def fetch_of(c_hbm, c_ref, sems, step):
    rows = c_ref.shape[1]
    return pltpu.make_async_copy(
        c_hbm.at[pl.ds(pl.multiple_of(step * rows, rows), rows)], c_ref.at[step], sems.at[step]
    )


def steps(c_hbm, c_ref, sems, body):
    def start(step, carry):
        fetch_of(c_hbm, c_ref, sems, step).start()
        return carry

    def run(step, carry):
        body(step)
        return carry

    lax.fori_loop(0, STEPS, start, 0)
    lax.fori_loop(0, STEPS, run, 0)


def fetch_scratch(value):
    size, width = value.shape
    return [pltpu.VMEM((STEPS, size // STEPS, width), BF16), pltpu.SemaphoreType.DMA((STEPS,))]


def columns_of(c_hbm, c_ref, sems, step):
    width = c_ref.shape[2]
    return pltpu.make_async_copy(
        c_hbm.at[:, pl.ds(pl.multiple_of(step * width, width), width)], c_ref.at[step], sems.at[step]
    )


def fetch_columns(c_hbm, c_ref, sems):
    def start(step, carry):
        columns_of(c_hbm, c_ref, sems, step).start()
        return carry

    lax.fori_loop(0, STEPS, start, 0)


def products(left, c_hbm, c_ref, sems, store):
    def run(step, carry):
        columns_of(c_hbm, c_ref, sems, step).wait()
        store(step, jnp.dot(left[...], c_ref[step], preferred_element_type=F32).astype(BF16))
        return carry

    lax.fori_loop(0, STEPS, run, 0)


def column_scratch(value):
    size, width = value.shape
    return [pltpu.VMEM((STEPS, size, width // STEPS), BF16), pltpu.SemaphoreType.DMA((STEPS,))]


def set_identity(eye):
    row = lax.broadcasted_iota(jnp.int32, eye.shape, 0)
    column = lax.broadcasted_iota(jnp.int32, eye.shape, 1)
    eye[...] = (row == column).astype(F32).astype(BF16)


def transposed(block, eye):
    size = block.shape[1]
    return lax.dot_general(
        eye[:size, :size], block, (((1,), (1,)), ((), ())), preferred_element_type=F32
    ).astype(BF16)


def pick_kernel(place, c_hbm, panel_hbm, out_hbm, main_hbm, c_ref, sems, chosen, out_sems, panel, main_sems):
    main_in = pltpu.make_async_copy(panel_hbm.at[pl.ds(0, main_hbm.shape[0])], panel, main_sems.at[0])
    main_out = pltpu.make_async_copy(panel, main_hbm, main_sems.at[1])
    main_in.start()
    block = c_hbm.shape[1] // BLOCKS
    lanes = block // CORE
    half = lanes // 2
    rows = c_hbm.shape[0] // STEPS

    def store_of(step):
        return pltpu.make_async_copy(
            chosen.at[step], out_hbm.at[pl.ds(pl.multiple_of(step * rows, rows), rows)], out_sems.at[step]
        )

    def choose(step):
        fetch_of(c_hbm, c_ref, sems, step).wait()
        for core in range(CORE):
            @pl.when(place[AT_CORE] == core)
            def _():
                for b in range(BLOCKS):
                    pieces = []
                    for y in range(YLO):
                        tile = c_ref[step, :, b * block + y * lanes:b * block + (y + 1) * lanes]
                        pieces.append(tile[:, core * half:(core + 1) * half])
                    chosen[step, :, b * lanes:(b + 1) * lanes] = jnp.concatenate(pieces, axis=1)
        store_of(step).start()

    def finish_store(step, carry):
        store_of(step).wait()
        return carry

    steps(c_hbm, c_ref, sems, choose)
    main_in.wait()
    main_out.start()
    lax.fori_loop(0, STEPS, finish_store, 0)
    main_out.wait()


def pick_columns(place, orbitals, half_panel, main_pairs):
    size = orbitals.shape[0]
    width = size // CORE
    return pl.pallas_call(
        pick_kernel,
        out_shape=[pltpu.HBM((size, width), BF16), pltpu.HBM((main_pairs,) + half_panel.shape[1:], BF16)],
        in_specs=[pl.BlockSpec(memory_space=pltpu.SMEM), HBM, HBM],
        out_specs=[HBM, HBM],
        scratch_shapes=fetch_scratch(orbitals) + [
            pltpu.VMEM((STEPS, size // STEPS, width), BF16), pltpu.SemaphoreType.DMA((STEPS,)),
            pltpu.VMEM((main_pairs,) + half_panel.shape[1:], BF16), pltpu.SemaphoreType.DMA((2,))],
        compiler_params=PARAMS,
        name="pick_columns",
    )(place, in_hbm(orbitals), in_hbm(half_panel))


def first_kernel(index, place, direct, direct_other, turned, turned_other, c_hbm, *rest):
    t_refs = rest[:-6]
    c_ref, sems, sym, turn, final, eye = rest[-6:]
    _, _, depth, rows, block = direct.shape
    mine, core = place[index], place[AT_CORE]
    fetch_columns(c_hbm, c_ref, sems)
    set_identity(eye)

    def build(b, carry):
        cols = pl.ds(pl.multiple_of(b * block, block), block)

        @pl.when(b >= mine)
        def _():
            for k in range(depth):
                for y in range(YLO):
                    at = k * block + y * CORE * rows
                    sym[pl.ds(pl.multiple_of(at + core * rows, rows), rows), cols] = direct[b, y, k]
                    sym[pl.ds(pl.multiple_of(at + (1 - core) * rows, rows), rows), cols] = direct_other[b, y, k]

        @pl.when(b == mine)
        def _():
            row = lax.broadcasted_iota(jnp.int32, (block, block), 0)
            column = lax.broadcasted_iota(jnp.int32, (block, block), 1)
            for k in range(depth):
                upper = sym[k * block:(k + 1) * block, cols]
                sym[k * block:(k + 1) * block, cols] = jnp.where(row <= column, upper, transposed(upper, eye))

        @pl.when(b < mine)
        def _():
            for k in range(depth):
                for y in range(YLO):
                    at = k * block + y * CORE * rows
                    turn[pl.ds(pl.multiple_of(at + core * rows, rows), rows), :] = turned[b, y, k]
                    turn[pl.ds(pl.multiple_of(at + (1 - core) * rows, rows), rows), :] = turned_other[b, y, k]
            for k in range(depth):
                sym[k * block:(k + 1) * block, cols] = transposed(turn[k * block:(k + 1) * block], eye)

        return carry

    def store(step, product):
        width = product.shape[1]
        final[:, pl.ds(pl.multiple_of(step * width, width), width)] = product

    lax.fori_loop(0, BLOCKS, build, 0)
    products(sym, c_hbm, c_ref, sems, store)
    if len(t_refs) == 1:
        lanes = t_refs[0].shape[3]
        for part in range(BLOCKS):
            for k in range(depth):
                t_refs[0][part, k] = final[k * block:(k + 1) * block, part * lanes:(part + 1) * lanes]
    else:
        lanes = t_refs[0].shape[2]
        for d in range(BLOCKS):
            part = (mine + ORDER[index][d]) % BLOCKS
            t_refs[d][0] = final[:, pl.ds(pl.multiple_of(part * lanes, lanes), lanes)]


def first_half(index, place, direct, direct_other, turned, turned_other, picked, outs, name):
    _, _, depth, rows, block = direct.shape
    size, width = picked.shape
    vmem = pl.BlockSpec(memory_space=pltpu.VMEM)
    return pl.pallas_call(
        functools.partial(first_kernel, index),
        out_shape=[jax.ShapeDtypeStruct(out, BF16) for out in outs],
        in_specs=[pl.BlockSpec(memory_space=pltpu.SMEM), vmem, vmem, vmem, vmem, HBM],
        out_specs=[vmem] * len(outs),
        scratch_shapes=column_scratch(picked) + [
            pltpu.VMEM((depth * block, size), BF16),
            pltpu.VMEM((depth * block, block), BF16),
            pltpu.VMEM((depth * block, width), BF16),
            pltpu.VMEM((block, block), BF16)],
        compiler_params=PARAMS,
        name=name,
    )(place, direct, direct_other, turned, turned_other, in_hbm(picked))


def second_kernel(t_ref, c_hbm, out_ref, c_ref, sems, left, eye):
    count, depth, block, lanes = t_ref.shape
    rows = lanes // YLO
    fetch_columns(c_hbm, c_ref, sems)
    set_identity(eye)

    def build(b, carry):
        for k in range(depth):
            left[k * lanes:(k + 1) * lanes, pl.ds(pl.multiple_of(b * block, block), block)] = transposed(t_ref[b, k], eye)
        return carry

    def store(step, product):
        per_step = COLS // STEPS
        for u in range(per_step):
            for y in range(YLO):
                for k in range(depth):
                    at = k * lanes + y * rows
                    out_ref[step * per_step + u, y, k] = product[at:at + rows, u * block:(u + 1) * block]

    lax.fori_loop(0, count, build, 0)
    products(left, c_hbm, c_ref, sems, store)


def second_half(partial_value, orbitals):
    _, depth, block, lanes = partial_value.shape
    size = orbitals.shape[0]
    vmem = pl.BlockSpec(memory_space=pltpu.VMEM)
    return pl.pallas_call(
        second_kernel,
        out_shape=jax.ShapeDtypeStruct((COLS, YLO, depth, lanes // YLO, block), BF16),
        in_specs=[vmem, HBM],
        out_specs=vmem,
        scratch_shapes=column_scratch(orbitals) + [
            pltpu.VMEM((depth * lanes, size), BF16),
            pltpu.VMEM((lanes, lanes), BF16)],
        compiler_params=PARAMS,
        name="second_half",
    )(partial_value, in_hbm(orbitals))


def second_side_kernel(place, t_ref, other_ref, c_hbm, keep, send, c_ref, sems, left, final, eye):
    count, _, block, lanes = t_ref.shape
    rows = lanes // YLO
    ylo, core = place[AT_YLO], place[AT_CORE]
    fetch_columns(c_hbm, c_ref, sems)
    set_identity(eye)

    def build(b, carry):
        cols = pl.ds(pl.multiple_of(b * block, block), block)
        own = transposed(t_ref[b, 0], eye)
        other = transposed(other_ref[b, 0], eye)
        for y in range(YLO):
            at = y * CORE * rows
            left[pl.ds(pl.multiple_of(at + core * rows, rows), rows), cols] = own[y * rows:(y + 1) * rows]
            left[pl.ds(pl.multiple_of(at + (1 - core) * rows, rows), rows), cols] = other[y * rows:(y + 1) * rows]
        return carry

    def store(step, product):
        width = product.shape[1]
        final[pl.ds(pl.multiple_of(step * width, width), width)] = transposed(product, eye)

    lax.fori_loop(0, count, build, 0)
    products(left, c_hbm, c_ref, sems, store)
    for z in range(Z):
        at = z * YLO * rows
        keep[z] = final[pl.ds(pl.multiple_of(at + ylo * rows, rows), rows)]
        send[z] = final[pl.ds(pl.multiple_of(at + (1 - ylo) * rows, rows), rows)]


def second_half_side(place, own, other, picked):
    _, _, block, lanes = own.shape
    size, width = picked.shape
    vmem = pl.BlockSpec(memory_space=pltpu.VMEM)
    out = jax.ShapeDtypeStruct((Z, lanes // YLO, block), BF16)
    return pl.pallas_call(
        second_side_kernel,
        out_shape=[out, out],
        in_specs=[pl.BlockSpec(memory_space=pltpu.SMEM), vmem, vmem, HBM],
        out_specs=[vmem, vmem],
        scratch_shapes=column_scratch(picked) + [
            pltpu.VMEM((block, size), BF16),
            pltpu.VMEM((width, block), BF16),
            pltpu.VMEM((block, block), BF16)],
        compiler_params=PARAMS,
        name="second_half_side",
    )(place, own, other, in_hbm(picked))


def spread_kernel(index, place, x_ref, *out_refs):
    for d in range(BLOCKS):
        out_refs[d][...] = x_ref[(place[index] + ORDER[index][d]) % BLOCKS]


def spread(index, place, value):
    vmem = pl.BlockSpec(memory_space=pltpu.VMEM)
    return pl.pallas_call(
        functools.partial(spread_kernel, index),
        out_shape=[jax.ShapeDtypeStruct(value.shape[1:], BF16)] * BLOCKS,
        in_specs=[pl.BlockSpec(memory_space=pltpu.SMEM), vmem],
        out_specs=[vmem] * BLOCKS,
        compiler_params=SMALL,
        name="spread",
    )(place, value)


def join_kernel(place, keep, got, *out_refs):
    z, ylo = place[AT_Z], place[AT_YLO]
    for d in range(BLOCKS):
        out_refs[d][ylo] = keep[(z + ORDER[AT_Z][d]) % BLOCKS]
        out_refs[d][1 - ylo] = got[(z + ORDER[AT_Z][d]) % BLOCKS]


def join_and_spread(place, keep, got):
    vmem = pl.BlockSpec(memory_space=pltpu.VMEM)
    return pl.pallas_call(
        join_kernel,
        out_shape=[jax.ShapeDtypeStruct((YLO,) + keep.shape[1:], BF16)] * BLOCKS,
        in_specs=[pl.BlockSpec(memory_space=pltpu.SMEM), vmem, vmem],
        out_specs=[vmem] * BLOCKS,
        compiler_params=SMALL,
        name="join_and_spread",
    )(place, keep, got)


def collect_kernel(index, place, *refs):
    out_ref = refs[BLOCKS]
    for d in range(BLOCKS):
        out_ref[(place[index] + BLOCKS - ORDER[index][d]) % BLOCKS] = refs[d][...]


def collect(index, place, parts):
    vmem = pl.BlockSpec(memory_space=pltpu.VMEM)
    return pl.pallas_call(
        functools.partial(collect_kernel, index),
        out_shape=jax.ShapeDtypeStruct((BLOCKS,) + parts[0].shape, BF16),
        in_specs=[pl.BlockSpec(memory_space=pltpu.SMEM)] + [vmem] * BLOCKS,
        out_specs=vmem,
        compiler_params=SMALL,
        name="collect",
    )(place, *parts)


def finish_kernel(place, *refs):
    main_ref, out_hbm, sems = refs[BLOCKS:]
    main = main_ref.shape[0]
    copies = [pltpu.make_async_copy(main_ref, out_hbm.at[pl.ds(0, main)], sems.at[BLOCKS * YLO])]
    for d in range(BLOCKS):
        for y in range(YLO):
            to = main + y * BLOCKS + (place[AT_Z] + BLOCKS - ORDER[AT_Z][d]) % BLOCKS
            copies.append(pltpu.make_async_copy(refs[d].at[y], out_hbm.at[to], sems.at[d * YLO + y]))
    for copy in copies:
        copy.start()
    for copy in copies:
        copy.wait()


def finish(place, parts, main):
    pairs, rows, block = main.shape
    vmem = pl.BlockSpec(memory_space=pltpu.VMEM)
    return pl.pallas_call(
        finish_kernel,
        out_shape=jax.ShapeDtypeStruct((pairs + YLO * BLOCKS, rows, block), BF16),
        in_specs=[pl.BlockSpec(memory_space=pltpu.SMEM)] + [vmem] * (BLOCKS + 1),
        out_specs=HBM,
        scratch_shapes=[pltpu.SemaphoreType.DMA((BLOCKS * YLO + 1,))],
        compiler_params=SMALL,
        name="finish",
    )(place, *parts, main)


def rotate(index, parts, axes):
    out = [parts[0]]
    for part, d in zip(parts[1:], ORDER[index][1:]):
        out.append(lax.ppermute(part, axes, [(i, (i + d) % BLOCKS) for i in range(BLOCKS)]))
    return out


def swap(value, axis):
    return lax.ppermute(value, axis, [(0, 1), (1, 0)])


def per_device(half_panel, orbitals):
    pairs, rows, block = half_panel.shape
    side_pairs = Z * YLO
    main_pairs = pairs - side_pairs
    depth = main_pairs // (COLS * YLO)
    z, ylo, core = lax.axis_index("z"), lax.axis_index("ylo"), lax.axis_index("core")
    c = lax.axis_index("x") * YHI + lax.axis_index("yhi")

    place = jnp.stack([z, ylo, core, c]).astype(jnp.int32)

    def deep(value):
        return value.reshape(BLOCKS, YLO, 1, rows, block)

    together = lax.optimization_barrier

    with jax.named_scope("side_in"):
        side = half_panel[main_pairs:].reshape(YLO, Z, rows, block)
        got = swap(lax.dynamic_index_in_dim(side, 1 - ylo, 0, keepdims=False), "ylo")
        keep = lax.dynamic_index_in_dim(side, ylo, 0, keepdims=False)
    picked, own = pick_columns(place, orbitals, half_panel, main_pairs)
    own = own.reshape(COLS * YLO, depth, rows, block)
    own, got, keep, picked = together((own, got, keep, picked))

    with jax.named_scope("panels_in"):
        own = lax.all_to_all(own, PLANE, 0, 0, tiled=True)
        own = own.reshape(COLS, YLO, depth, rows, block)
    with jax.named_scope("side_in"):
        parts = rotate(AT_Z, join_and_spread(place, keep, got), "z")
        side_own = collect(AT_Z, place, parts)
    own, side_own, picked = together((own, side_own, picked))

    with jax.named_scope("mirror"):
        own_low = lax.all_to_all(own, "z", 0, 0, tiled=True)
    other = swap(own, "core")
    with jax.named_scope("side_mirror"):
        side_other = swap(side_own, "core")
        parts = rotate(AT_C, spread(AT_C, place, side_own), SIDE)
        side_low = collect(AT_C, place, parts)
        side_other_low = swap(side_low, "core")
        side_partial = first_half(
            AT_C, place, deep(side_low), deep(side_other_low), deep(side_own), deep(side_other),
            picked, [(1, block, block // CORE)] * BLOCKS, "first_half_side"
        )
    own_low, other, side_partial = together((own_low, other, side_partial))

    other_low = swap(own_low, "core")
    partial_value, = first_half(
        AT_Z, place, own, other, own_low, other_low, picked,
        [(BLOCKS, depth, block, block // CORE)], "first_half"
    )
    with jax.named_scope("partial"):
        partial_value = lax.all_to_all(partial_value, "z", 0, 0, tiled=True)
    with jax.named_scope("side_partial"):
        parts = rotate(AT_C, side_partial, SIDE)
        side_partial = collect(AT_C, place, parts)
        side_partial_other = swap(side_partial, "core")
        keep, send = second_half_side(place, side_partial, side_partial_other, picked)
    got = swap(send, "ylo")
    partial_value, keep = together((partial_value, keep))

    result = second_half(partial_value, orbitals)
    result, got, keep = together((result, got, keep))

    with jax.named_scope("panels_out"):
        result = result.reshape(COLS * YLO, depth, rows, block)
        result = lax.all_to_all(result, PLANE, 0, 0, tiled=True)
        result = result.reshape(main_pairs, rows, block)
    with jax.named_scope("side_out"):
        parts = rotate(AT_Z, join_and_spread(place, keep, got), "z")
    return finish(place, parts, result)


def solution(mesh):
    fine = Mesh(mesh.devices.reshape(Z, YLO, CORE, X, YHI), ("z", "ylo", "core", "x", "yhi"))
    spec = P(None, ("z", "ylo", "core"), ("x", "yhi"))
    return jax.shard_map(
        per_device, mesh=fine, in_specs=(spec, P()), out_specs=spec, check_vma=False
    )
```

```python
import functools

import jax
import jax.numpy as jnp
from jax import lax
from jax.experimental import pallas as pl
from jax.experimental.pallas import tpu as pltpu
from jax.sharding import Mesh, PartitionSpec as P

Z, YLO, CORE, X, YHI = 8, 2, 2, 4, 2
COLS = X * YHI
BLOCKS = 8
PLANE = ("x", "yhi", "ylo")
SIDE = ("x", "yhi")
AT_Z, AT_YLO, AT_CORE, AT_C = range(4)
F32 = jnp.float32
BF16 = jnp.bfloat16
PARAMS = pltpu.CompilerParams(vmem_limit_bytes=24 * 2**20)
SMALL = pltpu.CompilerParams(vmem_limit_bytes=8 * 2**20)


ORDER = {AT_Z: (0, 4, 3, 5, 2, 6, 1, 7), AT_C: (0, 3, 5, 1, 7, 4, 2, 6)}
EARLY = 6
STEPS = 4
HBM = pl.BlockSpec(memory_space=pltpu.HBM)


def in_hbm(value):
    return pltpu.with_memory_space_constraint(value, pltpu.HBM)


def fetch_of(c_hbm, c_ref, sems, step):
    rows = c_ref.shape[1]
    return pltpu.make_async_copy(
        c_hbm.at[pl.ds(pl.multiple_of(step * rows, rows), rows)], c_ref.at[step], sems.at[step]
    )


def steps(c_hbm, c_ref, sems, body):
    def start(step, carry):
        fetch_of(c_hbm, c_ref, sems, step).start()
        return carry

    def run(step, carry):
        body(step)
        return carry

    lax.fori_loop(0, STEPS, start, 0)
    lax.fori_loop(0, STEPS, run, 0)


def fetch_scratch(value):
    size, width = value.shape
    return [pltpu.VMEM((STEPS, size // STEPS, width), BF16), pltpu.SemaphoreType.DMA((STEPS,))]


def columns_of(c_hbm, c_ref, sems, step):
    width = c_ref.shape[2]
    return pltpu.make_async_copy(
        c_hbm.at[:, pl.ds(pl.multiple_of(step * width, width), width)], c_ref.at[step], sems.at[step]
    )


def fetch_columns(c_hbm, c_ref, sems):
    def start(step, carry):
        columns_of(c_hbm, c_ref, sems, step).start()
        return carry

    lax.fori_loop(0, STEPS, start, 0)


def products(left, c_hbm, c_ref, sems, store):
    def run(step, carry):
        columns_of(c_hbm, c_ref, sems, step).wait()
        store(step, jnp.dot(left[...], c_ref[step], preferred_element_type=F32).astype(BF16))
        return carry

    lax.fori_loop(0, STEPS, run, 0)


def column_scratch(value):
    size, width = value.shape
    return [pltpu.VMEM((STEPS, size, width // STEPS), BF16), pltpu.SemaphoreType.DMA((STEPS,))]


def set_identity(eye):
    row = lax.broadcasted_iota(jnp.int32, eye.shape, 0)
    column = lax.broadcasted_iota(jnp.int32, eye.shape, 1)
    eye[...] = (row == column).astype(F32).astype(BF16)


def transposed(block, eye):
    size = block.shape[1]
    return lax.dot_general(
        eye[:size, :size], block, (((1,), (1,)), ((), ())), preferred_element_type=F32
    ).astype(BF16)


def pick_kernel(place, c_hbm, panel_hbm, out_hbm, main_hbm, c_ref, sems, chosen, out_sems, panel, main_sems):
    main_in = pltpu.make_async_copy(panel_hbm.at[pl.ds(0, main_hbm.shape[0])], panel, main_sems.at[0])
    main_out = pltpu.make_async_copy(panel, main_hbm, main_sems.at[1])
    main_in.start()
    block = c_hbm.shape[1] // BLOCKS
    lanes = block // CORE
    half = lanes // 2
    rows = c_hbm.shape[0] // STEPS

    def store_of(step):
        return pltpu.make_async_copy(
            chosen.at[step], out_hbm.at[pl.ds(pl.multiple_of(step * rows, rows), rows)], out_sems.at[step]
        )

    def choose(step):
        fetch_of(c_hbm, c_ref, sems, step).wait()
        for core in range(CORE):
            @pl.when(place[AT_CORE] == core)
            def _():
                for b in range(BLOCKS):
                    pieces = []
                    for y in range(YLO):
                        tile = c_ref[step, :, b * block + y * lanes:b * block + (y + 1) * lanes]
                        pieces.append(tile[:, core * half:(core + 1) * half])
                    chosen[step, :, b * lanes:(b + 1) * lanes] = jnp.concatenate(pieces, axis=1)
        store_of(step).start()

    def finish_store(step, carry):
        store_of(step).wait()
        return carry

    steps(c_hbm, c_ref, sems, choose)
    main_in.wait()
    main_out.start()
    lax.fori_loop(0, STEPS, finish_store, 0)
    main_out.wait()


def pick_columns(place, orbitals, half_panel, main_pairs):
    size = orbitals.shape[0]
    width = size // CORE
    return pl.pallas_call(
        pick_kernel,
        out_shape=[pltpu.HBM((size, width), BF16), pltpu.HBM((main_pairs,) + half_panel.shape[1:], BF16)],
        in_specs=[pl.BlockSpec(memory_space=pltpu.SMEM), HBM, HBM],
        out_specs=[HBM, HBM],
        scratch_shapes=fetch_scratch(orbitals) + [
            pltpu.VMEM((STEPS, size // STEPS, width), BF16), pltpu.SemaphoreType.DMA((STEPS,)),
            pltpu.VMEM((main_pairs,) + half_panel.shape[1:], BF16), pltpu.SemaphoreType.DMA((2,))],
        compiler_params=PARAMS,
        name="pick_columns",
    )(place, in_hbm(orbitals), in_hbm(half_panel))


def first_kernel(index, place, direct, direct_other, turned, turned_other, c_hbm, *rest):
    t_refs = rest[:-6]
    c_ref, sems, sym, turn, final, eye = rest[-6:]
    _, _, depth, rows, block = direct.shape
    mine, core = place[index], place[AT_CORE]
    fetch_columns(c_hbm, c_ref, sems)
    set_identity(eye)

    def build(b, carry):
        cols = pl.ds(pl.multiple_of(b * block, block), block)

        @pl.when(b >= mine)
        def _():
            for k in range(depth):
                for y in range(YLO):
                    at = k * block + y * CORE * rows
                    sym[pl.ds(pl.multiple_of(at + core * rows, rows), rows), cols] = direct[b, y, k]
                    sym[pl.ds(pl.multiple_of(at + (1 - core) * rows, rows), rows), cols] = direct_other[b, y, k]

        @pl.when(b == mine)
        def _():
            row = lax.broadcasted_iota(jnp.int32, (block, block), 0)
            column = lax.broadcasted_iota(jnp.int32, (block, block), 1)
            for k in range(depth):
                upper = sym[k * block:(k + 1) * block, cols]
                sym[k * block:(k + 1) * block, cols] = jnp.where(row <= column, upper, transposed(upper, eye))

        @pl.when(b < mine)
        def _():
            for k in range(depth):
                for y in range(YLO):
                    at = k * block + y * CORE * rows
                    turn[pl.ds(pl.multiple_of(at + core * rows, rows), rows), :] = turned[b, y, k]
                    turn[pl.ds(pl.multiple_of(at + (1 - core) * rows, rows), rows), :] = turned_other[b, y, k]
            for k in range(depth):
                sym[k * block:(k + 1) * block, cols] = transposed(turn[k * block:(k + 1) * block], eye)

        return carry

    def store(step, product):
        width = product.shape[1]
        if len(t_refs) > 1:
            final[:, pl.ds(pl.multiple_of(step * width, width), width)] = product
        else:
            lanes = t_refs[0].shape[3]
            per_step = width // lanes
            for u in range(per_step):
                for k in range(depth):
                    t_refs[0][step * per_step + u, k] = product[k * block:(k + 1) * block, u * lanes:(u + 1) * lanes]

    lax.fori_loop(0, BLOCKS, build, 0)
    products(sym, c_hbm, c_ref, sems, store)
    if len(t_refs) > 1:
        lanes = t_refs[0].shape[2]
        for d in range(BLOCKS):
            part = (mine + ORDER[index][d]) % BLOCKS
            t_refs[d][0] = final[:, pl.ds(pl.multiple_of(part * lanes, lanes), lanes)]


def first_half(index, place, direct, direct_other, turned, turned_other, picked, outs, name):
    _, _, depth, rows, block = direct.shape
    size, width = picked.shape
    vmem = pl.BlockSpec(memory_space=pltpu.VMEM)
    return pl.pallas_call(
        functools.partial(first_kernel, index),
        out_shape=[jax.ShapeDtypeStruct(out, BF16) for out in outs],
        in_specs=[pl.BlockSpec(memory_space=pltpu.SMEM), vmem, vmem, vmem, vmem, HBM],
        out_specs=[vmem] * len(outs),
        scratch_shapes=column_scratch(picked) + [
            pltpu.VMEM((depth * block, size), BF16),
            pltpu.VMEM((depth * block, block), BF16),
            pltpu.VMEM((depth * block, width), BF16),
            pltpu.VMEM((block, block), BF16)],
        compiler_params=PARAMS,
        name=name,
    )(place, direct, direct_other, turned, turned_other, in_hbm(picked))


def second_kernel(t_ref, c_hbm, out_ref, c_ref, sems, left, eye):
    count, depth, block, lanes = t_ref.shape
    rows = lanes // YLO
    fetch_columns(c_hbm, c_ref, sems)
    set_identity(eye)

    def build(b, carry):
        for k in range(depth):
            left[k * lanes:(k + 1) * lanes, pl.ds(pl.multiple_of(b * block, block), block)] = transposed(t_ref[b, k], eye)
        return carry

    def store(step, product):
        per_step = COLS // STEPS
        for u in range(per_step):
            for y in range(YLO):
                for k in range(depth):
                    at = k * lanes + y * rows
                    out_ref[step * per_step + u, y, k] = product[at:at + rows, u * block:(u + 1) * block]

    lax.fori_loop(0, count, build, 0)
    products(left, c_hbm, c_ref, sems, store)


def second_half(partial_value, orbitals):
    _, depth, block, lanes = partial_value.shape
    size = orbitals.shape[0]
    vmem = pl.BlockSpec(memory_space=pltpu.VMEM)
    return pl.pallas_call(
        second_kernel,
        out_shape=jax.ShapeDtypeStruct((COLS, YLO, depth, lanes // YLO, block), BF16),
        in_specs=[vmem, HBM],
        out_specs=vmem,
        scratch_shapes=column_scratch(orbitals) + [
            pltpu.VMEM((depth * lanes, size), BF16),
            pltpu.VMEM((lanes, lanes), BF16)],
        compiler_params=PARAMS,
        name="second_half",
    )(partial_value, in_hbm(orbitals))


def second_side_kernel(place, t_ref, other_ref, c_hbm, keep, send, c_ref, sems, left, final, eye):
    count, _, block, lanes = t_ref.shape
    rows = lanes // YLO
    ylo, core = place[AT_YLO], place[AT_CORE]
    fetch_columns(c_hbm, c_ref, sems)
    set_identity(eye)

    def build(b, carry):
        cols = pl.ds(pl.multiple_of(b * block, block), block)
        own = transposed(t_ref[b, 0], eye)
        other = transposed(other_ref[b, 0], eye)
        for y in range(YLO):
            at = y * CORE * rows
            left[pl.ds(pl.multiple_of(at + core * rows, rows), rows), cols] = own[y * rows:(y + 1) * rows]
            left[pl.ds(pl.multiple_of(at + (1 - core) * rows, rows), rows), cols] = other[y * rows:(y + 1) * rows]
        return carry

    def store(step, product):
        width = product.shape[1]
        final[pl.ds(pl.multiple_of(step * width, width), width)] = transposed(product, eye)

    lax.fori_loop(0, count, build, 0)
    products(left, c_hbm, c_ref, sems, store)
    for z in range(Z):
        at = z * YLO * rows
        keep[z] = final[pl.ds(pl.multiple_of(at + ylo * rows, rows), rows)]
        send[z] = final[pl.ds(pl.multiple_of(at + (1 - ylo) * rows, rows), rows)]


def second_half_side(place, own, other, picked):
    _, _, block, lanes = own.shape
    size, width = picked.shape
    vmem = pl.BlockSpec(memory_space=pltpu.VMEM)
    out = jax.ShapeDtypeStruct((Z, lanes // YLO, block), BF16)
    return pl.pallas_call(
        second_side_kernel,
        out_shape=[out, out],
        in_specs=[pl.BlockSpec(memory_space=pltpu.SMEM), vmem, vmem, HBM],
        out_specs=[vmem, vmem],
        scratch_shapes=column_scratch(picked) + [
            pltpu.VMEM((block, size), BF16),
            pltpu.VMEM((width, block), BF16),
            pltpu.VMEM((block, block), BF16)],
        compiler_params=PARAMS,
        name="second_half_side",
    )(place, own, other, in_hbm(picked))


def spread_kernel(index, place, x_ref, *out_refs):
    for d in range(BLOCKS):
        out_refs[d][...] = x_ref[(place[index] + ORDER[index][d]) % BLOCKS]


def spread(index, place, value):
    vmem = pl.BlockSpec(memory_space=pltpu.VMEM)
    return pl.pallas_call(
        functools.partial(spread_kernel, index),
        out_shape=[jax.ShapeDtypeStruct(value.shape[1:], BF16)] * BLOCKS,
        in_specs=[pl.BlockSpec(memory_space=pltpu.SMEM), vmem],
        out_specs=[vmem] * BLOCKS,
        compiler_params=SMALL,
        name="spread",
    )(place, value)


def join_kernel(place, keep, got, *out_refs):
    z, ylo = place[AT_Z], place[AT_YLO]
    for d in range(BLOCKS):
        out_refs[d][ylo] = keep[(z + ORDER[AT_Z][d]) % BLOCKS]
        out_refs[d][1 - ylo] = got[(z + ORDER[AT_Z][d]) % BLOCKS]


def join_and_spread(place, keep, got):
    vmem = pl.BlockSpec(memory_space=pltpu.VMEM)
    return pl.pallas_call(
        join_kernel,
        out_shape=[jax.ShapeDtypeStruct((YLO,) + keep.shape[1:], BF16)] * BLOCKS,
        in_specs=[pl.BlockSpec(memory_space=pltpu.SMEM), vmem, vmem],
        out_specs=[vmem] * BLOCKS,
        compiler_params=SMALL,
        name="join_and_spread",
    )(place, keep, got)


def collect_kernel(index, place, *refs):
    out_ref = refs[BLOCKS]
    for d in range(BLOCKS):
        out_ref[(place[index] + BLOCKS - ORDER[index][d]) % BLOCKS] = refs[d][...]


def collect(index, place, parts):
    vmem = pl.BlockSpec(memory_space=pltpu.VMEM)
    return pl.pallas_call(
        functools.partial(collect_kernel, index),
        out_shape=jax.ShapeDtypeStruct((BLOCKS,) + parts[0].shape, BF16),
        in_specs=[pl.BlockSpec(memory_space=pltpu.SMEM)] + [vmem] * BLOCKS,
        out_specs=vmem,
        compiler_params=SMALL,
        name="collect",
    )(place, *parts)


def finish_kernel(place, *refs):
    main_ref, out_hbm, sems = refs[BLOCKS:]
    main = main_ref.shape[0]
    copies = [pltpu.make_async_copy(main_ref, out_hbm.at[pl.ds(0, main)], sems.at[BLOCKS * YLO])]
    for d in range(BLOCKS):
        for y in range(YLO):
            to = main + y * BLOCKS + (place[AT_Z] + BLOCKS - ORDER[AT_Z][d]) % BLOCKS
            copies.append(pltpu.make_async_copy(refs[d].at[y], out_hbm.at[to], sems.at[d * YLO + y]))
    for copy in copies:
        copy.start()
    for copy in copies:
        copy.wait()


def finish(place, parts, main):
    pairs, rows, block = main.shape
    vmem = pl.BlockSpec(memory_space=pltpu.VMEM)
    return pl.pallas_call(
        finish_kernel,
        out_shape=jax.ShapeDtypeStruct((pairs + YLO * BLOCKS, rows, block), BF16),
        in_specs=[pl.BlockSpec(memory_space=pltpu.SMEM)] + [vmem] * (BLOCKS + 1),
        out_specs=HBM,
        scratch_shapes=[pltpu.SemaphoreType.DMA((BLOCKS * YLO + 1,))],
        compiler_params=SMALL,
        name="finish",
    )(place, *parts, main)


def rotate(index, parts, axes):
    out = [parts[0]]
    for part, d in zip(parts[1:], ORDER[index][1:]):
        out.append(lax.ppermute(part, axes, [(i, (i + d) % BLOCKS) for i in range(BLOCKS)]))
    return out


def swap(value, axis):
    return lax.ppermute(value, axis, [(0, 1), (1, 0)])


def per_device(half_panel, orbitals):
    pairs, rows, block = half_panel.shape
    side_pairs = Z * YLO
    main_pairs = pairs - side_pairs
    depth = main_pairs // (COLS * YLO)
    z, ylo, core = lax.axis_index("z"), lax.axis_index("ylo"), lax.axis_index("core")
    c = lax.axis_index("x") * YHI + lax.axis_index("yhi")

    place = jnp.stack([z, ylo, core, c]).astype(jnp.int32)

    def deep(value):
        return value.reshape(BLOCKS, YLO, 1, rows, block)

    together = lax.optimization_barrier

    with jax.named_scope("side_in"):
        side = half_panel[main_pairs:].reshape(YLO, Z, rows, block)
        got = swap(lax.dynamic_index_in_dim(side, 1 - ylo, 0, keepdims=False), "ylo")
        keep = lax.dynamic_index_in_dim(side, ylo, 0, keepdims=False)
    picked, own = pick_columns(place, orbitals, half_panel, main_pairs)
    own = own.reshape(COLS * YLO, depth, rows, block)
    own, got, keep, picked = together((own, got, keep, picked))

    with jax.named_scope("panels_in"):
        own = lax.all_to_all(own, PLANE, 0, 0, tiled=True)
        own = own.reshape(COLS, YLO, depth, rows, block)
    with jax.named_scope("side_in"):
        parts = rotate(AT_Z, join_and_spread(place, keep, got), "z")
    own, early, picked = together((own, parts[:EARLY], picked))
    side_own = collect(AT_Z, place, list(early) + parts[EARLY:])

    with jax.named_scope("mirror"):
        own_low = lax.all_to_all(own, "z", 0, 0, tiled=True)
    other = swap(own, "core")
    with jax.named_scope("side_mirror"):
        side_other = swap(side_own, "core")
        parts = rotate(AT_C, spread(AT_C, place, side_own), SIDE)
        side_low = collect(AT_C, place, parts)
        side_other_low = swap(side_low, "core")
        side_partial = first_half(
            AT_C, place, deep(side_low), deep(side_other_low), deep(side_own), deep(side_other),
            picked, [(1, block, block // CORE)] * BLOCKS, "first_half_side"
        )
    own_low, other, side_partial = together((own_low, other, side_partial))

    other_low = swap(own_low, "core")
    partial_value, = first_half(
        AT_Z, place, own, other, own_low, other_low, picked,
        [(BLOCKS, depth, block, block // CORE)], "first_half"
    )
    with jax.named_scope("partial"):
        partial_value = lax.all_to_all(partial_value, "z", 0, 0, tiled=True)
    with jax.named_scope("side_partial"):
        parts = rotate(AT_C, side_partial, SIDE)
        side_partial = collect(AT_C, place, parts)
        side_partial_other = swap(side_partial, "core")
        keep, send = second_half_side(place, side_partial, side_partial_other, picked)
    got = swap(send, "ylo")
    partial_value, keep = together((partial_value, keep))

    result = second_half(partial_value, orbitals)
    result, got, keep = together((result, got, keep))

    with jax.named_scope("panels_out"):
        result = result.reshape(COLS * YLO, depth, rows, block)
        result = lax.all_to_all(result, PLANE, 0, 0, tiled=True)
        result = result.reshape(main_pairs, rows, block)
    with jax.named_scope("side_out"):
        parts = rotate(AT_Z, join_and_spread(place, keep, got), "z")
    return finish(place, parts, result)


def solution(mesh):
    fine = Mesh(mesh.devices.reshape(Z, YLO, CORE, X, YHI), ("z", "ylo", "core", "x", "yhi"))
    spec = P(None, ("z", "ylo", "core"), ("x", "yhi"))
    return jax.shard_map(
        per_device, mesh=fine, in_specs=(spec, P()), out_specs=spec, check_vma=False
    )
```

```python
import functools

import jax
import jax.numpy as jnp
from jax import lax
from jax.experimental import pallas as pl
from jax.experimental.pallas import tpu as pltpu
from jax.sharding import Mesh, PartitionSpec as P

Z, YLO, CORE, X, YHI = 8, 2, 2, 4, 2
COLS = X * YHI
BLOCKS = 8
PLANE = ("x", "yhi", "ylo")
SIDE = ("x", "yhi")
AT_Z, AT_YLO, AT_CORE, AT_C = range(4)
F32 = jnp.float32
BF16 = jnp.bfloat16
PARAMS = pltpu.CompilerParams(vmem_limit_bytes=24 * 2**20)
SMALL = pltpu.CompilerParams(vmem_limit_bytes=8 * 2**20)


ORDER = {AT_Z: (0, 4, 3, 5, 2, 6, 1, 7), AT_C: (0, 3, 5, 1, 7, 4, 2, 6)}
STEPS = 4
HBM = pl.BlockSpec(memory_space=pltpu.HBM)


def in_hbm(value):
    return pltpu.with_memory_space_constraint(value, pltpu.HBM)


def fetch_of(c_hbm, c_ref, sems, step):
    rows = c_ref.shape[1]
    return pltpu.make_async_copy(
        c_hbm.at[pl.ds(pl.multiple_of(step * rows, rows), rows)], c_ref.at[step], sems.at[step]
    )


def steps(c_hbm, c_ref, sems, body):
    def start(step, carry):
        fetch_of(c_hbm, c_ref, sems, step).start()
        return carry

    def run(step, carry):
        body(step)
        return carry

    lax.fori_loop(0, STEPS, start, 0)
    lax.fori_loop(0, STEPS, run, 0)


def fetch_scratch(value):
    size, width = value.shape
    return [pltpu.VMEM((STEPS, size // STEPS, width), BF16), pltpu.SemaphoreType.DMA((STEPS,))]


def columns_of(c_hbm, c_ref, sems, step):
    width = c_ref.shape[2]
    return pltpu.make_async_copy(
        c_hbm.at[:, pl.ds(pl.multiple_of(step * width, width), width)], c_ref.at[step], sems.at[step]
    )


def fetch_columns(c_hbm, c_ref, sems):
    def start(step, carry):
        columns_of(c_hbm, c_ref, sems, step).start()
        return carry

    lax.fori_loop(0, STEPS, start, 0)


def products(left, c_hbm, c_ref, sems, store):
    def run(step, carry):
        columns_of(c_hbm, c_ref, sems, step).wait()
        store(step, jnp.dot(left[...], c_ref[step], preferred_element_type=F32).astype(BF16))
        return carry

    lax.fori_loop(0, STEPS, run, 0)


def column_scratch(value):
    size, width = value.shape
    return [pltpu.VMEM((STEPS, size, width // STEPS), BF16), pltpu.SemaphoreType.DMA((STEPS,))]


def set_identity(eye):
    row = lax.broadcasted_iota(jnp.int32, eye.shape, 0)
    column = lax.broadcasted_iota(jnp.int32, eye.shape, 1)
    eye[...] = (row == column).astype(F32).astype(BF16)


def transposed(block, eye):
    size = block.shape[1]
    return lax.dot_general(
        eye[:size, :size], block, (((1,), (1,)), ((), ())), preferred_element_type=F32
    ).astype(BF16)


def pick_kernel(place, c_hbm, panel_hbm, out_hbm, main_hbm, c_ref, sems, chosen, out_sems, panel, main_sems):
    main_in = pltpu.make_async_copy(panel_hbm.at[pl.ds(0, main_hbm.shape[0])], panel, main_sems.at[0])
    main_out = pltpu.make_async_copy(panel, main_hbm, main_sems.at[1])
    main_in.start()
    block = c_hbm.shape[1] // BLOCKS
    lanes = block // CORE
    half = lanes // 2
    rows = c_hbm.shape[0] // STEPS

    def store_of(step):
        return pltpu.make_async_copy(
            chosen.at[step], out_hbm.at[pl.ds(pl.multiple_of(step * rows, rows), rows)], out_sems.at[step]
        )

    def choose(step):
        fetch_of(c_hbm, c_ref, sems, step).wait()
        for core in range(CORE):
            @pl.when(place[AT_CORE] == core)
            def _():
                for b in range(BLOCKS):
                    pieces = []
                    for y in range(YLO):
                        tile = c_ref[step, :, b * block + y * lanes:b * block + (y + 1) * lanes]
                        pieces.append(tile[:, core * half:(core + 1) * half])
                    chosen[step, :, b * lanes:(b + 1) * lanes] = jnp.concatenate(pieces, axis=1)
        store_of(step).start()

    def finish_store(step, carry):
        store_of(step).wait()
        return carry

    steps(c_hbm, c_ref, sems, choose)
    main_in.wait()
    main_out.start()
    lax.fori_loop(0, STEPS, finish_store, 0)
    main_out.wait()


def pick_columns(place, orbitals, half_panel, main_pairs):
    size = orbitals.shape[0]
    width = size // CORE
    return pl.pallas_call(
        pick_kernel,
        out_shape=[pltpu.HBM((size, width), BF16), pltpu.HBM((main_pairs,) + half_panel.shape[1:], BF16)],
        in_specs=[pl.BlockSpec(memory_space=pltpu.SMEM), HBM, HBM],
        out_specs=[HBM, HBM],
        scratch_shapes=fetch_scratch(orbitals) + [
            pltpu.VMEM((STEPS, size // STEPS, width), BF16), pltpu.SemaphoreType.DMA((STEPS,)),
            pltpu.VMEM((main_pairs,) + half_panel.shape[1:], BF16), pltpu.SemaphoreType.DMA((2,))],
        compiler_params=PARAMS,
        name="pick_columns",
    )(place, in_hbm(orbitals), in_hbm(half_panel))


def first_kernel(index, place, direct, direct_other, turned, turned_other, c_hbm, *rest):
    t_refs = rest[:-6]
    c_ref, sems, sym, turn, final, eye = rest[-6:]
    _, _, depth, rows, block = direct.shape
    mine, core = place[index], place[AT_CORE]
    fetch_columns(c_hbm, c_ref, sems)
    set_identity(eye)

    def build(b, carry):
        cols = pl.ds(pl.multiple_of(b * block, block), block)

        @pl.when(b >= mine)
        def _():
            for k in range(depth):
                for y in range(YLO):
                    at = k * block + y * CORE * rows
                    sym[pl.ds(pl.multiple_of(at + core * rows, rows), rows), cols] = direct[b, y, k]
                    sym[pl.ds(pl.multiple_of(at + (1 - core) * rows, rows), rows), cols] = direct_other[b, y, k]

        @pl.when(b == mine)
        def _():
            row = lax.broadcasted_iota(jnp.int32, (block, block), 0)
            column = lax.broadcasted_iota(jnp.int32, (block, block), 1)
            for k in range(depth):
                upper = sym[k * block:(k + 1) * block, cols]
                sym[k * block:(k + 1) * block, cols] = jnp.where(row <= column, upper, transposed(upper, eye))

        @pl.when(b < mine)
        def _():
            for k in range(depth):
                for y in range(YLO):
                    at = k * block + y * CORE * rows
                    turn[pl.ds(pl.multiple_of(at + core * rows, rows), rows), :] = turned[b, y, k]
                    turn[pl.ds(pl.multiple_of(at + (1 - core) * rows, rows), rows), :] = turned_other[b, y, k]
            for k in range(depth):
                sym[k * block:(k + 1) * block, cols] = transposed(turn[k * block:(k + 1) * block], eye)

        return carry

    def store(step, product):
        width = product.shape[1]
        if len(t_refs) > 1:
            final[:, pl.ds(pl.multiple_of(step * width, width), width)] = product
        else:
            lanes = t_refs[0].shape[3]
            per_step = width // lanes
            for u in range(per_step):
                for k in range(depth):
                    t_refs[0][step * per_step + u, k] = product[k * block:(k + 1) * block, u * lanes:(u + 1) * lanes]

    lax.fori_loop(0, BLOCKS, build, 0)
    products(sym, c_hbm, c_ref, sems, store)
    if len(t_refs) > 1:
        lanes = t_refs[0].shape[2]
        for d in range(BLOCKS):
            part = (mine + ORDER[index][d]) % BLOCKS
            t_refs[d][0] = final[:, pl.ds(pl.multiple_of(part * lanes, lanes), lanes)]


def first_half(index, place, direct, direct_other, turned, turned_other, picked, outs, name):
    _, _, depth, rows, block = direct.shape
    size, width = picked.shape
    vmem = pl.BlockSpec(memory_space=pltpu.VMEM)
    return pl.pallas_call(
        functools.partial(first_kernel, index),
        out_shape=[jax.ShapeDtypeStruct(out, BF16) for out in outs],
        in_specs=[pl.BlockSpec(memory_space=pltpu.SMEM), vmem, vmem, vmem, vmem, HBM],
        out_specs=[vmem] * len(outs),
        scratch_shapes=column_scratch(picked) + [
            pltpu.VMEM((depth * block, size), BF16),
            pltpu.VMEM((depth * block, block), BF16),
            pltpu.VMEM((depth * block, width), BF16),
            pltpu.VMEM((block, block), BF16)],
        compiler_params=PARAMS,
        name=name,
    )(place, direct, direct_other, turned, turned_other, in_hbm(picked))


def second_kernel(t_ref, c_hbm, out_ref, c_ref, sems, left, eye):
    count, depth, block, lanes = t_ref.shape
    rows = lanes // YLO
    fetch_columns(c_hbm, c_ref, sems)
    set_identity(eye)

    def build(b, carry):
        for k in range(depth):
            left[k * lanes:(k + 1) * lanes, pl.ds(pl.multiple_of(b * block, block), block)] = transposed(t_ref[b, k], eye)
        return carry

    def store(step, product):
        per_step = COLS // STEPS
        for u in range(per_step):
            for y in range(YLO):
                for k in range(depth):
                    at = k * lanes + y * rows
                    out_ref[step * per_step + u, y, k] = product[at:at + rows, u * block:(u + 1) * block]

    lax.fori_loop(0, count, build, 0)
    products(left, c_hbm, c_ref, sems, store)


def second_half(partial_value, orbitals):
    _, depth, block, lanes = partial_value.shape
    size = orbitals.shape[0]
    vmem = pl.BlockSpec(memory_space=pltpu.VMEM)
    return pl.pallas_call(
        second_kernel,
        out_shape=jax.ShapeDtypeStruct((COLS, YLO, depth, lanes // YLO, block), BF16),
        in_specs=[vmem, HBM],
        out_specs=vmem,
        scratch_shapes=column_scratch(orbitals) + [
            pltpu.VMEM((depth * lanes, size), BF16),
            pltpu.VMEM((lanes, lanes), BF16)],
        compiler_params=PARAMS,
        name="second_half",
    )(partial_value, in_hbm(orbitals))


def second_side_kernel(place, t_ref, other_ref, c_hbm, keep, send, c_ref, sems, left, final, eye):
    count, _, block, lanes = t_ref.shape
    rows = lanes // YLO
    ylo, core = place[AT_YLO], place[AT_CORE]
    fetch_columns(c_hbm, c_ref, sems)
    set_identity(eye)

    def build(b, carry):
        cols = pl.ds(pl.multiple_of(b * block, block), block)
        own = transposed(t_ref[b, 0], eye)
        other = transposed(other_ref[b, 0], eye)
        for y in range(YLO):
            at = y * CORE * rows
            left[pl.ds(pl.multiple_of(at + core * rows, rows), rows), cols] = own[y * rows:(y + 1) * rows]
            left[pl.ds(pl.multiple_of(at + (1 - core) * rows, rows), rows), cols] = other[y * rows:(y + 1) * rows]
        return carry

    def store(step, product):
        width = product.shape[1]
        final[pl.ds(pl.multiple_of(step * width, width), width)] = transposed(product, eye)

    lax.fori_loop(0, count, build, 0)
    products(left, c_hbm, c_ref, sems, store)
    for z in range(Z):
        at = z * YLO * rows
        keep[z] = final[pl.ds(pl.multiple_of(at + ylo * rows, rows), rows)]
        send[z] = final[pl.ds(pl.multiple_of(at + (1 - ylo) * rows, rows), rows)]


def second_half_side(place, own, other, picked):
    _, _, block, lanes = own.shape
    size, width = picked.shape
    vmem = pl.BlockSpec(memory_space=pltpu.VMEM)
    out = jax.ShapeDtypeStruct((Z, lanes // YLO, block), BF16)
    return pl.pallas_call(
        second_side_kernel,
        out_shape=[out, out],
        in_specs=[pl.BlockSpec(memory_space=pltpu.SMEM), vmem, vmem, HBM],
        out_specs=[vmem, vmem],
        scratch_shapes=column_scratch(picked) + [
            pltpu.VMEM((block, size), BF16),
            pltpu.VMEM((width, block), BF16),
            pltpu.VMEM((block, block), BF16)],
        compiler_params=PARAMS,
        name="second_half_side",
    )(place, own, other, in_hbm(picked))


def spread_kernel(index, place, x_ref, *out_refs):
    for d in range(BLOCKS):
        out_refs[d][...] = x_ref[(place[index] + ORDER[index][d]) % BLOCKS]


def spread(index, place, value):
    vmem = pl.BlockSpec(memory_space=pltpu.VMEM)
    return pl.pallas_call(
        functools.partial(spread_kernel, index),
        out_shape=[jax.ShapeDtypeStruct(value.shape[1:], BF16)] * BLOCKS,
        in_specs=[pl.BlockSpec(memory_space=pltpu.SMEM), vmem],
        out_specs=[vmem] * BLOCKS,
        compiler_params=SMALL,
        name="spread",
    )(place, value)


def join_kernel(place, keep, got, *out_refs):
    z, ylo = place[AT_Z], place[AT_YLO]
    for d in range(BLOCKS):
        out_refs[d][ylo] = keep[(z + ORDER[AT_Z][d]) % BLOCKS]
        out_refs[d][1 - ylo] = got[(z + ORDER[AT_Z][d]) % BLOCKS]


def join_and_spread(place, keep, got):
    vmem = pl.BlockSpec(memory_space=pltpu.VMEM)
    return pl.pallas_call(
        join_kernel,
        out_shape=[jax.ShapeDtypeStruct((YLO,) + keep.shape[1:], BF16)] * BLOCKS,
        in_specs=[pl.BlockSpec(memory_space=pltpu.SMEM), vmem, vmem],
        out_specs=[vmem] * BLOCKS,
        compiler_params=SMALL,
        name="join_and_spread",
    )(place, keep, got)


def collect_kernel(index, place, *refs):
    out_ref = refs[BLOCKS]
    for d in range(BLOCKS):
        out_ref[(place[index] + BLOCKS - ORDER[index][d]) % BLOCKS] = refs[d][...]


def collect(index, place, parts):
    vmem = pl.BlockSpec(memory_space=pltpu.VMEM)
    return pl.pallas_call(
        functools.partial(collect_kernel, index),
        out_shape=jax.ShapeDtypeStruct((BLOCKS,) + parts[0].shape, BF16),
        in_specs=[pl.BlockSpec(memory_space=pltpu.SMEM)] + [vmem] * BLOCKS,
        out_specs=vmem,
        compiler_params=SMALL,
        name="collect",
    )(place, *parts)


def finish_kernel(place, *refs):
    main_ref, out_hbm, sems = refs[BLOCKS:]
    main = main_ref.shape[0]
    share = main // STEPS
    copies = []
    for g in range(STEPS):
        part = pl.ds(g * share, share)
        copies.append(pltpu.make_async_copy(main_ref.at[part], out_hbm.at[part], sems.at[BLOCKS * YLO + g]))
    for d in range(BLOCKS):
        for y in range(YLO):
            to = main + y * BLOCKS + (place[AT_Z] + BLOCKS - ORDER[AT_Z][d]) % BLOCKS
            copies.append(pltpu.make_async_copy(refs[d].at[y], out_hbm.at[to], sems.at[d * YLO + y]))
    for copy in copies:
        copy.start()
    for copy in copies:
        copy.wait()


def finish(place, parts, main):
    pairs, rows, block = main.shape
    vmem = pl.BlockSpec(memory_space=pltpu.VMEM)
    return pl.pallas_call(
        finish_kernel,
        out_shape=jax.ShapeDtypeStruct((pairs + YLO * BLOCKS, rows, block), BF16),
        in_specs=[pl.BlockSpec(memory_space=pltpu.SMEM)] + [vmem] * (BLOCKS + 1),
        out_specs=HBM,
        scratch_shapes=[pltpu.SemaphoreType.DMA((BLOCKS * YLO + STEPS,))],
        compiler_params=SMALL,
        name="finish",
    )(place, *parts, main)


def rotate(index, parts, axes):
    out = [parts[0]]
    for part, d in zip(parts[1:], ORDER[index][1:]):
        out.append(lax.ppermute(part, axes, [(i, (i + d) % BLOCKS) for i in range(BLOCKS)]))
    return out


def swap(value, axis):
    return lax.ppermute(value, axis, [(0, 1), (1, 0)])


def per_device(half_panel, orbitals):
    pairs, rows, block = half_panel.shape
    side_pairs = Z * YLO
    main_pairs = pairs - side_pairs
    depth = main_pairs // (COLS * YLO)
    z, ylo, core = lax.axis_index("z"), lax.axis_index("ylo"), lax.axis_index("core")
    c = lax.axis_index("x") * YHI + lax.axis_index("yhi")

    place = jnp.stack([z, ylo, core, c]).astype(jnp.int32)

    def deep(value):
        return value.reshape(BLOCKS, YLO, 1, rows, block)

    together = lax.optimization_barrier

    with jax.named_scope("side_in"):
        side = half_panel[main_pairs:].reshape(YLO, Z, rows, block)
        got = swap(lax.dynamic_index_in_dim(side, 1 - ylo, 0, keepdims=False), "ylo")
        keep = lax.dynamic_index_in_dim(side, ylo, 0, keepdims=False)
    picked, own = pick_columns(place, orbitals, half_panel, main_pairs)
    own = own.reshape(COLS * YLO, depth, rows, block)
    own, got, keep, picked = together((own, got, keep, picked))

    with jax.named_scope("panels_in"):
        own = lax.all_to_all(own, PLANE, 0, 0, tiled=True)
        own = own.reshape(COLS, YLO, depth, rows, block)
    with jax.named_scope("side_in"):
        parts = rotate(AT_Z, join_and_spread(place, keep, got), "z")
        side_own = collect(AT_Z, place, parts)
    own, side_own, picked = together((own, side_own, picked))

    with jax.named_scope("mirror"):
        own_low = lax.all_to_all(own, "z", 0, 0, tiled=True)
    other = swap(own, "core")
    with jax.named_scope("side_mirror"):
        side_other = swap(side_own, "core")
        parts = rotate(AT_C, spread(AT_C, place, side_own), SIDE)
        side_low = collect(AT_C, place, parts)
        side_other_low = swap(side_low, "core")
        side_partial = first_half(
            AT_C, place, deep(side_low), deep(side_other_low), deep(side_own), deep(side_other),
            picked, [(1, block, block // CORE)] * BLOCKS, "first_half_side"
        )
    own_low, other, side_partial = together((own_low, other, side_partial))

    other_low = swap(own_low, "core")
    partial_value, = first_half(
        AT_Z, place, own, other, own_low, other_low, picked,
        [(BLOCKS, depth, block, block // CORE)], "first_half"
    )
    with jax.named_scope("partial"):
        partial_value = lax.all_to_all(partial_value, "z", 0, 0, tiled=True)
    with jax.named_scope("side_partial"):
        parts = rotate(AT_C, side_partial, SIDE)
        side_partial = collect(AT_C, place, parts)
        side_partial_other = swap(side_partial, "core")
        keep, send = second_half_side(place, side_partial, side_partial_other, picked)
    got = swap(send, "ylo")
    partial_value, keep = together((partial_value, keep))

    result = second_half(partial_value, orbitals)
    result, got, keep = together((result, got, keep))

    with jax.named_scope("panels_out"):
        result = result.reshape(COLS * YLO, depth, rows, block)
        result = lax.all_to_all(result, PLANE, 0, 0, tiled=True)
        result = result.reshape(main_pairs, rows, block)
    with jax.named_scope("side_out"):
        parts = rotate(AT_Z, join_and_spread(place, keep, got), "z")
    return finish(place, parts, result)


def solution(mesh):
    fine = Mesh(mesh.devices.reshape(Z, YLO, CORE, X, YHI), ("z", "ylo", "core", "x", "yhi"))
    spec = P(None, ("z", "ylo", "core"), ("x", "yhi"))
    return jax.shard_map(
        per_device, mesh=fine, in_specs=(spec, P()), out_specs=spec, check_vma=False
    )
```

```python
import functools

import jax
import jax.numpy as jnp
from jax import lax
from jax.experimental import pallas as pl
from jax.experimental.pallas import tpu as pltpu
from jax.sharding import Mesh, PartitionSpec as P

Z, YLO, CORE, X, YHI = 8, 2, 2, 4, 2
COLS = X * YHI
BLOCKS = 8
PLANE = ("x", "yhi", "ylo")
SIDE = ("x", "yhi")
AT_Z, AT_YLO, AT_CORE, AT_C = range(4)
F32 = jnp.float32
BF16 = jnp.bfloat16
PARAMS = pltpu.CompilerParams(vmem_limit_bytes=24 * 2**20)
SMALL = pltpu.CompilerParams(vmem_limit_bytes=8 * 2**20)


ORDER = {AT_Z: (0, 3, 5, 4, 2, 6, 1, 7), AT_C: (0, 3, 5, 1, 7, 4, 2, 6)}
STEPS = 4
HBM = pl.BlockSpec(memory_space=pltpu.HBM)


def in_hbm(value):
    return pltpu.with_memory_space_constraint(value, pltpu.HBM)


def fetch_of(c_hbm, c_ref, sems, step):
    rows = c_ref.shape[1]
    return pltpu.make_async_copy(
        c_hbm.at[pl.ds(pl.multiple_of(step * rows, rows), rows)], c_ref.at[step], sems.at[step]
    )


def steps(c_hbm, c_ref, sems, body):
    def start(step, carry):
        fetch_of(c_hbm, c_ref, sems, step).start()
        return carry

    def run(step, carry):
        body(step)
        return carry

    lax.fori_loop(0, STEPS, start, 0)
    lax.fori_loop(0, STEPS, run, 0)


def fetch_scratch(value):
    size, width = value.shape
    return [pltpu.VMEM((STEPS, size // STEPS, width), BF16), pltpu.SemaphoreType.DMA((STEPS,))]


def columns_of(c_hbm, c_ref, sems, step):
    width = c_ref.shape[2]
    return pltpu.make_async_copy(
        c_hbm.at[:, pl.ds(pl.multiple_of(step * width, width), width)], c_ref.at[step], sems.at[step]
    )


def fetch_columns(c_hbm, c_ref, sems):
    def start(step, carry):
        columns_of(c_hbm, c_ref, sems, step).start()
        return carry

    lax.fori_loop(0, STEPS, start, 0)


def products(left, c_hbm, c_ref, sems, store):
    def run(step, carry):
        columns_of(c_hbm, c_ref, sems, step).wait()
        store(step, jnp.dot(left[...], c_ref[step], preferred_element_type=F32).astype(BF16))
        return carry

    lax.fori_loop(0, STEPS, run, 0)


def column_scratch(value):
    size, width = value.shape
    return [pltpu.VMEM((STEPS, size, width // STEPS), BF16), pltpu.SemaphoreType.DMA((STEPS,))]


def set_identity(eye):
    row = lax.broadcasted_iota(jnp.int32, eye.shape, 0)
    column = lax.broadcasted_iota(jnp.int32, eye.shape, 1)
    eye[...] = (row == column).astype(F32).astype(BF16)


def transposed(block, eye):
    size = block.shape[1]
    return lax.dot_general(
        eye[:size, :size], block, (((1,), (1,)), ((), ())), preferred_element_type=F32
    ).astype(BF16)


def pick_kernel(place, c_hbm, panel_hbm, out_hbm, main_hbm, c_ref, sems, chosen, out_sems, panel, main_sems):
    main_in = pltpu.make_async_copy(panel_hbm.at[pl.ds(0, main_hbm.shape[0])], panel, main_sems.at[0])
    main_out = pltpu.make_async_copy(panel, main_hbm, main_sems.at[1])
    main_in.start()
    block = c_hbm.shape[1] // BLOCKS
    lanes = block // CORE
    half = lanes // 2
    rows = c_hbm.shape[0] // STEPS

    def store_of(step):
        return pltpu.make_async_copy(
            chosen.at[step], out_hbm.at[pl.ds(pl.multiple_of(step * rows, rows), rows)], out_sems.at[step]
        )

    def choose(step):
        fetch_of(c_hbm, c_ref, sems, step).wait()
        for core in range(CORE):
            @pl.when(place[AT_CORE] == core)
            def _():
                for b in range(BLOCKS):
                    pieces = []
                    for y in range(YLO):
                        tile = c_ref[step, :, b * block + y * lanes:b * block + (y + 1) * lanes]
                        pieces.append(tile[:, core * half:(core + 1) * half])
                    chosen[step, :, b * lanes:(b + 1) * lanes] = jnp.concatenate(pieces, axis=1)
        store_of(step).start()

    def finish_store(step, carry):
        store_of(step).wait()
        return carry

    steps(c_hbm, c_ref, sems, choose)
    main_in.wait()
    main_out.start()
    lax.fori_loop(0, STEPS, finish_store, 0)
    main_out.wait()


def pick_columns(place, orbitals, half_panel, main_pairs):
    size = orbitals.shape[0]
    width = size // CORE
    return pl.pallas_call(
        pick_kernel,
        out_shape=[pltpu.HBM((size, width), BF16), pltpu.HBM((main_pairs,) + half_panel.shape[1:], BF16)],
        in_specs=[pl.BlockSpec(memory_space=pltpu.SMEM), HBM, HBM],
        out_specs=[HBM, HBM],
        scratch_shapes=fetch_scratch(orbitals) + [
            pltpu.VMEM((STEPS, size // STEPS, width), BF16), pltpu.SemaphoreType.DMA((STEPS,)),
            pltpu.VMEM((main_pairs,) + half_panel.shape[1:], BF16), pltpu.SemaphoreType.DMA((2,))],
        compiler_params=PARAMS,
        name="pick_columns",
    )(place, in_hbm(orbitals), in_hbm(half_panel))


def first_kernel(index, place, direct, direct_other, turned, turned_other, c_hbm, *rest):
    t_refs = rest[:-6]
    c_ref, sems, sym, turn, final, eye = rest[-6:]
    _, _, depth, rows, block = direct.shape
    mine, core = place[index], place[AT_CORE]
    fetch_columns(c_hbm, c_ref, sems)
    set_identity(eye)

    def build(b, carry):
        cols = pl.ds(pl.multiple_of(b * block, block), block)

        @pl.when(b >= mine)
        def _():
            for k in range(depth):
                for y in range(YLO):
                    at = k * block + y * CORE * rows
                    sym[pl.ds(pl.multiple_of(at + core * rows, rows), rows), cols] = direct[b, y, k]
                    sym[pl.ds(pl.multiple_of(at + (1 - core) * rows, rows), rows), cols] = direct_other[b, y, k]

        @pl.when(b == mine)
        def _():
            row = lax.broadcasted_iota(jnp.int32, (block, block), 0)
            column = lax.broadcasted_iota(jnp.int32, (block, block), 1)
            for k in range(depth):
                upper = sym[k * block:(k + 1) * block, cols]
                sym[k * block:(k + 1) * block, cols] = jnp.where(row <= column, upper, transposed(upper, eye))

        @pl.when(b < mine)
        def _():
            for k in range(depth):
                for y in range(YLO):
                    at = k * block + y * CORE * rows
                    turn[pl.ds(pl.multiple_of(at + core * rows, rows), rows), :] = turned[b, y, k]
                    turn[pl.ds(pl.multiple_of(at + (1 - core) * rows, rows), rows), :] = turned_other[b, y, k]
            for k in range(depth):
                sym[k * block:(k + 1) * block, cols] = transposed(turn[k * block:(k + 1) * block], eye)

        return carry

    def store(step, product):
        width = product.shape[1]
        if len(t_refs) > 1:
            final[:, pl.ds(pl.multiple_of(step * width, width), width)] = product
        else:
            lanes = t_refs[0].shape[3]
            per_step = width // lanes
            for u in range(per_step):
                for k in range(depth):
                    t_refs[0][step * per_step + u, k] = product[k * block:(k + 1) * block, u * lanes:(u + 1) * lanes]

    lax.fori_loop(0, BLOCKS, build, 0)
    products(sym, c_hbm, c_ref, sems, store)
    if len(t_refs) > 1:
        lanes = t_refs[0].shape[2]
        for d in range(BLOCKS):
            part = (mine + ORDER[index][d]) % BLOCKS
            t_refs[d][0] = final[:, pl.ds(pl.multiple_of(part * lanes, lanes), lanes)]


def first_half(index, place, direct, direct_other, turned, turned_other, picked, outs, name):
    _, _, depth, rows, block = direct.shape
    size, width = picked.shape
    vmem = pl.BlockSpec(memory_space=pltpu.VMEM)
    return pl.pallas_call(
        functools.partial(first_kernel, index),
        out_shape=[jax.ShapeDtypeStruct(out, BF16) for out in outs],
        in_specs=[pl.BlockSpec(memory_space=pltpu.SMEM), vmem, vmem, vmem, vmem, HBM],
        out_specs=[vmem] * len(outs),
        scratch_shapes=column_scratch(picked) + [
            pltpu.VMEM((depth * block, size), BF16),
            pltpu.VMEM((depth * block, block), BF16),
            pltpu.VMEM((depth * block, width), BF16),
            pltpu.VMEM((block, block), BF16)],
        compiler_params=PARAMS,
        name=name,
    )(place, direct, direct_other, turned, turned_other, in_hbm(picked))


def second_kernel(t_ref, c_hbm, out_ref, c_ref, sems, left, eye):
    count, depth, block, lanes = t_ref.shape
    rows = lanes // YLO
    fetch_columns(c_hbm, c_ref, sems)
    set_identity(eye)

    def build(b, carry):
        for k in range(depth):
            left[k * lanes:(k + 1) * lanes, pl.ds(pl.multiple_of(b * block, block), block)] = transposed(t_ref[b, k], eye)
        return carry

    def store(step, product):
        per_step = COLS // STEPS
        for u in range(per_step):
            for y in range(YLO):
                for k in range(depth):
                    at = k * lanes + y * rows
                    out_ref[step * per_step + u, y, k] = product[at:at + rows, u * block:(u + 1) * block]

    lax.fori_loop(0, count, build, 0)
    products(left, c_hbm, c_ref, sems, store)


def second_half(partial_value, orbitals):
    _, depth, block, lanes = partial_value.shape
    size = orbitals.shape[0]
    vmem = pl.BlockSpec(memory_space=pltpu.VMEM)
    return pl.pallas_call(
        second_kernel,
        out_shape=jax.ShapeDtypeStruct((COLS, YLO, depth, lanes // YLO, block), BF16),
        in_specs=[vmem, HBM],
        out_specs=vmem,
        scratch_shapes=column_scratch(orbitals) + [
            pltpu.VMEM((depth * lanes, size), BF16),
            pltpu.VMEM((lanes, lanes), BF16)],
        compiler_params=PARAMS,
        name="second_half",
    )(partial_value, in_hbm(orbitals))


def second_side_kernel(place, t_ref, other_ref, c_hbm, keep, send, c_ref, sems, left, final, eye):
    count, _, block, lanes = t_ref.shape
    rows = lanes // YLO
    ylo, core = place[AT_YLO], place[AT_CORE]
    fetch_columns(c_hbm, c_ref, sems)
    set_identity(eye)

    def build(b, carry):
        cols = pl.ds(pl.multiple_of(b * block, block), block)
        own = transposed(t_ref[b, 0], eye)
        other = transposed(other_ref[b, 0], eye)
        for y in range(YLO):
            at = y * CORE * rows
            left[pl.ds(pl.multiple_of(at + core * rows, rows), rows), cols] = own[y * rows:(y + 1) * rows]
            left[pl.ds(pl.multiple_of(at + (1 - core) * rows, rows), rows), cols] = other[y * rows:(y + 1) * rows]
        return carry

    def store(step, product):
        width = product.shape[1]
        final[pl.ds(pl.multiple_of(step * width, width), width)] = transposed(product, eye)

    lax.fori_loop(0, count, build, 0)
    products(left, c_hbm, c_ref, sems, store)
    for z in range(Z):
        at = z * YLO * rows
        keep[z] = final[pl.ds(pl.multiple_of(at + ylo * rows, rows), rows)]
        send[z] = final[pl.ds(pl.multiple_of(at + (1 - ylo) * rows, rows), rows)]


def second_half_side(place, own, other, picked):
    _, _, block, lanes = own.shape
    size, width = picked.shape
    vmem = pl.BlockSpec(memory_space=pltpu.VMEM)
    out = jax.ShapeDtypeStruct((Z, lanes // YLO, block), BF16)
    return pl.pallas_call(
        second_side_kernel,
        out_shape=[out, out],
        in_specs=[pl.BlockSpec(memory_space=pltpu.SMEM), vmem, vmem, HBM],
        out_specs=[vmem, vmem],
        scratch_shapes=column_scratch(picked) + [
            pltpu.VMEM((block, size), BF16),
            pltpu.VMEM((width, block), BF16),
            pltpu.VMEM((block, block), BF16)],
        compiler_params=PARAMS,
        name="second_half_side",
    )(place, own, other, in_hbm(picked))


def spread_kernel(index, place, x_ref, *out_refs):
    for d in range(BLOCKS):
        out_refs[d][...] = x_ref[(place[index] + ORDER[index][d]) % BLOCKS]


def spread(index, place, value):
    vmem = pl.BlockSpec(memory_space=pltpu.VMEM)
    return pl.pallas_call(
        functools.partial(spread_kernel, index),
        out_shape=[jax.ShapeDtypeStruct(value.shape[1:], BF16)] * BLOCKS,
        in_specs=[pl.BlockSpec(memory_space=pltpu.SMEM), vmem],
        out_specs=[vmem] * BLOCKS,
        compiler_params=SMALL,
        name="spread",
    )(place, value)


def join_kernel(place, keep, got, *out_refs):
    z, ylo = place[AT_Z], place[AT_YLO]
    for d in range(BLOCKS):
        out_refs[d][ylo] = keep[(z + ORDER[AT_Z][d]) % BLOCKS]
        out_refs[d][1 - ylo] = got[(z + ORDER[AT_Z][d]) % BLOCKS]


def join_and_spread(place, keep, got):
    vmem = pl.BlockSpec(memory_space=pltpu.VMEM)
    return pl.pallas_call(
        join_kernel,
        out_shape=[jax.ShapeDtypeStruct((YLO,) + keep.shape[1:], BF16)] * BLOCKS,
        in_specs=[pl.BlockSpec(memory_space=pltpu.SMEM), vmem, vmem],
        out_specs=[vmem] * BLOCKS,
        compiler_params=SMALL,
        name="join_and_spread",
    )(place, keep, got)


def collect_kernel(index, place, *refs):
    out_ref = refs[BLOCKS]
    for d in range(BLOCKS):
        out_ref[(place[index] + BLOCKS - ORDER[index][d]) % BLOCKS] = refs[d][...]


def collect(index, place, parts):
    vmem = pl.BlockSpec(memory_space=pltpu.VMEM)
    return pl.pallas_call(
        functools.partial(collect_kernel, index),
        out_shape=jax.ShapeDtypeStruct((BLOCKS,) + parts[0].shape, BF16),
        in_specs=[pl.BlockSpec(memory_space=pltpu.SMEM)] + [vmem] * BLOCKS,
        out_specs=vmem,
        compiler_params=SMALL,
        name="collect",
    )(place, *parts)


def finish_kernel(place, *refs):
    main_ref, out_hbm, sems = refs[BLOCKS:]
    main = main_ref.shape[0]
    share = main // STEPS
    copies = []
    for g in range(STEPS):
        part = pl.ds(g * share, share)
        copies.append(pltpu.make_async_copy(main_ref.at[part], out_hbm.at[part], sems.at[BLOCKS * YLO + g]))
    for d in range(BLOCKS):
        for y in range(YLO):
            to = main + y * BLOCKS + (place[AT_Z] + BLOCKS - ORDER[AT_Z][d]) % BLOCKS
            copies.append(pltpu.make_async_copy(refs[d].at[y], out_hbm.at[to], sems.at[d * YLO + y]))
    for copy in copies:
        copy.start()
    for copy in copies:
        copy.wait()


def finish(place, parts, main):
    pairs, rows, block = main.shape
    vmem = pl.BlockSpec(memory_space=pltpu.VMEM)
    return pl.pallas_call(
        finish_kernel,
        out_shape=jax.ShapeDtypeStruct((pairs + YLO * BLOCKS, rows, block), BF16),
        in_specs=[pl.BlockSpec(memory_space=pltpu.SMEM)] + [vmem] * (BLOCKS + 1),
        out_specs=HBM,
        scratch_shapes=[pltpu.SemaphoreType.DMA((BLOCKS * YLO + STEPS,))],
        compiler_params=SMALL,
        name="finish",
    )(place, *parts, main)


def rotate(index, parts, axes):
    out = [parts[0]]
    for part, d in zip(parts[1:], ORDER[index][1:]):
        out.append(lax.ppermute(part, axes, [(i, (i + d) % BLOCKS) for i in range(BLOCKS)]))
    return out


def swap(value, axis):
    return lax.ppermute(value, axis, [(0, 1), (1, 0)])


def per_device(half_panel, orbitals):
    pairs, rows, block = half_panel.shape
    side_pairs = Z * YLO
    main_pairs = pairs - side_pairs
    depth = main_pairs // (COLS * YLO)
    z, ylo, core = lax.axis_index("z"), lax.axis_index("ylo"), lax.axis_index("core")
    c = lax.axis_index("x") * YHI + lax.axis_index("yhi")

    place = jnp.stack([z, ylo, core, c]).astype(jnp.int32)

    def deep(value):
        return value.reshape(BLOCKS, YLO, 1, rows, block)

    together = lax.optimization_barrier

    with jax.named_scope("side_in"):
        side = half_panel[main_pairs:].reshape(YLO, Z, rows, block)
        got = swap(lax.dynamic_index_in_dim(side, 1 - ylo, 0, keepdims=False), "ylo")
        keep = lax.dynamic_index_in_dim(side, ylo, 0, keepdims=False)
    picked, own = pick_columns(place, orbitals, half_panel, main_pairs)
    own = own.reshape(COLS * YLO, depth, rows, block)
    own, got, keep, picked = together((own, got, keep, picked))

    with jax.named_scope("panels_in"):
        own = lax.all_to_all(own, PLANE, 0, 0, tiled=True)
        own = own.reshape(COLS, YLO, depth, rows, block)
    with jax.named_scope("side_in"):
        parts = rotate(AT_Z, join_and_spread(place, keep, got), "z")
        side_own = collect(AT_Z, place, parts)
    own, side_own, picked = together((own, side_own, picked))

    with jax.named_scope("mirror"):
        own_low = lax.all_to_all(own, "z", 0, 0, tiled=True)
    other = swap(own, "core")
    with jax.named_scope("side_mirror"):
        side_other = swap(side_own, "core")
        parts = rotate(AT_C, spread(AT_C, place, side_own), SIDE)
        side_low = collect(AT_C, place, parts)
        side_other_low = swap(side_low, "core")
        side_partial = first_half(
            AT_C, place, deep(side_low), deep(side_other_low), deep(side_own), deep(side_other),
            picked, [(1, block, block // CORE)] * BLOCKS, "first_half_side"
        )
    own_low, other, side_partial = together((own_low, other, side_partial))

    other_low = swap(own_low, "core")
    partial_value, = first_half(
        AT_Z, place, own, other, own_low, other_low, picked,
        [(BLOCKS, depth, block, block // CORE)], "first_half"
    )
    with jax.named_scope("partial"):
        partial_value = lax.all_to_all(partial_value, "z", 0, 0, tiled=True)
    with jax.named_scope("side_partial"):
        parts = rotate(AT_C, side_partial, SIDE)
        side_partial = collect(AT_C, place, parts)
        side_partial_other = swap(side_partial, "core")
        keep, send = second_half_side(place, side_partial, side_partial_other, picked)
    got = swap(send, "ylo")
    partial_value, keep = together((partial_value, keep))

    result = second_half(partial_value, orbitals)
    result, got, keep = together((result, got, keep))

    with jax.named_scope("panels_out"):
        result = result.reshape(COLS * YLO, depth, rows, block)
        result = lax.all_to_all(result, PLANE, 0, 0, tiled=True)
        result = result.reshape(main_pairs, rows, block)
    with jax.named_scope("side_out"):
        parts = rotate(AT_Z, join_and_spread(place, keep, got), "z")
    return finish(place, parts, result)


def solution(mesh):
    fine = Mesh(mesh.devices.reshape(Z, YLO, CORE, X, YHI), ("z", "ylo", "core", "x", "yhi"))
    spec = P(None, ("z", "ylo", "core"), ("x", "yhi"))
    return jax.shard_map(
        per_device, mesh=fine, in_specs=(spec, P()), out_specs=spec, check_vma=False
    )
```
